256 devices in a mesh: pages: 64 (over y, z, core), expert: 4 (over x).
Axes of the slice: x: 4, y: 4, z: 8, core: 2. Of those that a mesh axis runs over, the one named last changes fastest.
Arguments:
- old_keys: bfloat16 [512, 128, 2048], P('pages', None, 'expert'), may hold values from -6 to 6
- old_values: bfloat16 [512, 128, 2048], P('pages', None, 'expert'), may hold values from -6 to 6
- keep_lists: int32 [512, 31], P('pages'), may hold values from 0 to 127, as said below
- drop_weights: int32 [512, 128], P('pages'), may hold values from 1 to 8
- request_pages: int32 [64], replicated, may hold values from 4 to 12, as said below
- page_table: int32 [64, 12], replicated, may hold values from 0 to 511, as said below
- new_table: int32 [64, 3], replicated, may hold values from 0 to 255, as said below
- queries: bfloat16 [64, 2, 2048], P(None, None, 'expert'), may hold values from -20 to 20
- new_keys: bfloat16 [64, 2048], P('pages', 'expert'), may hold values from -12 to 12
- new_values: bfloat16 [64, 2048], P('pages', 'expert'), may hold values from -6 to 6
- expert_ids: int32 [64, 2], replicated, may hold values from 0 to 7, all different within a row
- router_logits: float32 [64, 8], P('pages'), may hold values from -6 to 6
- out_weight: bfloat16 [64, 2048, 256], P('pages', 'expert'), may hold values from -0.375 to 0.375
Outputs:
- compact_keys: bfloat16 [256, 128, 2048], P('pages', None, 'expert')
- compact_values: bfloat16 [256, 128, 2048], P('pages', None, 'expert')
- mixed: bfloat16 [64, 2048], P('pages', 'expert')
The draws below stay inside these ranges and needn't reach their ends.
Inputs may be any that keep to these rules, and one draw needn't show every extreme that they name: `request_pages`: every count is a multiple of 4; the counts sum to 512; one request has 12 pages. `page_table`: the first request_pages[r] entries of row r name that request's old pages in order and later entries are unused; every old page belongs to exactly one request; old page g lies on index g // 8 of pages; no index of pages holds more than 1 old pages whose new pages lie on one index, and some index holds that many. `new_table`: the first request_pages[r] / 4 entries of row r name distinct new slots and later entries are unused; slot s lies on index s // 4 of pages; some index has all 4 of its slots used. `keep_lists`: each row holds 31 distinct positions in increasing order.
All inputs are finite; a program needn't handle non-finite values.
Results may differ from the reference program's by a relative error of at most 0.012.
Values may be sent and summed in bfloat16 or wider, within the bound.
No kernel may reach another device: no remote copies, remote signals or barrier semaphores. Data moves between devices by JAX's collectives and lax.ppermute only.
A program may use at most 64 MiB of HBM per device.

```python
import math
import jax
import jax.numpy as jnp
from jax import lax

D = 2048
KVH = 16
HD = 128
EXPERTS = 8
TOPK = 2
PAGE = 128
KEEP = 31
SLOTS = 8
REQS = 64
CPP = 4
MEANM = 2
MAXM = 3
MAXP = 12
NEWCAP = 4
OLDTOTAL = 512
NEWTOTAL = 256
CB = 8
N_PAGES = 64


def paired_counts(draw_key, shuffle_key, count, middle, highest, pin_ends):
    halves = count // 2
    offsets = jax.random.randint(draw_key, (halves,), 1 - middle, middle).astype(jnp.int32)
    offsets = offsets.at[0].set(highest - middle)
    if pin_ends:
        rest = jax.random.permutation(shuffle_key, count - 2).astype(jnp.int32)
        shuffled = jnp.concatenate([jnp.array([count - 1], jnp.int32), rest[:halves - 1], jnp.array([count - 2], jnp.int32), rest[halves - 1:]])
    else:
        shuffled = jax.random.permutation(shuffle_key, count).astype(jnp.int32)
    result = jnp.zeros((count,), jnp.int32)
    result = result.at[shuffled[:halves]].set(middle + offsets)
    return result.at[shuffled[halves:]].set(middle - offsets)


def layout_world(base_key):
    folded = jax.random.fold_in(base_key, 9173)
    streams = jax.random.split(folded, 8)
    devices = N_PAGES
    request_counts = paired_counts(streams[0], streams[1], REQS, MEANM, MAXM, False)
    owner_loads = paired_counts(streams[2], streams[3], devices, MEANM, NEWCAP, True)
    live_new = MEANM * REQS
    receivers = jax.random.permutation(streams[4], devices).astype(jnp.int32)
    ordered_loads = owner_loads[receivers]
    load_ends = jnp.cumsum(ordered_loads).astype(jnp.int32)
    slot_index = jnp.arange(live_new, dtype=jnp.int32)
    load_pos = jnp.searchsorted(load_ends, slot_index, side='right').astype(jnp.int32)
    holder = receivers[load_pos]
    holder_slot = slot_index - (load_ends[load_pos] - ordered_loads[load_pos])
    picked = jax.random.permutation(streams[5], live_new).astype(jnp.int32)
    request_ends = jnp.cumsum(request_counts).astype(jnp.int32)
    request_of = jnp.searchsorted(request_ends, picked, side='right').astype(jnp.int32)
    page_of = picked - (request_ends[request_of] - request_counts[request_of])
    new_table = jnp.zeros((REQS, MAXM), jnp.int32).at[request_of, page_of].set(holder * NEWCAP + holder_slot)
    demand = jnp.arange(live_new * CPP, dtype=jnp.int32)
    slot_of = demand // CPP
    quarter = demand % CPP
    senders = jax.random.permutation(streams[6], devices).astype(jnp.int32)
    sender_keys = jax.random.split(streams[7], devices)
    slot_orders = jax.vmap(lambda subkey: jax.random.permutation(subkey, SLOTS))(sender_keys).astype(jnp.int32)
    sender = senders[demand % devices]
    physical = sender * SLOTS + slot_orders[sender, demand // devices]
    page_table = jnp.zeros((REQS, MAXP), jnp.int32).at[request_of[slot_of], page_of[slot_of] * CPP + quarter].set(physical)
    return ((request_counts * CPP).astype(jnp.int32), page_table, new_table)


def keep_table(base_key):
    folded = jax.random.fold_in(base_key, 4421)
    raw_scores = jax.random.randint(folded, (OLDTOTAL, PAGE), 0, 1 << 20).astype(jnp.int32) * PAGE
    raw_scores = raw_scores + jnp.arange(PAGE, dtype=jnp.int32)[None, :]
    ignored, chosen = lax.top_k(raw_scores, KEEP)
    return jnp.sort(chosen, axis=1).astype(jnp.int32)


def draw_request_pages(key, part):
    return layout_world(key)[0]


def draw_page_table(key, part):
    return layout_world(key)[1]


def draw_new_table(key, part):
    return layout_world(key)[2]


def draw_keep_lists(key, part):
    return keep_table(key)


def draw_old_keys(key, part):
    folded = jax.random.fold_in(key, 3301)
    entries = jnp.clip(jax.random.normal(folded, (OLDTOTAL, PAGE, KVH * HD), jnp.float32), -6.0, 6.0)
    return entries.astype(jnp.bfloat16)


def draw_queries(key, part):
    folded = jax.random.fold_in(key, 2207)
    entries = jnp.clip(jax.random.normal(folded, (REQS, TOPK, KVH * HD), jnp.float32), -6.0, 6.0)
    return entries.astype(jnp.bfloat16)


def with_ends(values, rng, low, high):
    dims = values.shape
    index_at = [jax.random.randint(jax.random.fold_in(rng, axis), (), 0, dims[axis]) for axis in range(len(dims))]
    values = values.at[tuple(index_at)].set(low)
    longest = dims.index(max(dims))
    index_at[longest] = (index_at[longest] + 1) % dims[longest]
    return values.at[tuple(index_at)].set(high)


def block_scale(key, extent, pieces, smallest, largest):
    def one(dim, shards_of):
        steps = jax.random.uniform(jax.random.fold_in(jax.random.fold_in(key, 6), dim), (shards_of,), jnp.float32, smallest / len(pieces), largest / len(pieces))
        return jnp.repeat(jnp.exp(steps), extent[dim] // shards_of).reshape((-1,) + (1,) * (len(extent) - dim - 1))

    level = one(*pieces[0])
    for cut in pieces[1:]:
        level = level * one(*cut)
    return level


def distinct(stream_key, rows, count, top, lift):
    ranking = jax.random.permutation(jax.random.fold_in(stream_key, 1), count)
    pull = ranking
    for power in range(3):
        pull = pull * pull // count
    pull = pull * lift // count
    chance = jax.random.randint(jax.random.fold_in(stream_key, 2), (rows, count), 0, 4096) + pull
    holders = jax.random.permutation(jax.random.fold_in(stream_key, 3), rows)[jnp.arange(count) % rows]
    chance = jnp.where(jnp.arange(rows)[:, None] == holders[None, :], 1 << 14, chance)
    score = chance * count + jnp.arange(count)
    return lax.top_k(score.astype(jnp.int32), top)[1].astype(jnp.int32)


def normal_values(key, shape, scale, bound, cuts=(), held_as=jnp.bfloat16):
    factor_of = block_scale(key, shape, cuts, -0.22, 0.18) if cuts else 1.0
    values = jax.random.normal(key, shape, jnp.float32) * scale * factor_of
    return jnp.minimum(jnp.maximum(values, -bound), bound).astype(held_as)


def setup_inputs(seed: int = 0) -> dict:
    splits = jax.random.split(jax.random.key(seed), 14)
    old_keys = draw_old_keys(jax.random.fold_in(splits[13], 71), 0)
    old_values = normal_values(splits[1], (OLDTOTAL, PAGE, KVH * HD), 1.0, 6.0, ((0, 64), (2, 4)))
    keep_lists = draw_keep_lists(jax.random.fold_in(splits[13], 71), 0)
    drop_weights = with_ends(jax.random.randint(splits[3], (OLDTOTAL, PAGE), 1, 9), jax.random.fold_in(splits[3], 1), 1, 8).astype(jnp.int32)
    request_pages = draw_request_pages(jax.random.fold_in(splits[13], 71), 0)
    page_table = draw_page_table(jax.random.fold_in(splits[13], 71), 0)
    new_table = draw_new_table(jax.random.fold_in(splits[13], 71), 0)
    queries = draw_queries(jax.random.fold_in(splits[13], 71), 0)
    new_keys = normal_values(splits[8], (REQS, KVH * HD), 3.0, 12.0, ((0, 64), (1, 4)))
    new_values = normal_values(splits[9], (REQS, KVH * HD), 1.0, 6.0, ((0, 64), (1, 4)))
    expert_ids = distinct(splits[10], REQS, EXPERTS, TOPK, 2048)
    router_logits = normal_values(splits[11], (REQS, EXPERTS), 1.0, 6.0, ((0, 64),), jnp.float32)
    out_weight = normal_values(splits[12], (N_PAGES, KVH * HD, D // CB), (KVH * HD // 8) ** -0.5, 0.375, ((0, 64), (1, 4)))
    return dict(old_keys=old_keys, old_values=old_values, keep_lists=keep_lists, drop_weights=drop_weights, request_pages=request_pages, page_table=page_table, new_table=new_table, queries=queries, new_keys=new_keys, new_values=new_values, expert_ids=expert_ids, router_logits=router_logits, out_weight=out_weight)


NEGATIVE = -1e+30

def compact_pages(caches, keep_lists, drop_weights):
    positions = jnp.arange(PAGE, dtype=jnp.int32)

    def one_page(inputs):
        page_cache, kept_positions, weights = inputs
        chosen = jnp.any(kept_positions[:, None] == positions[None, :], axis=0)
        merge_coef = jnp.where(chosen, 0.0, weights.astype(jnp.float32))
        kept_rows = jnp.take(page_cache, kept_positions, axis=0)
        merged = jnp.dot(merge_coef, page_cache.astype(jnp.float32), precision=lax.Precision.HIGHEST) / jnp.sum(merge_coef)
        return jnp.concatenate([kept_rows, merged[None, :].astype(jnp.bfloat16)], axis=0)
    return lax.map(one_page, (caches, keep_lists, drop_weights))

def reference(old_keys, old_values, keep_lists, drop_weights, request_pages, page_table, new_table, queries, new_keys, new_values, expert_ids, router_logits, out_weight):
    key_blocks = compact_pages(old_keys, keep_lists, drop_weights)
    value_blocks = compact_pages(old_values, keep_lists, drop_weights)
    block_rows = KEEP + 1
    kv_width = KVH * HD
    new_pages = request_pages // CPP
    page_index = jnp.arange(MAXM, dtype=jnp.int32)
    quarter = jnp.arange(CPP, dtype=jnp.int32)
    live_pages = page_index[None, :] < new_pages[:, None]
    targets = new_table[:, :, None] * CPP + quarter[None, None, :]
    targets = jnp.where(live_pages[:, :, None], targets, NEWTOTAL * CPP).astype(jnp.int32)
    flat_targets = targets.reshape(-1)
    flat_sources = page_table.reshape(-1).astype(jnp.int32)

    def place_rows(blocks):
        zero_rows = jnp.zeros((NEWTOTAL * CPP, block_rows, kv_width), jnp.bfloat16)
        filled = zero_rows.at[flat_targets].set(blocks[flat_sources], mode='drop')
        return filled.reshape(NEWTOTAL, CPP * block_rows, kv_width)
    compact_keys = place_rows(key_blocks)
    compact_values = place_rows(value_blocks)
    score_scale = 1.0 / math.sqrt(HD)
    bias_row = jnp.where(jnp.arange(block_rows) == block_rows - 1, math.log(PAGE - KEEP), 0.0).astype(jnp.float32)
    page_slots = jnp.arange(MAXP, dtype=jnp.int32)
    highest = lax.Precision.HIGHEST

    def attend(inputs):
        page_ids, page_count, query_row, own_key, own_value = inputs
        key_rows = key_blocks[page_ids].reshape(MAXP, block_rows, KVH, HD).astype(jnp.float32)
        value_rows = value_blocks[page_ids].reshape(MAXP, block_rows, KVH, HD).astype(jnp.float32)
        query_heads = query_row.reshape(TOPK, KVH, HD).astype(jnp.float32)
        scores = jnp.einsum('khd,pehd->khpe', query_heads, key_rows, precision=highest) * score_scale + bias_row[None, None, None, :]
        scores = jnp.where((page_slots < page_count)[None, None, :, None], scores, NEGATIVE)
        own_score = jnp.einsum('khd,hd->kh', query_heads, own_key.reshape(KVH, HD).astype(jnp.float32), precision=highest) * score_scale
        peak_score = jnp.maximum(lax.optimization_barrier(jnp.max(scores, axis=(2, 3))), own_score)
        softmax_terms = jnp.exp(scores - peak_score[:, :, None, None])
        own_prob = jnp.exp(own_score - peak_score)
        rounded = lax.optimization_barrier(softmax_terms.astype(jnp.bfloat16)).astype(jnp.float32)
        own_rounded = lax.optimization_barrier(own_prob.astype(jnp.bfloat16)).astype(jnp.float32)
        numerator = jnp.einsum('khpe,pehd->khd', rounded, value_rows, precision=highest)
        numerator = numerator + own_rounded[:, :, None] * own_value.reshape(KVH, HD).astype(jnp.float32)[None, :, :]
        denominator = lax.optimization_barrier(jnp.sum(softmax_terms, axis=(2, 3))) + own_prob
        return numerator / denominator[:, :, None]
    attention = lax.map(attend, (page_table, request_pages, queries, new_keys, new_values))
    chosen = jnp.take_along_axis(router_logits, expert_ids, axis=1)
    gate_weights = jax.nn.softmax(chosen, axis=1)
    weighted = (gate_weights[:, :, None, None] * attention).astype(jnp.bfloat16).reshape(REQS, TOPK, kv_width)
    expert_mats = out_weight.reshape(EXPERTS, CB, kv_width, D // CB).transpose(0, 2, 1, 3).reshape(EXPERTS, kv_width, D)

    def mix_request(inputs):
        gated_rows, expert_pair = inputs
        return jnp.einsum('kc,kcd->d', gated_rows.astype(jnp.float32), expert_mats[expert_pair].astype(jnp.float32), precision=highest)
    mixed = lax.map(mix_request, (weighted, expert_ids)).astype(jnp.bfloat16)
    return (compact_keys, compact_values, mixed)
```

```python
import math

import jax
import jax.numpy as jnp
from jax import lax
from jax.experimental import pallas as pl
from jax.experimental.pallas import tpu as pltpu
from jax.sharding import PartitionSpec as P

HD = 128
EXPERTS = 8
NEGATIVE = -1e30
F32 = jnp.float32
BF16 = jnp.bfloat16
VMEM = pl.BlockSpec(memory_space=pltpu.VMEM)
SMEM = pl.BlockSpec(memory_space=pltpu.SMEM)
NT = (((1,), (1,)), ((), ()))


def iota(shape, dim):
    return lax.broadcasted_iota(jnp.int32, shape, dim)


def dot(a, b):
    return jnp.dot(a, b, preferred_element_type=F32)


def source_kernel(
    my_ref, table_ref, keep_ref, drop_ref, k_ref, v_ref, q_ref, nk_ref, nv_ref, out_ref, kb, vb, acc
):
    my = my_ref[0]
    slots, page_len, width = k_ref.shape
    rows = keep_ref.shape[0]
    heads = width // HD
    topk = q_ref.shape[0]
    reqs = q_ref.shape[1]
    lane = iota((rows, page_len), 1)
    last = iota((rows, page_len), 0) == rows - 1
    for g in range(slots):
        onehot = jnp.where(keep_ref[:, g : g + 1] == lane, 1.0, 0.0)
        kept = jnp.max(onehot, axis=0, keepdims=True)
        coef = jnp.where(kept > 0.0, 0.0, drop_ref[g : g + 1, :].astype(F32))
        total = jnp.sum(coef, axis=1, keepdims=True)
        mat = jnp.where(last, coef, onehot).astype(BF16)
        denom = jnp.where(last[:, 0:1], total, 1.0)
        kb[g * rows : (g + 1) * rows, :] = (dot(mat, k_ref[g]) / denom).astype(BF16)
        vb[g * rows : (g + 1) * rows, :] = (dot(mat, v_ref[g]) / denom).astype(BF16)
    n = slots * rows
    to = iota((n, n), 0)
    fro = iota((n, n), 1)
    perm = jnp.where((to % slots == fro // rows) & (to // slots == fro % rows), 1.0, 0.0).astype(BF16)
    for base, blocks in ((0, kb), (rows, vb)):
        spread = dot(perm, blocks[...])
        for t in range(heads):
            out_ref[base : base + rows, t * slots : (t + 1) * slots, :] = (
                spread[:, t * HD : (t + 1) * HD].reshape(rows, slots, HD).astype(BF16)
            )
    ent = 2 * slots
    pad = table_ref.shape[1]
    ent_row = iota((ent, pad), 0)
    req_lane = iota((ent, pad), 1)
    sel = jnp.where((ent_row == slots) & (req_lane == my), 1.0, 0.0)
    for g in range(slots):
        hit = jnp.where(table_ref[...] == my * slots + g, 1.0, 0.0)
        sel = jnp.where(ent_row == g, jnp.max(hit, axis=0, keepdims=True), sel)
    sel_b = sel.astype(BF16)
    same = lax.dot_general(sel_b, sel_b, NT, preferred_element_type=F32)
    q_lane = iota((ent, width), 1) // HD
    pieces = []
    for k in range(topk):
        group_query = dot(sel_b[:, :reqs], q_ref[k])
        for h in range(heads):
            pieces.append(jnp.where(q_lane == h, group_query, 0.0))
    queries = jnp.concatenate(pieces, axis=0)
    kh = topk * heads
    scale = 1.0 / math.sqrt(HD)
    scores = lax.dot_general(queries.astype(BF16), kb[...], NT, preferred_element_type=F32) * scale
    col = iota((kh * ent, n), 1)
    scores = scores + jnp.where(col % rows == rows - 1, math.log(page_len - rows + 1), 0.0)
    of_page = jnp.where(iota((ent, n), 1) // rows == iota((ent, n), 0), 1.0, 0.0).astype(BF16)
    shared = dot(same.astype(BF16), of_page)
    mask = jnp.concatenate([shared] * kh, axis=0) > 0.5
    scores = jnp.where(mask, scores, NEGATIVE)
    is_own = iota((kh * ent, 1), 0) % ent == slots
    own = jnp.sum(queries * nk_ref[...].astype(F32), axis=1, keepdims=True) * scale
    own = jnp.where(is_own, own, NEGATIVE)
    peak = jnp.maximum(jnp.max(scores, axis=1, keepdims=True), own)
    shift = peak.astype(BF16).astype(F32)
    probs = jnp.where(mask, jnp.exp(scores - shift), 0.0)
    own_prob = jnp.where(is_own, jnp.exp(own - shift), 0.0)
    den = jnp.sum(probs, axis=1, keepdims=True) + own_prob
    num = dot(probs.astype(BF16), vb[...])
    num = num + own_prob.astype(BF16).astype(F32) * nv_ref[...].astype(F32)
    high = den.astype(BF16).astype(F32)
    stat_lane = iota((kh * ent, HD), 1)
    stats = jnp.where(stat_lane == 0, shift, jnp.where(stat_lane == 1, high, den - high))
    parts = [
        num[j * ent : (j + 1) * ent, (j % heads) * HD : (j % heads + 1) * HD] for j in range(kh)
    ] + [stats[j * ent : (j + 1) * ent, :] for j in range(kh)]
    entries = jnp.concatenate(parts, axis=1).astype(BF16)
    er = iota((ent, ent), 0)
    ec = iota((ent, ent), 1)
    before = jnp.sum(jnp.where((ec < er) | (ec == slots), same, 0.0), axis=1, keepdims=True)
    first = (ent_row == slots) | ((ent_row < slots) & (before < 0.5))
    pick = jnp.where(first, sel, 0.0).T[:reqs, :].astype(BF16)
    placed = dot(pick, entries)
    for j in range(2 * kh):
        acc[:, j, :] = placed[:, j * HD : (j + 1) * HD]
    out_ref[:, heads * slots :, :] = acc[...].astype(BF16)


def home_kernel(my_ref, ids_ref, logit_ref, got_ref, out_ref):
    my = my_ref[0]
    kh = got_ref.shape[1] // 2
    heads = kh // ids_ref.shape[0]
    got = got_ref[...].astype(F32)
    num = got[:, :kh, :]
    shift = got[:, kh:, 0:1]
    den = got[:, kh:, 1:2] + got[:, kh:, 2:3]
    live = den > 0.0
    peak = jnp.max(jnp.where(live, shift, NEGATIVE), axis=0, keepdims=True)
    factor = jnp.where(live, jnp.exp(shift - peak), 0.0)
    total = jnp.sum(factor * den, axis=0)
    value = jnp.sum(factor * num, axis=0) / total
    mine = iota(ids_ref.shape, 1) == my
    ids = jnp.sum(jnp.where(mine, ids_ref[...], 0), axis=1, keepdims=True)
    logits = jnp.sum(
        jnp.where(iota((ids.shape[0], EXPERTS), 1) == ids, logit_ref[...], 0.0), axis=1, keepdims=True
    )
    terms = jnp.exp(logits - jnp.max(logits, axis=0, keepdims=True))
    gate = terms / jnp.sum(terms, axis=0, keepdims=True)
    columns = out_ref.shape[0] // EXPERTS
    for e in range(EXPERTS):
        row = jnp.zeros((heads, HD), F32)
        for k in range(ids.shape[0]):
            weighted = gate[k : k + 1, :] * value[k * heads : (k + 1) * heads, :]
            row = jnp.where(ids[k : k + 1, :] == e, weighted, row)
        out_ref[e * columns : (e + 1) * columns] = jnp.broadcast_to(
            row[None], (columns, heads, HD)
        ).astype(BF16)


def relay_kernel(source_ref, low_ref, high_ref, out_ref):
    devices, per, _ = low_ref.shape
    slots = per // 2
    held = devices * slots
    tiles = []
    for ref in (low_ref, high_ref):
        for t in range(2):
            rows = ref[:, t * slots : (t + 1) * slots, :].astype(F32)
            tiles.append(rows.reshape(held, HD).astype(BF16))
    table = jnp.concatenate(tiles, axis=1)
    local = out_ref.shape[1]
    step = 16
    for c in range(0, devices, step):
        source = source_ref[c * local : (c + step) * local, :]
        pick = jnp.where(source == iota((step * local, held), 1), 1.0, 0.0).astype(BF16)
        out_ref[c : c + step] = dot(pick, table).reshape(step, local, table.shape[1]).astype(BF16)


def land_kernel(got_ref, k_ref, v_ref):
    total, local, width = got_ref.shape
    rows = total // 2
    n = rows * local
    to = iota((n, n), 0)
    fro = iota((n, n), 1)
    perm = jnp.where((to // rows == fro % local) & (to % rows == fro // local), 1.0, 0.0).astype(BF16)
    for base, ref in ((0, k_ref), (rows, v_ref)):
        flat = got_ref[base : base + rows].reshape(n, width)
        ref[...] = dot(perm, flat).reshape(ref.shape).astype(BF16)


def project_kernel(got_ref, w_ref, out_ref, acc):
    reqs, heads, _ = got_ref.shape
    acc[...] = got_ref[...].astype(F32)
    total = dot(acc[:, 0, :].astype(BF16), w_ref[0, 0:HD, :])
    for h in range(1, heads):
        total = total + dot(acc[:, h, :].astype(BF16), w_ref[0, h * HD : (h + 1) * HD, :])
    for c in range(out_ref.shape[1]):
        out_ref[:, c, :] = total[:, c * HD : (c + 1) * HD]


def shards(
    old_keys,
    old_values,
    keep_lists,
    drop_weights,
    request_pages,
    page_table,
    new_table,
    queries,
    new_keys,
    new_values,
    expert_ids,
    router_logits,
    out_weight,
):
    devices = lax.axis_size("pages")
    shard_count = lax.axis_size("expert")
    my = lax.axis_index("pages").astype(jnp.int32).reshape(1)
    slots, page_len, width = old_keys.shape
    rows = keep_lists.shape[1] + 1
    per_new = page_len // rows
    requests, max_pages = page_table.shape
    max_new = new_table.shape[1]
    new_cap = 2 * (slots // per_new)
    local = new_cap * per_new
    heads = width // HD
    topk = queries.shape[1]
    kh = topk * heads
    chunk = heads * slots + 2 * kh

    logical = jnp.arange(max_pages, dtype=jnp.int32)
    live_table = jnp.where(logical[:, None] < request_pages[None, :], page_table.T, -1)
    live_table = jnp.pad(live_table, ((0, 4), (0, 128 - requests)), constant_values=-1)
    keep_columns = jnp.pad(keep_lists.T, ((0, 1), (0, 0)), constant_values=-1)
    by_choice = queries.transpose(1, 0, 2)

    outbox = pl.pallas_call(
        source_kernel,
        out_shape=jax.ShapeDtypeStruct((devices, chunk, HD), BF16),
        in_specs=[SMEM] + [VMEM] * 8,
        out_specs=VMEM,
        scratch_shapes=[
            pltpu.VMEM((slots * rows, width), BF16),
            pltpu.VMEM((slots * rows, width), BF16),
            pltpu.VMEM((requests, 2 * kh, HD), F32),
        ],
        name="source",
    )(my, live_table, keep_columns, drop_weights, old_keys, old_values, by_choice, new_keys, new_values)
    inbox = lax.all_to_all(outbox, "pages", split_axis=0, concat_axis=0, tiled=True)

    part = 2 * kh
    weighted = pl.pallas_call(
        home_kernel,
        grid=(1,),
        out_shape=jax.ShapeDtypeStruct((devices, heads, HD), BF16),
        in_specs=[
            SMEM,
            VMEM,
            VMEM,
            pl.BlockSpec((devices, part, HD), lambda i: (0, heads * slots // part, 0)),
        ],
        out_specs=VMEM,
        name="home",
    )(my, expert_ids.T, router_logits, inbox)
    spread = lax.all_to_all(weighted, "pages", split_axis=0, concat_axis=0, tiled=True)

    new_live = jnp.arange(max_new, dtype=jnp.int32)[None, :] < (request_pages // per_new)[:, None]
    filled = jnp.where(new_live, new_table, -1).reshape(1, -1)
    fills = filled == jnp.arange(devices * new_cap, dtype=jnp.int32)[:, None]
    pages = page_table.reshape(-1, per_new) + 1
    source = (
        jnp.sum(jnp.where(fills[:, :, None], pages[None, :, :], 0), axis=1) - 1
    ).reshape(-1, 1)
    routed = pl.pallas_call(
        relay_kernel,
        grid=(1,),
        out_shape=jax.ShapeDtypeStruct((devices, local, width), BF16),
        in_specs=[
            VMEM,
            pl.BlockSpec((devices, 2 * slots, HD), lambda i: (0, 0, 0)),
            pl.BlockSpec((devices, 2 * slots, HD), lambda i: (0, 1, 0)),
        ],
        out_specs=VMEM,
        name="relay",
    )(source, inbox, inbox)

    block_cols = out_weight.shape[2]
    contrib = pl.pallas_call(
        project_kernel,
        out_shape=jax.ShapeDtypeStruct((requests, block_cols // HD, HD), F32),
        in_specs=[VMEM, VMEM],
        out_specs=VMEM,
        scratch_shapes=[pltpu.VMEM((requests, heads, HD), F32)],
        name="project",
    )(spread, out_weight)
    blocks = devices // EXPERTS
    per = blocks // shard_count
    moves = []
    for e in range(EXPERTS):
        for c in range(blocks):
            for s in range(shard_count):
                target = e * blocks + (c % per) * shard_count + s
                moves.append(((e * blocks + c) * shard_count + s, target * shard_count + c // per))
    contrib = lax.ppermute(contrib, ("pages", "expert"), moves)
    parts = lax.all_to_all(contrib, "pages", split_axis=0, concat_axis=0, tiled=True)
    mixed = jnp.sum(parts.reshape(EXPERTS, per, shard_count, block_cols // HD, HD), axis=(0, 2))
    mixed = mixed.reshape(1, -1).astype(BF16)

    landed = lax.all_to_all(routed, "pages", split_axis=0, concat_axis=0, tiled=True)
    new_page = jax.ShapeDtypeStruct((new_cap, per_new * rows, width), BF16)
    compact_keys, compact_values = pl.pallas_call(
        land_kernel,
        out_shape=(new_page, new_page),
        in_specs=[VMEM],
        out_specs=(VMEM, VMEM),
        name="land",
    )(landed)
    return (compact_keys, compact_values, mixed)


def solution(mesh):
    in_specs = (
        P("pages", None, "expert"),
        P("pages", None, "expert"),
        P("pages", None),
        P("pages", None),
        P(),
        P(),
        P(),
        P(None, None, "expert"),
        P("pages", "expert"),
        P("pages", "expert"),
        P(),
        P("pages", None),
        P("pages", "expert", None),
    )
    out_specs = (P("pages", None, "expert"), P("pages", None, "expert"), P("pages", "expert"))
    return jax.shard_map(shards, mesh=mesh, in_specs=in_specs, out_specs=out_specs, check_vma=False)
```

```python
import math

import jax
import jax.numpy as jnp
from jax import lax
from jax.experimental import pallas as pl
from jax.experimental.pallas import tpu as pltpu
from jax.sharding import PartitionSpec as P

HD = 128
EXPERTS = 8
NEGATIVE = -1e30
F32 = jnp.float32
BF16 = jnp.bfloat16
VMEM = pl.BlockSpec(memory_space=pltpu.VMEM)
SMEM = pl.BlockSpec(memory_space=pltpu.SMEM)
NT = (((1,), (1,)), ((), ()))


def iota(shape, dim):
    return lax.broadcasted_iota(jnp.int32, shape, dim)


def dot(a, b):
    return jnp.dot(a, b, preferred_element_type=F32)


def source_kernel(
    my_ref,
    table_ref,
    count_ref,
    ids_ref,
    keep_ref,
    drop_ref,
    k_ref,
    v_ref,
    q_ref,
    nk_ref,
    nv_ref,
    logit_ref,
    out_ref,
    kb,
    vb,
    keep_rows,
    q_rows,
):
    my = my_ref[0]
    slots, page_len, width = k_ref.shape
    keep_count = keep_ref.shape[1]
    rows = keep_count + 1
    heads = width // HD
    reqs, topk, _ = q_ref.shape
    keep_rows[...] = jnp.full(keep_rows.shape, -1.0, F32)
    keep_rows[:, 0:keep_count] = keep_ref[...].astype(F32)
    keep_columns = keep_rows[...].T[0:rows, :].astype(jnp.int32)
    q_rows[...] = q_ref[...].astype(F32)
    lane = iota((rows, page_len), 1)
    last = iota((rows, page_len), 0) == rows - 1
    for g in range(slots):
        onehot = jnp.where(keep_columns[:, g : g + 1] == lane, 1.0, 0.0)
        kept = jnp.max(onehot, axis=0, keepdims=True)
        coef = jnp.where(kept > 0.0, 0.0, drop_ref[g : g + 1, :].astype(F32))
        total = jnp.sum(coef, axis=1, keepdims=True)
        mat = jnp.where(last, coef, onehot).astype(BF16)
        denom = jnp.where(last[:, 0:1], total, 1.0)
        kb[g * rows : (g + 1) * rows, :] = (dot(mat, k_ref[g]) / denom).astype(BF16)
        vb[g * rows : (g + 1) * rows, :] = (dot(mat, v_ref[g]) / denom).astype(BF16)
    n = slots * rows
    to = iota((n, n), 0)
    fro = iota((n, n), 1)
    perm = jnp.where((to % slots == fro // rows) & (to // slots == fro % rows), 1.0, 0.0).astype(BF16)
    for base, blocks in ((0, kb), (rows, vb)):
        spread = dot(perm, blocks[...])
        for t in range(heads):
            out_ref[base : base + rows, t * slots : (t + 1) * slots, :] = (
                spread[:, t * HD : (t + 1) * HD].reshape(rows, slots, HD).astype(BF16)
            )
    ent = 2 * slots
    ent_row = iota((ent, reqs), 0)
    req_lane = iota((ent, reqs), 1)
    sel = jnp.where((ent_row == slots) & (req_lane == my), 1.0, 0.0)
    in_use = iota(table_ref.shape, 0) < count_ref[...]
    table = jnp.where(in_use, table_ref[...], -1)
    for g in range(slots):
        hit = jnp.where(table == my * slots + g, 1.0, 0.0)
        sel = jnp.where(ent_row == g, jnp.max(hit, axis=0, keepdims=True), sel)
    sel_b = sel.astype(BF16)
    same = lax.dot_general(sel_b, sel_b, NT, preferred_element_type=F32)
    q_lane = iota((ent, width), 1) // HD
    pieces = []
    for k in range(topk):
        group_query = dot(sel_b, q_rows[:, k, :].astype(BF16))
        for h in range(heads):
            pieces.append(jnp.where(q_lane == h, group_query, 0.0))
    queries = jnp.concatenate(pieces, axis=0)
    kh = topk * heads
    scale = 1.0 / math.sqrt(HD)
    scores = lax.dot_general(queries.astype(BF16), kb[...], NT, preferred_element_type=F32) * scale
    col = iota((kh * ent, n), 1)
    scores = scores + jnp.where(col % rows == rows - 1, math.log(page_len - rows + 1), 0.0)
    of_page = jnp.where(iota((ent, n), 1) // rows == iota((ent, n), 0), 1.0, 0.0).astype(BF16)
    shared = dot(same.astype(BF16), of_page)
    mask = jnp.concatenate([shared] * kh, axis=0) > 0.5
    scores = jnp.where(mask, scores, NEGATIVE)
    is_own = iota((kh * ent, 1), 0) % ent == slots
    own = jnp.sum(queries * nk_ref[...].astype(F32), axis=1, keepdims=True) * scale
    own = jnp.where(is_own, own, NEGATIVE)
    peak = jnp.maximum(jnp.max(scores, axis=1, keepdims=True), own)
    shift = peak.astype(BF16).astype(F32)
    probs = jnp.where(mask, jnp.exp(scores - shift), 0.0)
    own_prob = jnp.where(is_own, jnp.exp(own - shift), 0.0)
    den = jnp.sum(probs, axis=1, keepdims=True) + own_prob
    num = dot(probs.astype(BF16), vb[...])
    num = num + own_prob.astype(BF16).astype(F32) * nv_ref[...].astype(F32)
    high = den.astype(BF16).astype(F32)
    low = den - high
    er = iota((ent, ent), 0)
    ec = iota((ent, ent), 1)
    before = jnp.sum(jnp.where((ec < er) | (ec == slots), same, 0.0), axis=1, keepdims=True)
    row = ent_row[:, 0:1]
    first = (row == slots) | ((row < slots) & (before < 0.5))
    request = jnp.sum(jnp.where(sel > 0.5, req_lane.astype(F32), 0.0), axis=1, keepdims=True)
    expert = [
        jnp.sum(jnp.where(sel > 0.5, ids_ref[k : k + 1, :].astype(F32), 0.0), axis=1, keepdims=True)
        for k in range(topk)
    ]
    expert_lane = iota((1, EXPERTS), 1).astype(F32)
    logit = [
        jnp.sum(
            jnp.where(expert_lane == expert[k][slots : slots + 1, :], logit_ref[...], 0.0),
            axis=1,
            keepdims=True,
        )
        for k in range(topk)
    ]
    top = logit[0]
    for k in range(1, topk):
        top = jnp.maximum(top, logit[k])
    terms = [jnp.exp(logit[k] - top) for k in range(topk)]
    term_sum = terms[0]
    for k in range(1, topk):
        term_sum = term_sum + terms[k]
    stat_lane = iota((ent, HD), 1)
    by_choice = []
    for k in range(topk):
        gate = jnp.where(row == slots, terms[k] / term_sum, 0.0)
        gate_high = gate.astype(BF16).astype(F32)
        stats = jnp.where(stat_lane == 3 * heads, gate_high, 0.0)
        stats = jnp.where(stat_lane == 3 * heads + 1, gate - gate_high, stats)
        stats = jnp.where(stat_lane == 3 * heads + 2, request, stats)
        lanes = []
        for h in range(heads):
            at = slice((k * heads + h) * ent, (k * heads + h + 1) * ent)
            lanes.append(num[at, h * HD : (h + 1) * HD])
            for i, stat in enumerate((shift, high, low)):
                stats = jnp.where(stat_lane == 3 * h + i, stat[at, :], stats)
        by_choice.append(jnp.concatenate(lanes + [stats], axis=1))
    parts = []
    for e in range(EXPERTS):
        part = jnp.zeros(by_choice[0].shape, F32)
        for k in range(topk):
            part = jnp.where(first & (expert[k] == e), by_choice[k], part)
        parts.append(part)
    entries = jnp.concatenate(parts, axis=0).astype(BF16)
    columns = out_ref.shape[0] // EXPERTS
    cut = width // columns
    at = iota((width + HD, columns * HD), 1)
    l = at % HD
    j = at // HD
    head_stat = width + (j * cut // HD) * 3 + l - cut
    rest_stat = width + 3 * heads + l - cut - 3
    origin = jnp.where(l < cut, j * cut + l, jnp.where(l < cut + 3, head_stat, rest_stat))
    origin = jnp.where(l < cut + 6, origin, -1)
    choose = jnp.where(iota(at.shape, 0) == origin, 1.0, 0.0).astype(BF16)
    sent = dot(entries, choose).astype(BF16)
    for e in range(EXPERTS):
        for j in range(columns):
            out_ref[e * columns + j, heads * slots :, :] = sent[
                e * ent : (e + 1) * ent, j * HD : (j + 1) * HD
            ]


def expert_kernel(at_ref, got_ref, *refs):
    columns = got_ref.shape[0] // EXPERTS
    w_refs, out_refs, (stack,) = refs[:columns], refs[columns:-1], refs[-1:]
    j = at_ref[0]
    s = at_ref[1]
    reqs, ent, _ = got_ref.shape
    cut = w_refs[0].shape[0]
    for d in range(columns):
        stack[d] = w_refs[d][...]
    v = got_ref[...].astype(F32).reshape(reqs * ent, HD)
    lane = iota(v.shape, 1)
    shift = v[:, cut : cut + 1]
    den = v[:, cut + 1 : cut + 2] + v[:, cut + 2 : cut + 3]
    request = v[:, cut + 5 : cut + 6]
    live = den > 0.0
    owns = (request == lane.astype(F32)) & live
    peak = jnp.max(jnp.where(owns, shift, NEGATIVE), axis=0, keepdims=True)
    peak = jnp.sum(jnp.where(owns, peak, 0.0), axis=1, keepdims=True)
    factor = jnp.where(live, jnp.exp(shift - peak), 0.0)
    scaled = jnp.where((lane < cut + 3), v * factor, v)
    high = scaled.astype(BF16)
    low = (scaled - high.astype(F32)).astype(BF16)
    pick = jnp.where(owns, 1.0, 0.0).astype(BF16)
    TN = (((0,), (0,)), ((), ()))
    x = lax.dot_general(pick, high, TN, preferred_element_type=F32)
    x = x + lax.dot_general(pick, low, TN, preferred_element_type=F32)
    x = x[:reqs]
    den = x[:, cut + 1 : cut + 2] + x[:, cut + 2 : cut + 3]
    gate = x[:, cut + 3 : cut + 4] + x[:, cut + 4 : cut + 5]
    some = den > 0.0
    weighted = jnp.where(some, gate * (x / jnp.where(some, den, 1.0)), 0.0)[:, :cut].astype(BF16)
    per = columns // len(out_refs)
    for t, out_ref in enumerate(out_refs):
        for i in range(per):
            c = lax.rem(s + t, len(out_refs)) * per + i
            out_ref[i] = dot(weighted, stack[c ^ j]).astype(out_ref.dtype)


def gather_kernel(*refs):
    out_ref = refs[-1]
    per = refs[0].shape[0]
    tiles = out_ref.shape[1] // per
    for i in range(per):
        total = refs[0][i].astype(F32)
        for ref in refs[1:-1]:
            total = total + ref[i].astype(F32)
        for t in range(tiles):
            out_ref[:, i * tiles + t, :] = total[:, t * HD : (t + 1) * HD]


def route_kernel(new_ref, table_ref, count_ref, out_ref):
    max_new = new_ref.shape[0]
    per_new = table_ref.shape[0] // max_new
    shape = (out_ref.shape[0], new_ref.shape[1])
    slot = iota(shape, 0) // per_new
    quarter = iota(shape, 0) % per_new
    found = jnp.zeros(shape, jnp.int32)
    for i in range(max_new):
        filled = jnp.where(i * per_new < count_ref[...], new_ref[i : i + 1, :], -1)
        page = jnp.zeros(shape, jnp.int32)
        for w in range(per_new):
            page = jnp.where(quarter == w, table_ref[i * per_new + w : i * per_new + w + 1, :] + 1, page)
        found = jnp.where(filled == slot, page, found)
    out_ref[...] = jnp.sum(found, axis=1, keepdims=True) - 1


def relay_kernel(source_ref, low_ref, high_ref, out_ref):
    devices, per, _ = low_ref.shape
    slots = per // 2
    held = devices * slots
    tiles = []
    for ref in (low_ref, high_ref):
        for t in range(2):
            rows = ref[:, t * slots : (t + 1) * slots, :].astype(F32)
            tiles.append(rows.reshape(held, HD).astype(BF16))
    table = jnp.concatenate(tiles, axis=1)
    local = out_ref.shape[1]
    step = 16
    for c in range(0, devices, step):
        source = source_ref[c * local : (c + step) * local, :]
        pick = jnp.where(source == iota((step * local, held), 1), 1.0, 0.0).astype(BF16)
        out_ref[c : c + step] = dot(pick, table).reshape(step, local, table.shape[1]).astype(BF16)


def land_kernel(got_ref, k_ref, v_ref):
    total, local, width = got_ref.shape
    rows = total // 2
    n = rows * local
    to = iota((n, n), 0)
    fro = iota((n, n), 1)
    perm = jnp.where((to // rows == fro % local) & (to % rows == fro // local), 1.0, 0.0).astype(BF16)
    for base, ref in ((0, k_ref), (rows, v_ref)):
        flat = got_ref[base : base + rows].reshape(n, width)
        ref[...] = dot(perm, flat).reshape(ref.shape).astype(BF16)


def shards(
    old_keys,
    old_values,
    keep_lists,
    drop_weights,
    request_pages,
    page_table,
    new_table,
    queries,
    new_keys,
    new_values,
    expert_ids,
    router_logits,
    out_weight,
):
    devices = lax.axis_size("pages")
    shard_count = lax.axis_size("expert")
    my = lax.axis_index("pages").astype(jnp.int32)
    shard = lax.axis_index("expert").astype(jnp.int32)
    slots, page_len, width = old_keys.shape
    rows = keep_lists.shape[1] + 1
    per_new = page_len // rows
    requests, max_pages = page_table.shape
    new_cap = 2 * (slots // per_new)
    local = new_cap * per_new
    heads = width // HD
    topk = queries.shape[1]
    ent = 2 * slots
    chunk = heads * slots + ent
    columns = devices // EXPERTS
    cut = width // columns
    place = lax.rem(my, columns)
    table = page_table.T
    counts = request_pages.reshape(1, -1)

    outbox = pl.pallas_call(
        source_kernel,
        out_shape=jax.ShapeDtypeStruct((devices, chunk, HD), BF16),
        in_specs=[SMEM] + [VMEM] * 11,
        out_specs=VMEM,
        scratch_shapes=[
            pltpu.VMEM((slots * rows, width), BF16),
            pltpu.VMEM((slots * rows, width), BF16),
            pltpu.VMEM((slots, HD), F32),
            pltpu.VMEM((requests, topk, width), F32),
        ],
        name="source",
    )(
        my.reshape(1),
        table,
        counts,
        expert_ids.T,
        keep_lists,
        drop_weights,
        old_keys,
        old_values,
        queries,
        new_keys,
        new_values,
        router_logits,
    )
    inbox = lax.all_to_all(outbox, "pages", split_axis=0, concat_axis=0, tiled=True)

    weight, _ = lax.optimization_barrier((out_weight[0], outbox))
    weight_rows = []
    for d in range(columns):
        piece = lax.dynamic_slice_in_dim(weight, (place ^ d) * cut, cut, 0)
        if d:
            swap = [(p, p // columns * columns + (p % columns ^ d)) for p in range(devices)]
            piece = lax.ppermute(piece, "pages", swap)
        weight_rows.append(piece)
    table, weight_rows = lax.optimization_barrier((table, weight_rows))

    source = pl.pallas_call(
        route_kernel,
        out_shape=jax.ShapeDtypeStruct((devices * local, 1), jnp.int32),
        in_specs=[VMEM] * 3,
        out_specs=VMEM,
        name="route",
    )(new_table.T, table, counts)
    routed = pl.pallas_call(
        relay_kernel,
        grid=(1,),
        out_shape=jax.ShapeDtypeStruct((devices, local, width), BF16),
        in_specs=[
            VMEM,
            pl.BlockSpec((devices, 2 * slots, HD), lambda i: (0, 0, 0)),
            pl.BlockSpec((devices, 2 * slots, HD), lambda i: (0, 1, 0)),
        ],
        out_specs=VMEM,
        name="relay",
    )(source, inbox, inbox)
    landed = lax.all_to_all(routed, "pages", split_axis=0, concat_axis=0, tiled=True)

    inbox, _ = lax.optimization_barrier((inbox, routed))
    per = columns // shard_count
    block_cols = out_weight.shape[2]
    contribs = pl.pallas_call(
        expert_kernel,
        grid=(1,),
        out_shape=[jax.ShapeDtypeStruct((per, requests, block_cols), BF16)] * shard_count,
        in_specs=[
            SMEM,
            pl.BlockSpec((devices, ent, HD), lambda i: (0, heads * slots // ent, 0)),
        ]
        + [VMEM] * columns,
        out_specs=[VMEM] * shard_count,
        scratch_shapes=[pltpu.VMEM((columns, cut, block_cols), BF16)],
        name="expert",
    )(jnp.stack([place, shard]), inbox, *weight_rows)
    moved = [contribs[0]]
    for t in range(1, shard_count):
        moved.append(
            lax.ppermute(contribs[t], "expert", [(i, (i + t) % shard_count) for i in range(shard_count)])
        )
    summed = pl.pallas_call(
        gather_kernel,
        out_shape=jax.ShapeDtypeStruct((requests, per * block_cols // HD, HD), F32),
        in_specs=[VMEM] * shard_count,
        out_specs=VMEM,
        name="gather",
    )(*moved)
    summed, landed = lax.optimization_barrier((summed, landed))
    parts = lax.all_to_all(summed, "pages", split_axis=0, concat_axis=0, tiled=True)
    mixed = jnp.sum(parts, axis=0).reshape(1, -1).astype(BF16)

    new_page = jax.ShapeDtypeStruct((new_cap, per_new * rows, width), BF16)
    compact_keys, compact_values = pl.pallas_call(
        land_kernel,
        out_shape=(new_page, new_page),
        in_specs=[VMEM],
        out_specs=(VMEM, VMEM),
        name="land",
    )(landed)
    return (compact_keys, compact_values, mixed)


def solution(mesh):
    in_specs = (
        P("pages", None, "expert"),
        P("pages", None, "expert"),
        P("pages", None),
        P("pages", None),
        P(),
        P(),
        P(),
        P(None, None, "expert"),
        P("pages", "expert"),
        P("pages", "expert"),
        P(),
        P("pages", None),
        P("pages", "expert", None),
    )
    out_specs = (P("pages", None, "expert"), P("pages", None, "expert"), P("pages", "expert"))
    return jax.shard_map(shards, mesh=mesh, in_specs=in_specs, out_specs=out_specs, check_vma=False)
```

```python
import math

import jax
import jax.numpy as jnp
from jax import lax
from jax.experimental import pallas as pl
from jax.experimental.pallas import tpu as pltpu
from jax.sharding import PartitionSpec as P

HD = 128
EXPERTS = 8
NEGATIVE = -1e30
F32 = jnp.float32
BF16 = jnp.bfloat16
VMEM = pl.BlockSpec(memory_space=pltpu.VMEM)
SMEM = pl.BlockSpec(memory_space=pltpu.SMEM)
NT = (((1,), (1,)), ((), ()))


def iota(shape, dim):
    return lax.broadcasted_iota(jnp.int32, shape, dim)


def dot(a, b):
    return jnp.dot(a, b, preferred_element_type=F32)


def source_kernel(
    my_ref,
    table_ref,
    count_ref,
    ids_ref,
    keep_ref,
    drop_ref,
    k_ref,
    v_ref,
    q_ref,
    nk_ref,
    nv_ref,
    logit_ref,
    out_ref,
    part_ref,
    kb,
    vb,
    keep_rows,
    q_rows,
):
    my = my_ref[0]
    slots, page_len, width = k_ref.shape
    keep_count = keep_ref.shape[1]
    rows = keep_count + 1
    heads = width // HD
    reqs, topk, _ = q_ref.shape
    keep_rows[...] = jnp.full(keep_rows.shape, -1.0, F32)
    keep_rows[:, 0:keep_count] = keep_ref[...].astype(F32)
    keep_columns = keep_rows[...].T[0:rows, :].astype(jnp.int32)
    q_rows[...] = q_ref[...].astype(F32)
    lane = iota((rows, page_len), 1)
    last = iota((rows, page_len), 0) == rows - 1
    for g in range(slots):
        onehot = jnp.where(keep_columns[:, g : g + 1] == lane, 1.0, 0.0)
        kept = jnp.max(onehot, axis=0, keepdims=True)
        coef = jnp.where(kept > 0.0, 0.0, drop_ref[g : g + 1, :].astype(F32))
        total = jnp.sum(coef, axis=1, keepdims=True)
        mat = jnp.where(last, coef, onehot).astype(BF16)
        denom = jnp.where(last[:, 0:1], total, 1.0)
        kb[g * rows : (g + 1) * rows, :] = (dot(mat, k_ref[g]) / denom).astype(BF16)
        vb[g * rows : (g + 1) * rows, :] = (dot(mat, v_ref[g]) / denom).astype(BF16)
    n = slots * rows
    to = iota((n, n), 0)
    fro = iota((n, n), 1)
    perm = jnp.where((to % slots == fro // rows) & (to // slots == fro % rows), 1.0, 0.0).astype(BF16)
    for base, blocks in ((0, kb), (rows, vb)):
        spread = dot(perm, blocks[...])
        for t in range(heads):
            out_ref[base : base + rows, t * slots : (t + 1) * slots, :] = (
                spread[:, t * HD : (t + 1) * HD].reshape(rows, slots, HD).astype(BF16)
            )
    ent = 2 * slots
    ent_row = iota((ent, reqs), 0)
    req_lane = iota((ent, reqs), 1)
    sel = jnp.where((ent_row == slots) & (req_lane == my), 1.0, 0.0)
    in_use = iota(table_ref.shape, 0) < count_ref[...]
    table = jnp.where(in_use, table_ref[...], -1)
    for g in range(slots):
        hit = jnp.where(table == my * slots + g, 1.0, 0.0)
        sel = jnp.where(ent_row == g, jnp.max(hit, axis=0, keepdims=True), sel)
    sel_b = sel.astype(BF16)
    same = lax.dot_general(sel_b, sel_b, NT, preferred_element_type=F32)
    q_lane = iota((ent, width), 1) // HD
    pieces = []
    for k in range(topk):
        group_query = dot(sel_b, q_rows[:, k, :].astype(BF16))
        for h in range(heads):
            pieces.append(jnp.where(q_lane == h, group_query, 0.0))
    queries = jnp.concatenate(pieces, axis=0)
    kh = topk * heads
    scale = 1.0 / math.sqrt(HD)
    scores = lax.dot_general(queries.astype(BF16), kb[...], NT, preferred_element_type=F32) * scale
    col = iota((kh * ent, n), 1)
    scores = scores + jnp.where(col % rows == rows - 1, math.log(page_len - rows + 1), 0.0)
    of_page = jnp.where(iota((ent, n), 1) // rows == iota((ent, n), 0), 1.0, 0.0).astype(BF16)
    shared = dot(same.astype(BF16), of_page)
    mask = jnp.concatenate([shared] * kh, axis=0) > 0.5
    scores = jnp.where(mask, scores, NEGATIVE)
    is_own = iota((kh * ent, 1), 0) % ent == slots
    own = jnp.sum(queries * nk_ref[...].astype(F32), axis=1, keepdims=True) * scale
    own = jnp.where(is_own, own, NEGATIVE)
    peak = jnp.maximum(jnp.max(scores, axis=1, keepdims=True), own)
    shift = peak.astype(BF16).astype(F32)
    probs = jnp.where(mask, jnp.exp(scores - shift), 0.0)
    own_prob = jnp.where(is_own, jnp.exp(own - shift), 0.0)
    den = jnp.sum(probs, axis=1, keepdims=True) + own_prob
    num = dot(probs.astype(BF16), vb[...])
    num = num + own_prob.astype(BF16).astype(F32) * nv_ref[...].astype(F32)
    high = den.astype(BF16).astype(F32)
    low = den - high
    er = iota((ent, ent), 0)
    ec = iota((ent, ent), 1)
    before = jnp.sum(jnp.where((ec < er) | (ec == slots), same, 0.0), axis=1, keepdims=True)
    row = ent_row[:, 0:1]
    first = (row == slots) | ((row < slots) & (before < 0.5))
    request = jnp.sum(jnp.where(sel > 0.5, req_lane.astype(F32), 0.0), axis=1, keepdims=True)
    expert = [
        jnp.sum(jnp.where(sel > 0.5, ids_ref[k : k + 1, :].astype(F32), 0.0), axis=1, keepdims=True)
        for k in range(topk)
    ]
    expert_lane = iota((1, EXPERTS), 1).astype(F32)
    logit = [
        jnp.sum(
            jnp.where(expert_lane == expert[k][slots : slots + 1, :], logit_ref[...], 0.0),
            axis=1,
            keepdims=True,
        )
        for k in range(topk)
    ]
    top = logit[0]
    for k in range(1, topk):
        top = jnp.maximum(top, logit[k])
    terms = [jnp.exp(logit[k] - top) for k in range(topk)]
    term_sum = terms[0]
    for k in range(1, topk):
        term_sum = term_sum + terms[k]
    stat_lane = iota((ent, HD), 1)
    by_choice = []
    for k in range(topk):
        gate = jnp.where(row == slots, terms[k] / term_sum, 0.0)
        gate_high = gate.astype(BF16).astype(F32)
        stats = jnp.where(stat_lane == 3 * heads, gate_high, 0.0)
        stats = jnp.where(stat_lane == 3 * heads + 1, gate - gate_high, stats)
        stats = jnp.where(stat_lane == 3 * heads + 2, request, stats)
        lanes = []
        for h in range(heads):
            at = slice((k * heads + h) * ent, (k * heads + h + 1) * ent)
            lanes.append(num[at, h * HD : (h + 1) * HD])
            for i, stat in enumerate((shift, high, low)):
                stats = jnp.where(stat_lane == 3 * h + i, stat[at, :], stats)
        by_choice.append(jnp.concatenate(lanes + [stats], axis=1))
    parts = []
    for e in range(EXPERTS):
        part = jnp.zeros(by_choice[0].shape, F32)
        for k in range(topk):
            part = jnp.where(first & (expert[k] == e), by_choice[k], part)
        parts.append(part)
    entries = jnp.concatenate(parts, axis=0).astype(BF16)
    columns = out_ref.shape[0] // EXPERTS
    cut = width // columns
    at = iota((width + HD, columns * HD), 1)
    l = at % HD
    j = at // HD
    head_stat = width + (j * cut // HD) * 3 + l - cut
    rest_stat = width + 3 * heads + l - cut - 3
    origin = jnp.where(l < cut, j * cut + l, jnp.where(l < cut + 3, head_stat, rest_stat))
    origin = jnp.where(l < cut + 6, origin, -1)
    choose = jnp.where(iota(at.shape, 0) == origin, 1.0, 0.0).astype(BF16)
    sent = dot(entries, choose).astype(BF16)
    for e in range(EXPERTS):
        for j in range(columns):
            part_ref[e * columns + j] = sent[e * ent : (e + 1) * ent, j * HD : (j + 1) * HD]


def expert_kernel(at_ref, got_ref, *refs):
    columns = got_ref.shape[0] // EXPERTS
    w_refs, out_refs, (stack,) = refs[:columns], refs[columns:-1], refs[-1:]
    j = at_ref[0]
    s = at_ref[1]
    reqs, ent, _ = got_ref.shape
    cut = w_refs[0].shape[0]
    for d in range(columns):
        stack[d] = w_refs[d][...]
    v = got_ref[...].astype(F32).reshape(reqs * ent, HD)
    lane = iota(v.shape, 1)
    shift = v[:, cut : cut + 1]
    den = v[:, cut + 1 : cut + 2] + v[:, cut + 2 : cut + 3]
    request = v[:, cut + 5 : cut + 6]
    live = den > 0.0
    owns = (request == lane.astype(F32)) & live
    peak = jnp.max(jnp.where(owns, shift, NEGATIVE), axis=0, keepdims=True)
    peak = jnp.sum(jnp.where(owns, peak, 0.0), axis=1, keepdims=True)
    factor = jnp.where(live, jnp.exp(shift - peak), 0.0)
    scaled = jnp.where((lane < cut + 3), v * factor, v)
    high = scaled.astype(BF16)
    low = (scaled - high.astype(F32)).astype(BF16)
    pick = jnp.where(owns, 1.0, 0.0).astype(BF16)
    TN = (((0,), (0,)), ((), ()))
    x = lax.dot_general(pick, high, TN, preferred_element_type=F32)
    x = x + lax.dot_general(pick, low, TN, preferred_element_type=F32)
    x = x[:reqs]
    den = x[:, cut + 1 : cut + 2] + x[:, cut + 2 : cut + 3]
    gate = x[:, cut + 3 : cut + 4] + x[:, cut + 4 : cut + 5]
    some = den > 0.0
    weighted = jnp.where(some, gate * (x / jnp.where(some, den, 1.0)), 0.0)[:, :cut].astype(BF16)
    per = columns // len(out_refs)
    for t, out_ref in enumerate(out_refs):
        for i in range(per):
            c = lax.rem(s + t, len(out_refs)) * per + i
            out_ref[i] = dot(weighted, stack[c ^ j]).astype(out_ref.dtype)


def route_kernel(new_ref, table_ref, count_ref, out_ref):
    max_new = new_ref.shape[0]
    per_new = table_ref.shape[0] // max_new
    shape = (out_ref.shape[0], new_ref.shape[1])
    slot = iota(shape, 0) // per_new
    quarter = iota(shape, 0) % per_new
    found = jnp.zeros(shape, jnp.int32)
    for i in range(max_new):
        filled = jnp.where(i * per_new < count_ref[...], new_ref[i : i + 1, :], -1)
        page = jnp.zeros(shape, jnp.int32)
        for w in range(per_new):
            page = jnp.where(quarter == w, table_ref[i * per_new + w : i * per_new + w + 1, :] + 1, page)
        found = jnp.where(filled == slot, page, found)
    out_ref[...] = jnp.sum(found, axis=1, keepdims=True) - 1


def relay_kernel(source_ref, rows_ref, *refs):
    sum_refs, (out_ref, terms) = refs[:-2], refs[-2:]
    devices, lines, _ = rows_ref.shape
    terms_at = out_ref.shape[1] - terms.shape[1]
    half = terms.shape[1] // 2
    per = sum_refs[0].shape[0]
    for i in range(per):
        total = sum_refs[0][i].astype(F32)
        for ref in sum_refs[1:]:
            total = total + ref[i].astype(F32)
        for t in range(half // per):
            part = total[:, t * HD : (t + 1) * HD]
            high = part.astype(BF16).astype(F32)
            terms[:, i * (half // per) + t, :] = high
            terms[:, half + i * (half // per) + t, :] = part - high
    out_ref[:, terms_at:, :] = terms[...].astype(BF16)
    tiles = 4
    slots = lines // tiles
    held = devices * slots
    local = terms_at // tiles
    table = jnp.concatenate(
        [
            rows_ref[:, t * slots : (t + 1) * slots, :].astype(F32).reshape(held, HD).astype(BF16)
            for t in range(tiles)
        ],
        axis=1,
    )
    step = 16
    for c in range(0, devices, step):
        source = source_ref[c * local : (c + step) * local, :]
        pick = jnp.where(source == iota((step * local, held), 1), 1.0, 0.0).astype(BF16)
        rows = dot(pick, table)
        for t in range(tiles):
            out_ref[c : c + step, t * local : (t + 1) * local, :] = (
                rows[:, t * HD : (t + 1) * HD].reshape(step, local, HD).astype(BF16)
            )


def land_kernel(got_ref, k_ref, v_ref, mixed_ref):
    total = got_ref.shape[0]
    tiles = k_ref.shape[2] // HD
    terms_at = got_ref.shape[1] - 2 * tiles
    local = terms_at // tiles
    rows = total // 2
    n = rows * local
    to = iota((n, n), 0)
    fro = iota((n, n), 1)
    perm = jnp.where((to // rows == fro % local) & (to % rows == fro // local), 1.0, 0.0).astype(BF16)
    for base, ref in ((0, k_ref), (rows, v_ref)):
        flat = jnp.concatenate(
            [
                got_ref[base : base + rows, t * local : (t + 1) * local, :].reshape(n, HD)
                for t in range(tiles)
            ],
            axis=1,
        )
        ref[...] = dot(perm, flat).reshape(ref.shape).astype(BF16)
    terms = jnp.sum(got_ref[:, terms_at:, :].astype(F32), axis=0)
    mixed = (terms[:tiles] + terms[tiles:]).astype(BF16)
    for t in range(tiles):
        mixed_ref[:, t * HD : (t + 1) * HD] = mixed[t : t + 1, :]


def shards(
    old_keys,
    old_values,
    keep_lists,
    drop_weights,
    request_pages,
    page_table,
    new_table,
    queries,
    new_keys,
    new_values,
    expert_ids,
    router_logits,
    out_weight,
):
    devices = lax.axis_size("pages")
    shard_count = lax.axis_size("expert")
    my = lax.axis_index("pages").astype(jnp.int32)
    shard = lax.axis_index("expert").astype(jnp.int32)
    slots, page_len, width = old_keys.shape
    rows = keep_lists.shape[1] + 1
    per_new = page_len // rows
    requests, max_pages = page_table.shape
    new_cap = 2 * (slots // per_new)
    local = new_cap * per_new
    heads = width // HD
    topk = queries.shape[1]
    ent = 2 * slots
    columns = devices // EXPERTS
    cut = width // columns
    place = lax.rem(my, columns)
    table = page_table.T
    counts = request_pages.reshape(1, -1)

    row_outbox, part_outbox = pl.pallas_call(
        source_kernel,
        out_shape=(
            jax.ShapeDtypeStruct((devices, heads * slots, HD), BF16),
            jax.ShapeDtypeStruct((devices, ent, HD), BF16),
        ),
        in_specs=[SMEM] + [VMEM] * 11,
        out_specs=(VMEM, VMEM),
        scratch_shapes=[
            pltpu.VMEM((slots * rows, width), BF16),
            pltpu.VMEM((slots * rows, width), BF16),
            pltpu.VMEM((slots, HD), F32),
            pltpu.VMEM((requests, topk, width), F32),
        ],
        name="source",
    )(
        my.reshape(1),
        table,
        counts,
        expert_ids.T,
        keep_lists,
        drop_weights,
        old_keys,
        old_values,
        queries,
        new_keys,
        new_values,
        router_logits,
    )
    part_inbox = lax.all_to_all(part_outbox, "pages", split_axis=0, concat_axis=0, tiled=True)

    weight, _ = lax.optimization_barrier((out_weight[0], part_outbox))
    weight_rows = []
    for d in range(columns):
        piece = lax.dynamic_slice_in_dim(weight, (place ^ d) * cut, cut, 0)
        if d:
            swap = [(p, p // columns * columns + (p % columns ^ d)) for p in range(devices)]
            piece = lax.ppermute(piece, "pages", swap)
        weight_rows.append(piece)
    row_outbox, part_inbox, weight_rows = lax.optimization_barrier(
        (row_outbox, part_inbox, weight_rows)
    )
    row_inbox = lax.all_to_all(row_outbox, "pages", split_axis=0, concat_axis=0, tiled=True)

    source = pl.pallas_call(
        route_kernel,
        out_shape=jax.ShapeDtypeStruct((devices * local, 1), jnp.int32),
        in_specs=[VMEM] * 3,
        out_specs=VMEM,
        name="route",
    )(new_table.T, table, counts)
    per = columns // shard_count
    block_cols = out_weight.shape[2]
    contribs = pl.pallas_call(
        expert_kernel,
        out_shape=[jax.ShapeDtypeStruct((per, requests, block_cols), BF16)] * shard_count,
        in_specs=[SMEM] + [VMEM] * (1 + columns),
        out_specs=[VMEM] * shard_count,
        scratch_shapes=[pltpu.VMEM((columns, cut, block_cols), BF16)],
        name="expert",
    )(jnp.stack([place, shard]), part_inbox, *weight_rows)
    moved = [contribs[0]]
    for t in range(1, shard_count):
        moved.append(
            lax.ppermute(contribs[t], "expert", [(i, (i + t) % shard_count) for i in range(shard_count)])
        )
    terms = 2 * per * block_cols // HD
    routed = pl.pallas_call(
        relay_kernel,
        out_shape=jax.ShapeDtypeStruct((devices, heads * local + terms, HD), BF16),
        in_specs=[VMEM] * (2 + shard_count),
        out_specs=VMEM,
        scratch_shapes=[pltpu.VMEM((requests, terms, HD), F32)],
        name="relay",
    )(source, row_inbox, *moved)
    landed = lax.all_to_all(routed, "pages", split_axis=0, concat_axis=0, tiled=True)
    new_page = jax.ShapeDtypeStruct((new_cap, per_new * rows, width), BF16)
    return pl.pallas_call(
        land_kernel,
        out_shape=(new_page, new_page, jax.ShapeDtypeStruct((1, width), BF16)),
        in_specs=[VMEM],
        out_specs=(VMEM, VMEM, VMEM),
        name="land",
    )(landed)


def solution(mesh):
    in_specs = (
        P("pages", None, "expert"),
        P("pages", None, "expert"),
        P("pages", None),
        P("pages", None),
        P(),
        P(),
        P(),
        P(None, None, "expert"),
        P("pages", "expert"),
        P("pages", "expert"),
        P(),
        P("pages", None),
        P("pages", "expert", None),
    )
    out_specs = (P("pages", None, "expert"), P("pages", None, "expert"), P("pages", "expert"))
    return jax.shard_map(shards, mesh=mesh, in_specs=in_specs, out_specs=out_specs, check_vma=False)
```

```python
import math

import jax
import jax.numpy as jnp
from jax import lax
from jax.experimental import pallas as pl
from jax.experimental.pallas import tpu as pltpu
from jax.sharding import PartitionSpec as P

HD = 128
EXPERTS = 8
NEGATIVE = -1e30
F32 = jnp.float32
BF16 = jnp.bfloat16
VMEM = pl.BlockSpec(memory_space=pltpu.VMEM)
SMEM = pl.BlockSpec(memory_space=pltpu.SMEM)
NT = (((1,), (1,)), ((), ()))


def iota(shape, dim):
    return lax.broadcasted_iota(jnp.int32, shape, dim)


def dot(a, b):
    return jnp.dot(a, b, preferred_element_type=F32)


def source_kernel(
    my_ref,
    table_ref,
    count_ref,
    ids_ref,
    keep_ref,
    drop_ref,
    k_ref,
    v_ref,
    q_ref,
    nk_ref,
    nv_ref,
    logit_ref,
    part_ref,
    kb,
    vb,
    keep_rows,
    q_rows,
):
    my = my_ref[0]
    slots, page_len, width = k_ref.shape
    keep_count = keep_ref.shape[1]
    rows = keep_count + 1
    heads = width // HD
    reqs, topk, _ = q_ref.shape
    keep_rows[...] = jnp.full(keep_rows.shape, -1.0, F32)
    keep_rows[:, 0:keep_count] = keep_ref[...].astype(F32)
    keep_columns = keep_rows[...].T[0:rows, :].astype(jnp.int32)
    q_rows[...] = q_ref[...].astype(F32)
    lane = iota((rows, page_len), 1)
    last = iota((rows, page_len), 0) == rows - 1
    for g in range(slots):
        onehot = jnp.where(keep_columns[:, g : g + 1] == lane, 1.0, 0.0)
        kept = jnp.max(onehot, axis=0, keepdims=True)
        coef = jnp.where(kept > 0.0, 0.0, drop_ref[g : g + 1, :].astype(F32))
        total = jnp.sum(coef, axis=1, keepdims=True)
        mat = jnp.where(last, coef, onehot).astype(BF16)
        denom = jnp.where(last[:, 0:1], total, 1.0)
        kb[g * rows : (g + 1) * rows, :] = (dot(mat, k_ref[g]) / denom).astype(BF16)
        vb[g * rows : (g + 1) * rows, :] = (dot(mat, v_ref[g]) / denom).astype(BF16)
    n = slots * rows
    ent = 2 * slots
    ent_row = iota((ent, reqs), 0)
    req_lane = iota((ent, reqs), 1)
    sel = jnp.where((ent_row == slots) & (req_lane == my), 1.0, 0.0)
    in_use = iota(table_ref.shape, 0) < count_ref[...]
    table = jnp.where(in_use, table_ref[...], -1)
    for g in range(slots):
        hit = jnp.where(table == my * slots + g, 1.0, 0.0)
        sel = jnp.where(ent_row == g, jnp.max(hit, axis=0, keepdims=True), sel)
    sel_b = sel.astype(BF16)
    same = lax.dot_general(sel_b, sel_b, NT, preferred_element_type=F32)
    q_lane = iota((ent, width), 1) // HD
    pieces = []
    for k in range(topk):
        group_query = dot(sel_b, q_rows[:, k, :].astype(BF16))
        for h in range(heads):
            pieces.append(jnp.where(q_lane == h, group_query, 0.0))
    queries = jnp.concatenate(pieces, axis=0)
    kh = topk * heads
    scale = 1.0 / math.sqrt(HD)
    scores = lax.dot_general(queries.astype(BF16), kb[...], NT, preferred_element_type=F32) * scale
    col = iota((kh * ent, n), 1)
    scores = scores + jnp.where(col % rows == rows - 1, math.log(page_len - rows + 1), 0.0)
    of_page = jnp.where(iota((ent, n), 1) // rows == iota((ent, n), 0), 1.0, 0.0).astype(BF16)
    shared = dot(same.astype(BF16), of_page)
    mask = jnp.concatenate([shared] * kh, axis=0) > 0.5
    scores = jnp.where(mask, scores, NEGATIVE)
    is_own = iota((kh * ent, 1), 0) % ent == slots
    own = jnp.sum(queries * nk_ref[...].astype(F32), axis=1, keepdims=True) * scale
    own = jnp.where(is_own, own, NEGATIVE)
    peak = jnp.maximum(jnp.max(scores, axis=1, keepdims=True), own)
    shift = peak.astype(BF16).astype(F32)
    probs = jnp.where(mask, jnp.exp(scores - shift), 0.0)
    own_prob = jnp.where(is_own, jnp.exp(own - shift), 0.0)
    den = jnp.sum(probs, axis=1, keepdims=True) + own_prob
    num = dot(probs.astype(BF16), vb[...])
    num = num + own_prob.astype(BF16).astype(F32) * nv_ref[...].astype(F32)
    high = den.astype(BF16).astype(F32)
    low = den - high
    er = iota((ent, ent), 0)
    ec = iota((ent, ent), 1)
    before = jnp.sum(jnp.where((ec < er) | (ec == slots), same, 0.0), axis=1, keepdims=True)
    row = ent_row[:, 0:1]
    first = (row == slots) | ((row < slots) & (before < 0.5))
    request = jnp.sum(jnp.where(sel > 0.5, req_lane.astype(F32), 0.0), axis=1, keepdims=True)
    expert = [
        jnp.sum(jnp.where(sel > 0.5, ids_ref[k : k + 1, :].astype(F32), 0.0), axis=1, keepdims=True)
        for k in range(topk)
    ]
    expert_lane = iota((1, EXPERTS), 1).astype(F32)
    logit = [
        jnp.sum(
            jnp.where(expert_lane == expert[k][slots : slots + 1, :], logit_ref[...], 0.0),
            axis=1,
            keepdims=True,
        )
        for k in range(topk)
    ]
    top = logit[0]
    for k in range(1, topk):
        top = jnp.maximum(top, logit[k])
    terms = [jnp.exp(logit[k] - top) for k in range(topk)]
    term_sum = terms[0]
    for k in range(1, topk):
        term_sum = term_sum + terms[k]
    stat_lane = iota((ent, HD), 1)
    by_choice = []
    for k in range(topk):
        gate = jnp.where(row == slots, terms[k] / term_sum, 0.0)
        gate_high = gate.astype(BF16).astype(F32)
        stats = jnp.where(stat_lane == 3 * heads, gate_high, 0.0)
        stats = jnp.where(stat_lane == 3 * heads + 1, gate - gate_high, stats)
        stats = jnp.where(stat_lane == 3 * heads + 2, request, stats)
        lanes = []
        for h in range(heads):
            at = slice((k * heads + h) * ent, (k * heads + h + 1) * ent)
            lanes.append(num[at, h * HD : (h + 1) * HD])
            for i, stat in enumerate((shift, high, low)):
                stats = jnp.where(stat_lane == 3 * h + i, stat[at, :], stats)
        by_choice.append(jnp.concatenate(lanes + [stats], axis=1))
    parts = []
    for e in range(EXPERTS):
        part = jnp.zeros(by_choice[0].shape, F32)
        for k in range(topk):
            part = jnp.where(first & (expert[k] == e), by_choice[k], part)
        parts.append(part)
    entries = jnp.concatenate(parts, axis=0).astype(BF16)
    devices, lines, _ = part_ref.shape
    columns = devices // EXPERTS
    to = iota((EXPERTS * lines, EXPERTS * ent), 0)
    fro = iota((EXPERTS * lines, EXPERTS * ent), 1)
    alike = to // lines == fro // ent
    line = to % lines
    entry = fro % ent
    one = jnp.where(alike & (line == entry) & (entry <= slots), 1.0, 0.0).astype(BF16)
    two_line = jnp.where(entry == slots, slots + 1, 2 * slots + entry)
    two = jnp.where(alike & (line == two_line) & (entry <= slots), 1.0, 0.0).astype(BF16)
    flat = jnp.where(alike & (line == slots + 2), 1.0, 0.0).astype(BF16)
    for c in range(2):
        base = c * 2 * HD
        lane_out = iota((HD, HD), 1)
        item = lane_out % 9
        origin = jnp.where(item < 6, 6 * c + item, 3 * heads + item - 6)
        copy = jnp.where(iota((HD, HD), 0) == origin, 1.0, 0.0).astype(BF16)
        stats = dot(entries[:, width:], copy)
        mine = iota(stats.shape, 1) // 9 == iota(stats.shape, 0) % ent
        stats = jnp.where(mine, stats, 0.0).astype(BF16)
        sent = dot(one, entries[:, base : base + HD]) + dot(two, entries[:, base + HD : base + 2 * HD])
        sent = (sent + dot(flat, stats)).astype(BF16)
        for e in range(EXPERTS):
            for z in range(columns // 2):
                part_ref[e * columns + 2 * z + c] = sent[e * lines : (e + 1) * lines, :]


def spread_kernel(kb_ref, vb_ref, out_ref):
    n, width = kb_ref.shape
    rows = out_ref.shape[0] // 2
    slots = n // rows
    to = iota((n, n), 0)
    fro = iota((n, n), 1)
    perm = jnp.where((to % slots == fro // rows) & (to // slots == fro % rows), 1.0, 0.0).astype(BF16)
    for base, blocks in ((0, kb_ref), (rows, vb_ref)):
        spread = dot(perm, blocks[...])
        for t in range(width // HD):
            out_ref[base : base + rows, t * slots : (t + 1) * slots, :] = (
                spread[:, t * HD : (t + 1) * HD].reshape(rows, slots, HD).astype(BF16)
            )


def expert_kernel(core_ref, got_ref, w_ref, pair_ref, out_ref, scr):
    core = core_ref[0]
    reqs, lines, _ = got_ref.shape
    slots = lines // 3
    scr[...] = got_ref[...].astype(F32)
    stats = scr[:, slots + 2, :]
    lane = iota((reqs, HD), 1).astype(F32)
    picks = []
    peaks = [jnp.full((1, HD), NEGATIVE, F32) for _ in range(2)]
    for g in range(slots + 1):
        request = stats[:, 9 * g + 8 : 9 * g + 9]
        live = stats[:, 9 * g + 1 : 9 * g + 2] > 0.0
        pick = (request == lane) & live
        picks.append((pick, live))
        for i in range(2):
            shift = stats[:, 9 * g + 3 * i : 9 * g + 3 * i + 1]
            peaks[i] = jnp.maximum(
                peaks[i], jnp.max(jnp.where(pick, shift, NEGATIVE), axis=0, keepdims=True)
            )
    whole = []
    for g in range(slots + 1):
        pick, live = picks[g]
        lanes = []
        sums = jnp.where(lane == 2.0, stats[:, 9 * g + 6 : 9 * g + 7] + stats[:, 9 * g + 7 : 9 * g + 8], 0.0)
        for i in range(2):
            at = 9 * g + 3 * i
            peak = jnp.sum(jnp.where(pick, peaks[i], 0.0), axis=1, keepdims=True)
            factor = jnp.where(live, jnp.exp(stats[:, at : at + 1] - peak), 0.0)
            line = g if i == 0 else (2 * slots + g if g < slots else slots + 1)
            lanes.append(scr[:, line, :] * factor)
            den = stats[:, at + 1 : at + 2] + stats[:, at + 2 : at + 3]
            sums = jnp.where(lane == float(i), den * factor, sums)
        whole.append(jnp.concatenate(lanes + [sums], axis=1))
    pick = jnp.concatenate([jnp.where(p, 1.0, 0.0) for p, _ in picks], axis=0).astype(BF16)
    scaled = jnp.concatenate(whole, axis=0)
    high = scaled.astype(BF16)
    low = (scaled - high.astype(F32)).astype(BF16)
    TN = (((0,), (0,)), ((), ()))
    x = lax.dot_general(pick, high, TN, preferred_element_type=F32)
    x = x + lax.dot_general(pick, low, TN, preferred_element_type=F32)
    x = x[:reqs]
    gate = x[:, 2 * HD + 2 : 2 * HD + 3]
    halves = []
    for i in range(2):
        den = x[:, 2 * HD + i : 2 * HD + i + 1]
        some = den > 0.0
        value = x[:, i * HD : (i + 1) * HD] / jnp.where(some, den, 1.0)
        halves.append(jnp.where(some, gate * value, 0.0))
    weighted = jnp.concatenate(halves, axis=1).astype(BF16)
    depth = weighted.shape[1]
    out_ref[core] = dot(weighted, w_ref[0, pl.ds(core * depth, depth), :])
    out_ref[1 - core] = dot(weighted, pair_ref[...])


def route_kernel(new_ref, table_ref, count_ref, out_ref):
    max_new = new_ref.shape[0]
    per_new = table_ref.shape[0] // max_new
    shape = (out_ref.shape[0], new_ref.shape[1])
    slot = iota(shape, 0) // per_new
    quarter = iota(shape, 0) % per_new
    found = jnp.zeros(shape, jnp.int32)
    for i in range(max_new):
        filled = jnp.where(i * per_new < count_ref[...], new_ref[i : i + 1, :], -1)
        page = jnp.zeros(shape, jnp.int32)
        for w in range(per_new):
            page = jnp.where(quarter == w, table_ref[i * per_new + w : i * per_new + w + 1, :] + 1, page)
        found = jnp.where(filled == slot, page, found)
    out_ref[...] = jnp.sum(found, axis=1, keepdims=True) - 1


def relay_kernel(source_ref, rows_ref, sum_ref, out_ref, terms):
    devices, lines, _ = rows_ref.shape
    terms_at = out_ref.shape[1] - terms.shape[1]
    half = terms.shape[1] // 2
    per = sum_ref.shape[0]
    for i in range(per):
        for t in range(half // per):
            part = sum_ref[i, :, t * HD : (t + 1) * HD]
            high = part.astype(BF16).astype(F32)
            terms[:, i * (half // per) + t, :] = high
            terms[:, half + i * (half // per) + t, :] = part - high
    out_ref[:, terms_at:, :] = terms[...].astype(BF16)
    tiles = 4
    slots = lines // tiles
    held = devices * slots
    local = terms_at // tiles
    table = jnp.concatenate(
        [
            rows_ref[:, t * slots : (t + 1) * slots, :].astype(F32).reshape(held, HD).astype(BF16)
            for t in range(tiles)
        ],
        axis=1,
    )
    step = 16
    for c in range(0, devices, step):
        source = source_ref[c * local : (c + step) * local, :]
        pick = jnp.where(source == iota((step * local, held), 1), 1.0, 0.0).astype(BF16)
        rows = dot(pick, table)
        for t in range(tiles):
            out_ref[c : c + step, t * local : (t + 1) * local, :] = (
                rows[:, t * HD : (t + 1) * HD].reshape(step, local, HD).astype(BF16)
            )


def land_kernel(got_ref, k_ref, v_ref, mixed_ref):
    total = got_ref.shape[0]
    tiles = k_ref.shape[2] // HD
    terms_at = got_ref.shape[1] - 2 * tiles
    local = terms_at // tiles
    rows = total // 2
    n = rows * local
    to = iota((n, n), 0)
    fro = iota((n, n), 1)
    perm = jnp.where((to // rows == fro % local) & (to % rows == fro // local), 1.0, 0.0).astype(BF16)
    for base, ref in ((0, k_ref), (rows, v_ref)):
        flat = jnp.concatenate(
            [
                got_ref[base : base + rows, t * local : (t + 1) * local, :].reshape(n, HD)
                for t in range(tiles)
            ],
            axis=1,
        )
        ref[...] = dot(perm, flat).reshape(ref.shape).astype(BF16)
    terms = jnp.sum(got_ref[:, terms_at:, :].astype(F32), axis=0)
    mixed = (terms[:tiles] + terms[tiles:]).astype(BF16)
    for t in range(tiles):
        mixed_ref[:, t * HD : (t + 1) * HD] = mixed[t : t + 1, :]


def shards(
    old_keys,
    old_values,
    keep_lists,
    drop_weights,
    request_pages,
    page_table,
    new_table,
    queries,
    new_keys,
    new_values,
    expert_ids,
    router_logits,
    out_weight,
):
    devices = lax.axis_size("pages")
    shard_count = lax.axis_size("expert")
    my = lax.axis_index("pages").astype(jnp.int32)
    slots, page_len, width = old_keys.shape
    rows = keep_lists.shape[1] + 1
    per_new = page_len // rows
    requests, max_pages = page_table.shape
    new_cap = 2 * (slots // per_new)
    local = new_cap * per_new
    heads = width // HD
    topk = queries.shape[1]
    lines = 3 * slots
    columns = devices // EXPERTS
    core = lax.rem(my, 2)
    table = page_table.T
    counts = request_pages.reshape(1, -1)

    part_outbox, key_blocks, value_blocks = pl.pallas_call(
        source_kernel,
        out_shape=(
            jax.ShapeDtypeStruct((devices, lines, HD), BF16),
            jax.ShapeDtypeStruct((slots * rows, width), BF16),
            jax.ShapeDtypeStruct((slots * rows, width), BF16),
        ),
        in_specs=[SMEM] + [VMEM] * 11,
        out_specs=(VMEM, VMEM, VMEM),
        scratch_shapes=[
            pltpu.VMEM((slots, HD), F32),
            pltpu.VMEM((requests, topk, width), F32),
        ],
        name="source",
    )(
        my.reshape(1),
        table,
        counts,
        expert_ids.T,
        keep_lists,
        drop_weights,
        old_keys,
        old_values,
        queries,
        new_keys,
        new_values,
        router_logits,
    )
    part_inbox = lax.all_to_all(part_outbox, "pages", split_axis=0, concat_axis=0, tiled=True)

    weight, _ = lax.optimization_barrier((out_weight[0], part_outbox))
    depth = width // 2
    pair_weight = lax.ppermute(
        lax.dynamic_slice_in_dim(weight, (1 - core) * depth, depth, 0),
        "pages",
        [(p, p ^ 1) for p in range(devices)],
    )
    row_outbox = pl.pallas_call(
        spread_kernel,
        out_shape=jax.ShapeDtypeStruct((devices, heads * slots, HD), BF16),
        in_specs=[VMEM, VMEM],
        out_specs=VMEM,
        name="spread",
    )(key_blocks, value_blocks)
    source = pl.pallas_call(
        route_kernel,
        out_shape=jax.ShapeDtypeStruct((devices * local, 1), jnp.int32),
        in_specs=[VMEM] * 3,
        out_specs=VMEM,
        name="route",
    )(new_table.T, table, counts)
    row_outbox, part_inbox, pair_weight, source = lax.optimization_barrier(
        (row_outbox, part_inbox, pair_weight, source)
    )
    row_inbox = lax.all_to_all(row_outbox, "pages", split_axis=0, concat_axis=0, tiled=True)

    block_cols = out_weight.shape[2]
    contrib = pl.pallas_call(
        expert_kernel,
        out_shape=jax.ShapeDtypeStruct((2, requests, block_cols), F32),
        in_specs=[SMEM] + [VMEM] * 3,
        out_specs=VMEM,
        scratch_shapes=[pltpu.VMEM((requests, lines, HD), F32)],
        name="expert",
    )(core.reshape(1), part_inbox, out_weight, pair_weight)
    moves = []
    for e in range(EXPERTS):
        for z in range(columns // 2):
            for c in range(2):
                for s in range(shard_count):
                    here = e * columns + 2 * z + c
                    there = e * columns + 2 * s + c
                    moves.append((here * shard_count + s, there * shard_count + z))
    moved = lax.ppermute(contrib, ("pages", "expert"), moves)
    terms = 2 * 2 * block_cols // HD
    routed = pl.pallas_call(
        relay_kernel,
        out_shape=jax.ShapeDtypeStruct((devices, heads * local + terms, HD), BF16),
        in_specs=[VMEM] * 3,
        out_specs=VMEM,
        scratch_shapes=[pltpu.VMEM((requests, terms, HD), F32)],
        name="relay",
    )(source, row_inbox, moved)
    landed = lax.all_to_all(routed, "pages", split_axis=0, concat_axis=0, tiled=True)
    new_page = jax.ShapeDtypeStruct((new_cap, per_new * rows, width), BF16)
    return pl.pallas_call(
        land_kernel,
        out_shape=(new_page, new_page, jax.ShapeDtypeStruct((1, width), BF16)),
        in_specs=[VMEM],
        out_specs=(VMEM, VMEM, VMEM),
        name="land",
    )(landed)


def solution(mesh):
    in_specs = (
        P("pages", None, "expert"),
        P("pages", None, "expert"),
        P("pages", None),
        P("pages", None),
        P(),
        P(),
        P(),
        P(None, None, "expert"),
        P("pages", "expert"),
        P("pages", "expert"),
        P(),
        P("pages", None),
        P("pages", "expert", None),
    )
    out_specs = (P("pages", None, "expert"), P("pages", None, "expert"), P("pages", "expert"))
    return jax.shard_map(shards, mesh=mesh, in_specs=in_specs, out_specs=out_specs, check_vma=False)
```

```python
import math

import jax
import jax.numpy as jnp
from jax import lax
from jax.experimental import pallas as pl
from jax.experimental.pallas import tpu as pltpu
from jax.sharding import PartitionSpec as P

HD = 128
EXPERTS = 8
NEGATIVE = -1e30
F32 = jnp.float32
BF16 = jnp.bfloat16
VMEM = pl.BlockSpec(memory_space=pltpu.VMEM)
SMEM = pl.BlockSpec(memory_space=pltpu.SMEM)
NT = (((1,), (1,)), ((), ()))


def iota(shape, dim):
    return lax.broadcasted_iota(jnp.int32, shape, dim)


def dot(a, b):
    return jnp.dot(a, b, preferred_element_type=F32)


def source_kernel(
    my_ref,
    table_ref,
    count_ref,
    ids_ref,
    keep_ref,
    drop_ref,
    k_ref,
    v_ref,
    q_ref,
    nk_ref,
    nv_ref,
    logit_ref,
    out_ref,
    kb,
    vb,
    keep_rows,
    q_rows,
):
    my = my_ref[0]
    slots, page_len, width = k_ref.shape
    keep_count = keep_ref.shape[1]
    rows = keep_count + 1
    heads = width // HD
    reqs, topk, _ = q_ref.shape
    keep_rows[...] = jnp.full(keep_rows.shape, -1.0, F32)
    keep_rows[:, 0:keep_count] = keep_ref[...].astype(F32)
    keep_columns = keep_rows[...].T[0:rows, :].astype(jnp.int32)
    q_rows[...] = q_ref[...].astype(F32)
    lane = iota((rows, page_len), 1)
    last = iota((rows, page_len), 0) == rows - 1
    for g in range(slots):
        onehot = jnp.where(keep_columns[:, g : g + 1] == lane, 1.0, 0.0)
        kept = jnp.max(onehot, axis=0, keepdims=True)
        coef = jnp.where(kept > 0.0, 0.0, drop_ref[g : g + 1, :].astype(F32))
        total = jnp.sum(coef, axis=1, keepdims=True)
        mat = jnp.where(last, coef, onehot).astype(BF16)
        denom = jnp.where(last[:, 0:1], total, 1.0)
        kb[g * rows : (g + 1) * rows, :] = (dot(mat, k_ref[g]) / denom).astype(BF16)
        vb[g * rows : (g + 1) * rows, :] = (dot(mat, v_ref[g]) / denom).astype(BF16)
    n = slots * rows
    ent = 2 * slots
    ent_row = iota((ent, reqs), 0)
    req_lane = iota((ent, reqs), 1)
    sel = jnp.where((ent_row == slots) & (req_lane == my), 1.0, 0.0)
    in_use = iota(table_ref.shape, 0) < count_ref[...]
    table = jnp.where(in_use, table_ref[...], -1)
    for g in range(slots):
        hit = jnp.where(table == my * slots + g, 1.0, 0.0)
        sel = jnp.where(ent_row == g, jnp.max(hit, axis=0, keepdims=True), sel)
    sel_b = sel.astype(BF16)
    same = lax.dot_general(sel_b, sel_b, NT, preferred_element_type=F32)
    q_lane = iota((ent, width), 1) // HD
    pieces = []
    for k in range(topk):
        group_query = dot(sel_b, q_rows[:, k, :].astype(BF16))
        for h in range(heads):
            pieces.append(jnp.where(q_lane == h, group_query, 0.0))
    queries = jnp.concatenate(pieces, axis=0)
    kh = topk * heads
    scale = 1.0 / math.sqrt(HD)
    scores = lax.dot_general(queries.astype(BF16), kb[...], NT, preferred_element_type=F32) * scale
    col = iota((kh * ent, n), 1)
    scores = scores + jnp.where(col % rows == rows - 1, math.log(page_len - rows + 1), 0.0)
    of_page = jnp.where(iota((ent, n), 1) // rows == iota((ent, n), 0), 1.0, 0.0).astype(BF16)
    shared = dot(same.astype(BF16), of_page)
    mask = jnp.concatenate([shared] * kh, axis=0) > 0.5
    scores = jnp.where(mask, scores, NEGATIVE)
    is_own = iota((kh * ent, 1), 0) % ent == slots
    own = jnp.sum(queries * nk_ref[...].astype(F32), axis=1, keepdims=True) * scale
    own = jnp.where(is_own, own, NEGATIVE)
    peak = jnp.maximum(jnp.max(scores, axis=1, keepdims=True), own)
    shift = peak.astype(BF16).astype(F32)
    probs = jnp.where(mask, jnp.exp(scores - shift), 0.0)
    own_prob = jnp.where(is_own, jnp.exp(own - shift), 0.0)
    den = jnp.sum(probs, axis=1, keepdims=True) + own_prob
    num = dot(probs.astype(BF16), vb[...])
    num = num + own_prob.astype(BF16).astype(F32) * nv_ref[...].astype(F32)
    high = den.astype(BF16).astype(F32)
    low = den - high
    er = iota((ent, ent), 0)
    ec = iota((ent, ent), 1)
    before = jnp.sum(jnp.where((ec < er) | (ec == slots), same, 0.0), axis=1, keepdims=True)
    row = ent_row[:, 0:1]
    first = (row == slots) | ((row < slots) & (before < 0.5))
    request = jnp.sum(jnp.where(sel > 0.5, req_lane.astype(F32), 0.0), axis=1, keepdims=True)
    expert = [
        jnp.sum(jnp.where(sel > 0.5, ids_ref[k : k + 1, :].astype(F32), 0.0), axis=1, keepdims=True)
        for k in range(topk)
    ]
    expert_lane = iota((1, EXPERTS), 1).astype(F32)
    logit = [
        jnp.sum(
            jnp.where(expert_lane == expert[k][slots : slots + 1, :], logit_ref[...], 0.0),
            axis=1,
            keepdims=True,
        )
        for k in range(topk)
    ]
    top = logit[0]
    for k in range(1, topk):
        top = jnp.maximum(top, logit[k])
    terms = [jnp.exp(logit[k] - top) for k in range(topk)]
    term_sum = terms[0]
    for k in range(1, topk):
        term_sum = term_sum + terms[k]
    stat_lane = iota((ent, HD), 1)
    by_choice = []
    for k in range(topk):
        gate = jnp.where(row == slots, terms[k] / term_sum, 0.0)
        gate_high = gate.astype(BF16).astype(F32)
        stats = jnp.where(stat_lane == 3 * heads, gate_high, 0.0)
        stats = jnp.where(stat_lane == 3 * heads + 1, gate - gate_high, stats)
        stats = jnp.where(stat_lane == 3 * heads + 2, request, stats)
        lanes = []
        for h in range(heads):
            at = slice((k * heads + h) * ent, (k * heads + h + 1) * ent)
            lanes.append(num[at, h * HD : (h + 1) * HD])
            for i, stat in enumerate((shift, high, low)):
                stats = jnp.where(stat_lane == 3 * h + i, stat[at, :], stats)
        by_choice.append(jnp.concatenate(lanes + [stats], axis=1))
    parts = []
    for e in range(EXPERTS):
        part = jnp.zeros(by_choice[0].shape, F32)
        for k in range(topk):
            part = jnp.where(first & (expert[k] == e), by_choice[k], part)
        parts.append(part)
    entries = jnp.concatenate(parts, axis=0).astype(BF16)
    devices = out_ref.shape[0]
    lines = out_ref.shape[1] - heads * slots
    columns = devices // EXPERTS
    to = iota((EXPERTS * lines, EXPERTS * ent), 0)
    fro = iota((EXPERTS * lines, EXPERTS * ent), 1)
    alike = to // lines == fro // ent
    line = to % lines
    entry = fro % ent
    one = jnp.where(alike & (line == entry) & (entry <= slots), 1.0, 0.0).astype(BF16)
    two_line = jnp.where(entry == slots, slots + 1, 2 * slots + entry)
    two = jnp.where(alike & (line == two_line) & (entry <= slots), 1.0, 0.0).astype(BF16)
    flat = jnp.where(alike & (line == slots + 2), 1.0, 0.0).astype(BF16)
    for c in range(2):
        base = c * 2 * HD
        lane_out = iota((HD, HD), 1)
        item = lane_out % 9
        origin = jnp.where(item < 6, 6 * c + item, 3 * heads + item - 6)
        copy = jnp.where(iota((HD, HD), 0) == origin, 1.0, 0.0).astype(BF16)
        stats = dot(entries[:, width:], copy)
        mine = iota(stats.shape, 1) // 9 == iota(stats.shape, 0) % ent
        stats = jnp.where(mine, stats, 0.0).astype(BF16)
        sent = dot(one, entries[:, base : base + HD]) + dot(two, entries[:, base + HD : base + 2 * HD])
        sent = (sent + dot(flat, stats)).astype(BF16)
        for e in range(EXPERTS):
            for z in range(columns // 2):
                out_ref[e * columns + 2 * z + c, 0:lines, :] = sent[e * lines : (e + 1) * lines, :]
    to = iota((n, n), 0)
    fro = iota((n, n), 1)
    perm = jnp.where((to % slots == fro // rows) & (to // slots == fro % rows), 1.0, 0.0).astype(BF16)
    for base, blocks in ((0, kb), (rows, vb)):
        spread = dot(perm, blocks[...])
        for t in range(heads):
            at = slice(lines + t * slots, lines + (t + 1) * slots)
            out_ref[base : base + rows, at, :] = (
                spread[:, t * HD : (t + 1) * HD].reshape(rows, slots, HD).astype(BF16)
            )


def expert_kernel(core_ref, got_ref, w_ref, pair_ref, out_ref, scr):
    core = core_ref[0]
    reqs, lines, _ = got_ref.shape
    slots = lines // 3
    scr[...] = got_ref[...].astype(F32)
    stats = scr[:, slots + 2, :]
    stats = jnp.concatenate([stats, stats], axis=0).T
    left = iota((1, 2 * reqs), 1) < reqs
    target = iota((reqs, 2 * reqs), 0).astype(F32)

    def item(g, i):
        first = stats[9 * g + i : 9 * g + i + 1, :]
        if g == slots:
            return jnp.where(left, first, 0.0)
        return jnp.where(left, first, stats[9 * g + 9 + i : 9 * g + 10 + i, :])

    groups = range(0, slots + 1, 2)
    picks = [(item(g, 8) == target) & (item(g, 1) > 0.0) for g in groups]
    gate = jnp.zeros(target.shape, F32)
    for g, pick in zip(groups, picks):
        gate = gate + jnp.where(pick, item(g, 6) + item(g, 7), 0.0)
    gate = jnp.sum(gate, axis=1, keepdims=True)
    halves = []
    for i in range(2):
        peak = jnp.full(target.shape, NEGATIVE, F32)
        for g, pick in zip(groups, picks):
            peak = jnp.maximum(peak, jnp.where(pick, item(g, 3 * i), NEGATIVE))
        peak = jnp.max(peak, axis=1, keepdims=True)
        den = jnp.zeros(target.shape, F32)
        num = jnp.zeros((2 * reqs, HD), F32)
        for g, pick in zip(groups, picks):
            factor = jnp.where(pick, jnp.exp(item(g, 3 * i) - peak), 0.0)
            den = den + factor * (item(g, 3 * i + 1) + item(g, 3 * i + 2))
            high = factor.astype(BF16)
            low = (factor - high.astype(F32)).astype(BF16)
            entries = []
            for entry in (g, min(g + 1, slots)):
                line = entry if i == 0 else (2 * slots + entry if entry < slots else slots + 1)
                entries.append(scr[:, line, :])
            entries = jnp.concatenate(entries, axis=0).astype(BF16)
            num = num + dot(jnp.concatenate([high, low], axis=0), entries)
        den = jnp.sum(den, axis=1, keepdims=True)
        some = den > 0.0
        value = (num[:reqs] + num[reqs:]) / jnp.where(some, den, 1.0)
        halves.append(jnp.where(some, gate * value, 0.0))
    weighted = jnp.concatenate(halves, axis=1).astype(BF16)
    depth = weighted.shape[1]
    out_ref[core] = dot(weighted, w_ref[0, pl.ds(core * depth, depth), :]).astype(BF16)
    out_ref[1 - core] = dot(weighted, pair_ref[...]).astype(BF16)


def route_kernel(new_ref, table_ref, count_ref, out_ref):
    max_new = new_ref.shape[0]
    per_new = table_ref.shape[0] // max_new
    shape = (out_ref.shape[0], new_ref.shape[1])
    slot = iota(shape, 0) // per_new
    quarter = iota(shape, 0) % per_new
    found = jnp.zeros(shape, jnp.int32)
    for i in range(max_new):
        filled = jnp.where(i * per_new < count_ref[...], new_ref[i : i + 1, :], -1)
        page = jnp.zeros(shape, jnp.int32)
        for w in range(per_new):
            page = jnp.where(quarter == w, table_ref[i * per_new + w : i * per_new + w + 1, :] + 1, page)
        found = jnp.where(filled == slot, page, found)
    out_ref[...] = jnp.sum(found, axis=1, keepdims=True) - 1


def relay_kernel(source_ref, *refs):
    row_refs, out_ref = refs[:-1], refs[-1]
    tiles = len(row_refs)
    devices, slots, _ = row_refs[0].shape
    held = devices * slots
    local = source_ref.shape[0] // devices
    table = jnp.concatenate(
        [ref[...].astype(F32).reshape(held, HD).astype(BF16) for ref in row_refs], axis=1
    )
    step = 16
    for c in range(0, devices, step):
        source = source_ref[c * local : (c + step) * local, :]
        pick = jnp.where(source == iota((step * local, held), 1), 1.0, 0.0).astype(BF16)
        rows = dot(pick, table)
        for t in range(tiles):
            out_ref[c : c + step, t * local : (t + 1) * local, :] = (
                rows[:, t * HD : (t + 1) * HD].reshape(step, local, HD).astype(BF16)
            )


def append_kernel(routed_ref, sum_ref, out_ref, terms):
    del routed_ref
    terms[...] = jnp.zeros(terms.shape, F32)
    per, _, cols = sum_ref.shape
    for i in range(per):
        for t in range(cols // HD):
            terms[:, i * (cols // HD) + t, :] = sum_ref[i, :, t * HD : (t + 1) * HD].astype(F32)
    out_ref[...] = terms[...].astype(BF16)


def land_kernel(got_ref, k_ref, v_ref, mixed_ref):
    total = got_ref.shape[0]
    tiles = k_ref.shape[2] // HD
    terms_at = got_ref.shape[1] // (4 * tiles) * (4 * tiles)
    local = terms_at // tiles
    rows = total // 2
    n = rows * local
    to = iota((n, n), 0)
    fro = iota((n, n), 1)
    perm = jnp.where((to // rows == fro % local) & (to % rows == fro // local), 1.0, 0.0).astype(BF16)
    for base, ref in ((0, k_ref), (rows, v_ref)):
        flat = jnp.concatenate(
            [
                got_ref[base : base + rows, t * local : (t + 1) * local, :].reshape(n, HD)
                for t in range(tiles)
            ],
            axis=1,
        )
        ref[...] = dot(perm, flat).reshape(ref.shape).astype(BF16)
    terms = jnp.sum(got_ref[:, terms_at:, :].astype(F32), axis=0)
    mixed = terms[:tiles].astype(BF16)
    for t in range(tiles):
        mixed_ref[:, t * HD : (t + 1) * HD] = mixed[t : t + 1, :]


def shards(
    old_keys,
    old_values,
    keep_lists,
    drop_weights,
    request_pages,
    page_table,
    new_table,
    queries,
    new_keys,
    new_values,
    expert_ids,
    router_logits,
    out_weight,
):
    devices = lax.axis_size("pages")
    shard_count = lax.axis_size("expert")
    my = lax.axis_index("pages").astype(jnp.int32)
    slots, page_len, width = old_keys.shape
    rows = keep_lists.shape[1] + 1
    per_new = page_len // rows
    requests, max_pages = page_table.shape
    new_cap = 2 * (slots // per_new)
    local = new_cap * per_new
    heads = width // HD
    topk = queries.shape[1]
    lines = 3 * slots
    columns = devices // EXPERTS
    core = lax.rem(my, 2)
    table = page_table.T
    counts = request_pages.reshape(1, -1)

    outbox = pl.pallas_call(
        source_kernel,
        out_shape=jax.ShapeDtypeStruct((devices, lines + heads * slots, HD), BF16),
        in_specs=[SMEM] + [VMEM] * 11,
        out_specs=VMEM,
        scratch_shapes=[
            pltpu.VMEM((slots * rows, width), BF16),
            pltpu.VMEM((slots * rows, width), BF16),
            pltpu.VMEM((slots, HD), F32),
            pltpu.VMEM((requests, topk, width), F32),
        ],
        name="source",
    )(
        my.reshape(1),
        table,
        counts,
        expert_ids.T,
        keep_lists,
        drop_weights,
        old_keys,
        old_values,
        queries,
        new_keys,
        new_values,
        router_logits,
    )
    inbox = lax.all_to_all(outbox, "pages", split_axis=0, concat_axis=0, tiled=True)

    weight, _ = lax.optimization_barrier((out_weight[0], outbox))
    depth = width // 2
    pair_weight = lax.ppermute(
        lax.dynamic_slice_in_dim(weight, (1 - core) * depth, depth, 0),
        "pages",
        [(p, p ^ 1) for p in range(devices)],
    )
    source = pl.pallas_call(
        route_kernel,
        out_shape=jax.ShapeDtypeStruct((devices * local, 1), jnp.int32),
        in_specs=[VMEM] * 3,
        out_specs=VMEM,
        name="route",
    )(new_table.T, table, counts)
    inbox, pair_weight, source = lax.optimization_barrier((inbox, pair_weight, source))

    block_cols = out_weight.shape[2]
    contrib = pl.pallas_call(
        expert_kernel,
        grid=(1,),
        out_shape=jax.ShapeDtypeStruct((2, requests, block_cols), BF16),
        in_specs=[SMEM, pl.BlockSpec((devices, lines, HD), lambda i: (0, 0, 0)), VMEM, VMEM],
        out_specs=VMEM,
        scratch_shapes=[pltpu.VMEM((requests, lines, HD), F32)],
        name="expert",
    )(core.reshape(1), inbox, out_weight, pair_weight)
    moves = []
    for e in range(EXPERTS):
        for z in range(columns // 2):
            for c in range(2):
                for s in range(shard_count):
                    here = e * columns + 2 * z + c
                    there = e * columns + 2 * s + c
                    moves.append((here * shard_count + s, there * shard_count + z))
    moved = lax.ppermute(contrib, ("pages", "expert"), moves)

    source, _ = lax.optimization_barrier((source, contrib))
    chunk = heads * local + slots
    routed = pl.pallas_call(
        relay_kernel,
        grid=(1,),
        out_shape=jax.ShapeDtypeStruct((devices, chunk, HD), BF16),
        in_specs=[VMEM]
        + [
            pl.BlockSpec((devices, slots, HD), lambda i, t=t: (0, lines // slots + t, 0))
            for t in range(heads)
        ],
        out_specs=VMEM,
        name="relay",
    )(source, *[inbox] * heads)
    routed = pl.pallas_call(
        append_kernel,
        grid=(1,),
        out_shape=jax.ShapeDtypeStruct((devices, chunk, HD), BF16),
        in_specs=[pl.BlockSpec(memory_space=pl.ANY), VMEM],
        out_specs=pl.BlockSpec((devices, slots, HD), lambda i: (0, heads * local // slots, 0)),
        scratch_shapes=[pltpu.VMEM((requests, slots, HD), F32)],
        input_output_aliases={0: 0},
        name="append",
    )(routed, moved)
    landed = lax.all_to_all(routed, "pages", split_axis=0, concat_axis=0, tiled=True)
    new_page = jax.ShapeDtypeStruct((new_cap, per_new * rows, width), BF16)
    return pl.pallas_call(
        land_kernel,
        out_shape=(new_page, new_page, jax.ShapeDtypeStruct((1, width), BF16)),
        in_specs=[VMEM],
        out_specs=(VMEM, VMEM, VMEM),
        name="land",
    )(landed)


def solution(mesh):
    in_specs = (
        P("pages", None, "expert"),
        P("pages", None, "expert"),
        P("pages", None),
        P("pages", None),
        P(),
        P(),
        P(),
        P(None, None, "expert"),
        P("pages", "expert"),
        P("pages", "expert"),
        P(),
        P("pages", None),
        P("pages", "expert", None),
    )
    out_specs = (P("pages", None, "expert"), P("pages", None, "expert"), P("pages", "expert"))
    return jax.shard_map(shards, mesh=mesh, in_specs=in_specs, out_specs=out_specs, check_vma=False)
```

```python
import math

import jax
import jax.numpy as jnp
from jax import lax
from jax.experimental import pallas as pl
from jax.experimental.pallas import tpu as pltpu
from jax.sharding import PartitionSpec as P

HD = 128
EXPERTS = 8
NEGATIVE = -1e30
F32 = jnp.float32
BF16 = jnp.bfloat16
VMEM = pl.BlockSpec(memory_space=pltpu.VMEM)
SMEM = pl.BlockSpec(memory_space=pltpu.SMEM)
NT = (((1,), (1,)), ((), ()))


def iota(shape, dim):
    return lax.broadcasted_iota(jnp.int32, shape, dim)


def dot(a, b):
    return jnp.dot(a, b, preferred_element_type=F32)


def source_kernel(
    my_ref,
    table_ref,
    count_ref,
    ids_ref,
    keep_ref,
    drop_ref,
    k_ref,
    v_ref,
    q_ref,
    nk_ref,
    nv_ref,
    logit_ref,
    out_ref,
    kb,
    vb,
    keep_rows,
    q_rows,
):
    my = my_ref[0]
    slots, page_len, width = k_ref.shape
    keep_count = keep_ref.shape[1]
    rows = keep_count + 1
    heads = width // HD
    reqs, topk, _ = q_ref.shape
    keep_rows[...] = jnp.full(keep_rows.shape, -1.0, F32)
    keep_rows[:, 0:keep_count] = keep_ref[...].astype(F32)
    keep_columns = keep_rows[...].T[0:rows, :].astype(jnp.int32)
    q_rows[...] = q_ref[...].astype(F32)
    lane = iota((rows, page_len), 1)
    last = iota((rows, page_len), 0) == rows - 1
    for g in range(slots):
        onehot = jnp.where(keep_columns[:, g : g + 1] == lane, 1.0, 0.0)
        kept = jnp.max(onehot, axis=0, keepdims=True)
        coef = jnp.where(kept > 0.0, 0.0, drop_ref[g : g + 1, :].astype(F32))
        total = jnp.sum(coef, axis=1, keepdims=True)
        mat = jnp.where(last, coef, onehot).astype(BF16)
        denom = jnp.where(last[:, 0:1], total, 1.0)
        kb[g * rows : (g + 1) * rows, :] = (dot(mat, k_ref[g]) / denom).astype(BF16)
        vb[g * rows : (g + 1) * rows, :] = (dot(mat, v_ref[g]) / denom).astype(BF16)
    n = slots * rows
    ent = 2 * slots
    ent_row = iota((ent, reqs), 0)
    req_lane = iota((ent, reqs), 1)
    sel = jnp.where((ent_row == slots) & (req_lane == my), 1.0, 0.0)
    in_use = iota(table_ref.shape, 0) < count_ref[...]
    table = jnp.where(in_use, table_ref[...], -1)
    for g in range(slots):
        hit = jnp.where(table == my * slots + g, 1.0, 0.0)
        sel = jnp.where(ent_row == g, jnp.max(hit, axis=0, keepdims=True), sel)
    sel_b = sel.astype(BF16)
    same = lax.dot_general(sel_b, sel_b, NT, preferred_element_type=F32)
    q_lane = iota((ent, width), 1) // HD
    pieces = []
    for k in range(topk):
        group_query = dot(sel_b, q_rows[:, k, :].astype(BF16))
        for h in range(heads):
            pieces.append(jnp.where(q_lane == h, group_query, 0.0))
    queries = jnp.concatenate(pieces, axis=0)
    kh = topk * heads
    scale = 1.0 / math.sqrt(HD)
    scores = lax.dot_general(queries.astype(BF16), kb[...], NT, preferred_element_type=F32) * scale
    col = iota((kh * ent, n), 1)
    scores = scores + jnp.where(col % rows == rows - 1, math.log(page_len - rows + 1), 0.0)
    of_page = jnp.where(iota((ent, n), 1) // rows == iota((ent, n), 0), 1.0, 0.0).astype(BF16)
    shared = dot(same.astype(BF16), of_page)
    mask = jnp.concatenate([shared] * kh, axis=0) > 0.5
    scores = jnp.where(mask, scores, NEGATIVE)
    is_own = iota((kh * ent, 1), 0) % ent == slots
    own = jnp.sum(queries * nk_ref[...].astype(F32), axis=1, keepdims=True) * scale
    own = jnp.where(is_own, own, NEGATIVE)
    peak = jnp.maximum(jnp.max(scores, axis=1, keepdims=True), own)
    shift = peak.astype(BF16).astype(F32)
    probs = jnp.where(mask, jnp.exp(scores - shift), 0.0)
    own_prob = jnp.where(is_own, jnp.exp(own - shift), 0.0)
    den = jnp.sum(probs, axis=1, keepdims=True) + own_prob
    num = dot(probs.astype(BF16), vb[...])
    num = num + own_prob.astype(BF16).astype(F32) * nv_ref[...].astype(F32)
    high = den.astype(BF16).astype(F32)
    low = den - high
    er = iota((ent, ent), 0)
    ec = iota((ent, ent), 1)
    before = jnp.sum(jnp.where((ec < er) | (ec == slots), same, 0.0), axis=1, keepdims=True)
    row = ent_row[:, 0:1]
    first = (row == slots) | ((row < slots) & (before < 0.5))
    request = jnp.sum(jnp.where(sel > 0.5, req_lane.astype(F32), 0.0), axis=1, keepdims=True)
    expert = [
        jnp.sum(jnp.where(sel > 0.5, ids_ref[k : k + 1, :].astype(F32), 0.0), axis=1, keepdims=True)
        for k in range(topk)
    ]
    expert_lane = iota((1, EXPERTS), 1).astype(F32)
    logit = [
        jnp.sum(
            jnp.where(expert_lane == expert[k][slots : slots + 1, :], logit_ref[...], 0.0),
            axis=1,
            keepdims=True,
        )
        for k in range(topk)
    ]
    top = logit[0]
    for k in range(1, topk):
        top = jnp.maximum(top, logit[k])
    terms = [jnp.exp(logit[k] - top) for k in range(topk)]
    term_sum = terms[0]
    for k in range(1, topk):
        term_sum = term_sum + terms[k]
    stat_lane = iota((ent, HD), 1)
    by_choice = []
    for k in range(topk):
        gate = jnp.where(row == slots, terms[k] / term_sum, 0.0)
        gate_high = gate.astype(BF16).astype(F32)
        stats = jnp.where(stat_lane == 3 * heads, gate_high, 0.0)
        stats = jnp.where(stat_lane == 3 * heads + 1, gate - gate_high, stats)
        stats = jnp.where(stat_lane == 3 * heads + 2, request, stats)
        lanes = []
        for h in range(heads):
            at = slice((k * heads + h) * ent, (k * heads + h + 1) * ent)
            lanes.append(num[at, h * HD : (h + 1) * HD])
            for i, stat in enumerate((shift, high, low)):
                stats = jnp.where(stat_lane == 3 * h + i, stat[at, :], stats)
        by_choice.append(jnp.concatenate(lanes + [stats], axis=1))
    parts = []
    for e in range(EXPERTS):
        part = jnp.zeros(by_choice[0].shape, F32)
        for k in range(topk):
            part = jnp.where(first & (expert[k] == e), by_choice[k], part)
        parts.append(part)
    entries = jnp.concatenate(parts, axis=0)
    stats = entries[:, width:].astype(BF16)
    devices = out_ref.shape[0]
    lines = out_ref.shape[1] - heads * slots
    columns = devices // EXPERTS
    to = iota((EXPERTS * lines, EXPERTS * ent), 0)
    fro = iota((EXPERTS * lines, EXPERTS * ent), 1)
    flat = (to // lines == fro // ent) & (to % lines == slots + 1)
    flat = jnp.where(flat, 1.0, 0.0).astype(BF16)
    square = iota((HD, HD), 0)
    item = iota((HD, HD), 1) % 6
    mine = iota((EXPERTS * ent, HD), 1) // 6 == iota((EXPERTS * ent, HD), 0) % ent
    for h in range(heads):
        origin = jnp.where(item < 3, 3 * h + item, 3 * heads + item - 3)
        spread = dot(stats, jnp.where(square == origin, 1.0, 0.0).astype(BF16))
        line = dot(flat, jnp.where(mine, spread, 0.0).astype(BF16))
        sent = (entries[:, h * HD : (h + 1) * HD] + line).astype(BF16)
        for e in range(EXPERTS):
            for z in range(columns // heads):
                out_ref[e * columns + z * heads + h, 0:lines, :] = sent[e * lines : (e + 1) * lines, :]
    to = iota((n, n), 0)
    fro = iota((n, n), 1)
    perm = jnp.where((to % slots == fro // rows) & (to // slots == fro % rows), 1.0, 0.0).astype(BF16)
    for base, blocks in ((0, kb), (rows, vb)):
        spread = dot(perm, blocks[...])
        for t in range(heads):
            at = slice(lines + t * slots, lines + (t + 1) * slots)
            out_ref[base : base + rows, at, :] = (
                spread[:, t * HD : (t + 1) * HD].reshape(rows, slots, HD).astype(BF16)
            )


def middle_kernel(head_ref, got_ref, pick_ref, *refs):
    w_refs, (out_ref, scr, terms, stack) = refs[:-4], refs[-4:]
    heads = len(w_refs)
    head = head_ref[0]
    reqs, lines, _ = scr.shape
    slots = lines // 2
    depth = stack.shape[1]
    stack[0] = w_refs[0][0, pl.ds(head * depth, depth), :]
    for d in range(1, heads):
        stack[d] = w_refs[d][...]
    scr[...] = got_ref[:, 0:lines, :].astype(F32)
    stats = scr[:, slots + 1, :]
    stats = jnp.concatenate([stats, stats], axis=0).T
    left = iota((1, 2 * reqs), 1) < reqs
    target = iota((reqs, 2 * reqs), 0).astype(F32)

    def item(g, i):
        first = stats[6 * g + i : 6 * g + i + 1, :]
        if g == slots:
            return jnp.where(left, first, 0.0)
        return jnp.where(left, first, stats[6 * g + 6 + i : 6 * g + 7 + i, :])

    groups = range(0, slots + 1, 2)
    picks = [(item(g, 5) == target) & (item(g, 1) > 0.0) for g in groups]
    gate = jnp.zeros(target.shape, F32)
    peak = jnp.full(target.shape, NEGATIVE, F32)
    for g, pick in zip(groups, picks):
        gate = gate + jnp.where(pick, item(g, 3) + item(g, 4), 0.0)
        peak = jnp.maximum(peak, jnp.where(pick, item(g, 0), NEGATIVE))
    gate = jnp.sum(gate, axis=1, keepdims=True)
    peak = jnp.max(peak, axis=1, keepdims=True)
    den = jnp.zeros(target.shape, F32)
    num = jnp.zeros((2 * reqs, HD), F32)
    for g, pick in zip(groups, picks):
        factor = jnp.where(pick, jnp.exp(item(g, 0) - peak), 0.0)
        den = den + factor * (item(g, 1) + item(g, 2))
        high = factor.astype(BF16)
        low = (factor - high.astype(F32)).astype(BF16)
        entries = jnp.concatenate([scr[:, g, :], scr[:, min(g + 1, slots), :]], axis=0).astype(BF16)
        num = num + dot(jnp.concatenate([high, low], axis=0), entries)
    den = jnp.sum(den, axis=1, keepdims=True)
    some = den > 0.0
    value = (num[:reqs] + num[reqs:]) / jnp.where(some, den, 1.0)
    weighted = jnp.where(some, gate * value, 0.0).astype(BF16)
    tiles = stack.shape[2] // HD
    for b in range(heads):
        part = dot(weighted, stack[b ^ head])
        for t in range(tiles):
            terms[:, b * tiles + t, :] = part[:, t * HD : (t + 1) * HD]
    terms_at = out_ref.shape[1] - heads * tiles
    out_ref[:, terms_at:, :] = terms[...].astype(BF16)
    held = reqs * slots
    local = pick_ref.shape[0] // reqs
    table = jnp.concatenate(
        [
            got_ref[:, lines + t * slots : lines + (t + 1) * slots, :]
            .astype(F32)
            .reshape(held, HD)
            .astype(BF16)
            for t in range(terms_at // local)
        ],
        axis=1,
    )
    step = 16
    for c in range(0, reqs, step):
        rows = dot(pick_ref[c * local : (c + step) * local, :], table)
        for t in range(terms_at // local):
            out_ref[c : c + step, t * local : (t + 1) * local, :] = (
                rows[:, t * HD : (t + 1) * HD].reshape(step, local, HD).astype(BF16)
            )


def route_kernel(new_ref, table_ref, count_ref, out_ref):
    max_new = new_ref.shape[0]
    per_new = table_ref.shape[0] // max_new
    shape = (out_ref.shape[0], new_ref.shape[1])
    slot = iota(shape, 0) // per_new
    quarter = iota(shape, 0) % per_new
    found = jnp.zeros(shape, jnp.int32)
    for i in range(max_new):
        filled = jnp.where(i * per_new < count_ref[...], new_ref[i : i + 1, :], -1)
        page = jnp.zeros(shape, jnp.int32)
        for w in range(per_new):
            page = jnp.where(quarter == w, table_ref[i * per_new + w : i * per_new + w + 1, :] + 1, page)
        found = jnp.where(filled == slot, page, found)
    source = jnp.sum(found, axis=1, keepdims=True) - 1
    out_ref[...] = jnp.where(source == iota(out_ref.shape, 1), 1.0, 0.0).astype(BF16)


def sum_kernel(shard_ref, got_ref, *refs):
    out_refs, (quarters,) = refs[:-1], refs[-1:]
    s = shard_ref[0]
    count = len(out_refs)
    heads = count
    columns = got_ref.shape[0] // EXPERTS
    got = got_ref[...].astype(F32)
    per = got.shape[1] // 2
    for z in range(columns // heads):
        total = jnp.zeros(got.shape[1:], F32)
        for e in range(EXPERTS):
            at = e * columns + z * heads
            total = total + jnp.sum(got[at : at + heads], axis=0)
        for i in range(2):
            quarters[2 * z + i] = total[i * per : (i + 1) * per]
    for t, out_ref in enumerate(out_refs):
        out_ref[...] = quarters[lax.rem(s + t, count)]


def final_kernel(*refs):
    out_ref = refs[-1]
    total = refs[0][...]
    for ref in refs[1:-1]:
        total = total + ref[...]
    mixed = total.astype(BF16)
    for t in range(mixed.shape[0]):
        out_ref[:, t * HD : (t + 1) * HD] = mixed[t : t + 1, :]


def land_kernel(got_ref, k_ref, v_ref):
    total = got_ref.shape[0]
    tiles = k_ref.shape[2] // HD
    rows = total // 2
    n = k_ref.shape[0] * k_ref.shape[1]
    local = n // rows
    to = iota((n, n), 0)
    fro = iota((n, n), 1)
    perm = jnp.where((to // rows == fro % local) & (to % rows == fro // local), 1.0, 0.0).astype(BF16)
    for base, ref in ((0, k_ref), (rows, v_ref)):
        flat = jnp.concatenate(
            [
                got_ref[base : base + rows, t * local : (t + 1) * local, :].reshape(n, HD)
                for t in range(tiles)
            ],
            axis=1,
        )
        ref[...] = dot(perm, flat).reshape(ref.shape).astype(BF16)


def shards(
    old_keys,
    old_values,
    keep_lists,
    drop_weights,
    request_pages,
    page_table,
    new_table,
    queries,
    new_keys,
    new_values,
    expert_ids,
    router_logits,
    out_weight,
):
    devices = lax.axis_size("pages")
    shard_count = lax.axis_size("expert")
    my = lax.axis_index("pages").astype(jnp.int32)
    slots, page_len, width = old_keys.shape
    rows = keep_lists.shape[1] + 1
    per_new = page_len // rows
    requests, max_pages = page_table.shape
    new_cap = 2 * (slots // per_new)
    local = new_cap * per_new
    heads = width // HD
    topk = queries.shape[1]
    lines = 2 * slots
    columns = devices // EXPERTS
    head = lax.rem(my, heads)
    shard = lax.axis_index("expert").astype(jnp.int32).reshape(1)
    table = page_table.T
    counts = request_pages.reshape(1, -1)

    outbox = pl.pallas_call(
        source_kernel,
        out_shape=jax.ShapeDtypeStruct((devices, lines + heads * slots, HD), BF16),
        in_specs=[SMEM] + [VMEM] * 11,
        out_specs=VMEM,
        scratch_shapes=[
            pltpu.VMEM((slots * rows, width), BF16),
            pltpu.VMEM((slots * rows, width), BF16),
            pltpu.VMEM((slots, HD), F32),
            pltpu.VMEM((requests, topk, width), F32),
        ],
        name="source",
    )(
        my.reshape(1),
        table,
        counts,
        expert_ids.T,
        keep_lists,
        drop_weights,
        old_keys,
        old_values,
        queries,
        new_keys,
        new_values,
        router_logits,
    )
    inbox = lax.all_to_all(outbox, "pages", split_axis=0, concat_axis=0, tiled=True)

    weight, _ = lax.optimization_barrier((out_weight[0], outbox))
    weights = [out_weight]
    for d in range(1, heads):
        weights.append(
            lax.ppermute(
                lax.dynamic_slice_in_dim(weight, (head ^ d) * HD, HD, 0),
                "pages",
                [(p, p ^ d) for p in range(devices)],
            )
        )
    pick = pl.pallas_call(
        route_kernel,
        out_shape=jax.ShapeDtypeStruct((devices * local, devices * slots), BF16),
        in_specs=[VMEM] * 3,
        out_specs=VMEM,
        name="route",
    )(new_table.T, table, counts)
    inbox, pick, weights = lax.optimization_barrier((inbox, pick, weights))

    block_cols = out_weight.shape[2]
    terms = heads * block_cols // HD
    routed = pl.pallas_call(
        middle_kernel,
        out_shape=jax.ShapeDtypeStruct((devices, heads * local + terms, HD), BF16),
        in_specs=[SMEM] + [VMEM] * (2 + heads),
        out_specs=VMEM,
        scratch_shapes=[
            pltpu.VMEM((requests, lines, HD), F32),
            pltpu.VMEM((requests, terms, HD), F32),
            pltpu.VMEM((heads, HD, block_cols), BF16),
        ],
        name="middle",
    )(head.reshape(1), inbox, pick, *weights)
    landed = lax.all_to_all(routed, "pages", split_axis=0, concat_axis=0, tiled=True)

    quarter = jax.ShapeDtypeStruct((width // HD, HD), F32)
    quarters = pl.pallas_call(
        sum_kernel,
        grid=(1,),
        out_shape=[quarter] * shard_count,
        in_specs=[
            SMEM,
            pl.BlockSpec((devices, terms, HD), lambda i: (0, heads * local // terms, 0)),
        ],
        out_specs=[VMEM] * shard_count,
        scratch_shapes=[pltpu.VMEM((shard_count, width // HD, HD), F32)],
        name="sum",
    )(shard, landed)
    landed, quarters = lax.optimization_barrier((landed, quarters))
    moved = [quarters[0]]
    for t in range(1, shard_count):
        moved.append(
            lax.ppermute(quarters[t], "expert", [(i, (i + t) % shard_count) for i in range(shard_count)])
        )
    new_page = jax.ShapeDtypeStruct((new_cap, per_new * rows, width), BF16)
    compact_keys, compact_values = pl.pallas_call(
        land_kernel,
        out_shape=(new_page, new_page),
        in_specs=[VMEM],
        out_specs=(VMEM, VMEM),
        name="land",
    )(landed)
    mixed = pl.pallas_call(
        final_kernel,
        out_shape=jax.ShapeDtypeStruct((1, width), BF16),
        in_specs=[VMEM] * shard_count,
        out_specs=VMEM,
        name="final",
    )(*moved)
    return (compact_keys, compact_values, mixed)


def solution(mesh):
    in_specs = (
        P("pages", None, "expert"),
        P("pages", None, "expert"),
        P("pages", None),
        P("pages", None),
        P(),
        P(),
        P(),
        P(None, None, "expert"),
        P("pages", "expert"),
        P("pages", "expert"),
        P(),
        P("pages", None),
        P("pages", "expert", None),
    )
    out_specs = (P("pages", None, "expert"), P("pages", None, "expert"), P("pages", "expert"))
    return jax.shard_map(shards, mesh=mesh, in_specs=in_specs, out_specs=out_specs, check_vma=False)
```

```python
import math

import jax
import jax.numpy as jnp
from jax import lax
from jax.experimental import pallas as pl
from jax.experimental.pallas import tpu as pltpu
from jax.sharding import PartitionSpec as P

HD = 128
EXPERTS = 8
NEGATIVE = -1e30
F32 = jnp.float32
BF16 = jnp.bfloat16
VMEM = pl.BlockSpec(memory_space=pltpu.VMEM)
SMEM = pl.BlockSpec(memory_space=pltpu.SMEM)
ANY = pl.BlockSpec(memory_space=pl.ANY)
PARAMS = pltpu.CompilerParams(vmem_limit_bytes=28 << 20)
NT = (((1,), (1,)), ((), ()))


def iota(shape, dim):
    return lax.broadcasted_iota(jnp.int32, shape, dim)


def dot(a, b):
    return jnp.dot(a, b, preferred_element_type=F32)


def source_kernel(
    my_ref,
    table_ref,
    count_ref,
    ids_ref,
    keep_ref,
    drop_ref,
    k_hbm,
    v_hbm,
    q_ref,
    nk_ref,
    nv_ref,
    logit_ref,
    out_hbm,
    kb,
    vb,
    keep_rows,
    q_rows,
    k_ref,
    v_ref,
    out_ref,
    sems,
    out_sem,
):
    my = my_ref[0]
    slots, page_len, width = k_ref.shape
    loads = []
    for g in range(slots):
        loads.append(
            (
                pltpu.make_async_copy(k_hbm.at[g], k_ref.at[g], sems.at[2 * g]),
                pltpu.make_async_copy(v_hbm.at[g], v_ref.at[g], sems.at[2 * g + 1]),
            )
        )
        for load in loads[g]:
            load.start()
    keep_count = keep_ref.shape[1]
    rows = keep_count + 1
    heads = width // HD
    reqs, topk, _ = q_ref.shape
    keep_rows[...] = jnp.full(keep_rows.shape, -1.0, F32)
    keep_rows[:, 0:keep_count] = keep_ref[...].astype(F32)
    keep_columns = keep_rows[...].T[0:rows, :].astype(jnp.int32)
    q_rows[...] = q_ref[...].astype(F32)
    lane = iota((rows, page_len), 1)
    last = iota((rows, page_len), 0) == rows - 1
    for g in range(slots):
        onehot = jnp.where(keep_columns[:, g : g + 1] == lane, 1.0, 0.0)
        kept = jnp.max(onehot, axis=0, keepdims=True)
        coef = jnp.where(kept > 0.0, 0.0, drop_ref[g : g + 1, :].astype(F32))
        total = jnp.sum(coef, axis=1, keepdims=True)
        mat = jnp.where(last, coef, onehot).astype(BF16)
        denom = jnp.where(last[:, 0:1], total, 1.0)
        for load in loads[g]:
            load.wait()
        kb[g * rows : (g + 1) * rows, :] = (dot(mat, k_ref[g]) / denom).astype(BF16)
        vb[g * rows : (g + 1) * rows, :] = (dot(mat, v_ref[g]) / denom).astype(BF16)
    n = slots * rows
    ent = 2 * slots
    ent_row = iota((ent, reqs), 0)
    req_lane = iota((ent, reqs), 1)
    sel = jnp.where((ent_row == slots) & (req_lane == my), 1.0, 0.0)
    in_use = iota(table_ref.shape, 0) < count_ref[...]
    table = jnp.where(in_use, table_ref[...], -1)
    for g in range(slots):
        hit = jnp.where(table == my * slots + g, 1.0, 0.0)
        sel = jnp.where(ent_row == g, jnp.max(hit, axis=0, keepdims=True), sel)
    sel_b = sel.astype(BF16)
    same = lax.dot_general(sel_b, sel_b, NT, preferred_element_type=F32)
    q_lane = iota((ent, width), 1) // HD
    pieces = []
    for k in range(topk):
        group_query = dot(sel_b, q_rows[:, k, :].astype(BF16))
        for h in range(heads):
            pieces.append(jnp.where(q_lane == h, group_query, 0.0))
    queries = jnp.concatenate(pieces, axis=0)
    kh = topk * heads
    scale = 1.0 / math.sqrt(HD)
    scores = lax.dot_general(queries.astype(BF16), kb[...], NT, preferred_element_type=F32) * scale
    col = iota((kh * ent, n), 1)
    scores = scores + jnp.where(col % rows == rows - 1, math.log(page_len - rows + 1), 0.0)
    of_page = jnp.where(iota((ent, n), 1) // rows == iota((ent, n), 0), 1.0, 0.0).astype(BF16)
    shared = dot(same.astype(BF16), of_page)
    mask = jnp.concatenate([shared] * kh, axis=0) > 0.5
    scores = jnp.where(mask, scores, NEGATIVE)
    is_own = iota((kh * ent, 1), 0) % ent == slots
    own = jnp.sum(queries * nk_ref[...].astype(F32), axis=1, keepdims=True) * scale
    own = jnp.where(is_own, own, NEGATIVE)
    peak = jnp.maximum(jnp.max(scores, axis=1, keepdims=True), own)
    shift = peak.astype(BF16).astype(F32)
    probs = jnp.where(mask, jnp.exp(scores - shift), 0.0)
    own_prob = jnp.where(is_own, jnp.exp(own - shift), 0.0)
    den = jnp.sum(probs, axis=1, keepdims=True) + own_prob
    num = dot(probs.astype(BF16), vb[...])
    num = num + own_prob.astype(BF16).astype(F32) * nv_ref[...].astype(F32)
    high = den.astype(BF16).astype(F32)
    low = den - high
    er = iota((ent, ent), 0)
    ec = iota((ent, ent), 1)
    before = jnp.sum(jnp.where((ec < er) | (ec == slots), same, 0.0), axis=1, keepdims=True)
    row = ent_row[:, 0:1]
    first = (row == slots) | ((row < slots) & (before < 0.5))
    request = jnp.sum(jnp.where(sel > 0.5, req_lane.astype(F32), 0.0), axis=1, keepdims=True)
    expert = [
        jnp.sum(jnp.where(sel > 0.5, ids_ref[k : k + 1, :].astype(F32), 0.0), axis=1, keepdims=True)
        for k in range(topk)
    ]
    expert_lane = iota((1, EXPERTS), 1).astype(F32)
    logit = [
        jnp.sum(
            jnp.where(expert_lane == expert[k][slots : slots + 1, :], logit_ref[...], 0.0),
            axis=1,
            keepdims=True,
        )
        for k in range(topk)
    ]
    top = logit[0]
    for k in range(1, topk):
        top = jnp.maximum(top, logit[k])
    terms = [jnp.exp(logit[k] - top) for k in range(topk)]
    term_sum = terms[0]
    for k in range(1, topk):
        term_sum = term_sum + terms[k]
    stat_lane = iota((ent, HD), 1)
    by_choice = []
    for k in range(topk):
        gate = jnp.where(row == slots, terms[k] / term_sum, 0.0)
        gate_high = gate.astype(BF16).astype(F32)
        stats = jnp.where(stat_lane == 3 * heads, gate_high, 0.0)
        stats = jnp.where(stat_lane == 3 * heads + 1, gate - gate_high, stats)
        stats = jnp.where(stat_lane == 3 * heads + 2, request, stats)
        lanes = []
        for h in range(heads):
            at = slice((k * heads + h) * ent, (k * heads + h + 1) * ent)
            lanes.append(num[at, h * HD : (h + 1) * HD])
            for i, stat in enumerate((shift, high, low)):
                stats = jnp.where(stat_lane == 3 * h + i, stat[at, :], stats)
        by_choice.append(jnp.concatenate(lanes + [stats], axis=1))
    parts = []
    for e in range(EXPERTS):
        part = jnp.zeros(by_choice[0].shape, F32)
        for k in range(topk):
            part = jnp.where(first & (expert[k] == e), by_choice[k], part)
        parts.append(part)
    entries = jnp.concatenate(parts, axis=0)
    stats = entries[:, width:].astype(BF16)
    devices = out_ref.shape[0]
    lines = out_ref.shape[1] - heads * slots
    columns = devices // EXPERTS
    to = iota((EXPERTS * lines, EXPERTS * ent), 0)
    fro = iota((EXPERTS * lines, EXPERTS * ent), 1)
    flat = (to // lines == fro // ent) & (to % lines == slots + 1)
    flat = jnp.where(flat, 1.0, 0.0).astype(BF16)
    square = iota((HD, HD), 0)
    item = iota((HD, HD), 1) % 6
    mine = iota((EXPERTS * ent, HD), 1) // 6 == iota((EXPERTS * ent, HD), 0) % ent
    for h in range(heads):
        origin = jnp.where(item < 3, 3 * h + item, 3 * heads + item - 3)
        spread = dot(stats, jnp.where(square == origin, 1.0, 0.0).astype(BF16))
        line = dot(flat, jnp.where(mine, spread, 0.0).astype(BF16))
        sent = (entries[:, h * HD : (h + 1) * HD] + line).astype(BF16)
        for e in range(EXPERTS):
            for z in range(columns // heads):
                out_ref[e * columns + z * heads + h, 0:lines, :] = sent[e * lines : (e + 1) * lines, :]
    to = iota((n, n), 0)
    fro = iota((n, n), 1)
    perm = jnp.where((to % slots == fro // rows) & (to // slots == fro % rows), 1.0, 0.0).astype(BF16)
    for base, blocks in ((0, kb), (rows, vb)):
        spread = dot(perm, blocks[...])
        for t in range(heads):
            at = slice(lines + t * slots, lines + (t + 1) * slots)
            out_ref[base : base + rows, at, :] = (
                spread[:, t * HD : (t + 1) * HD].reshape(rows, slots, HD).astype(BF16)
            )
    store = pltpu.make_async_copy(out_ref, out_hbm, out_sem)
    store.start()
    store.wait()


def middle_kernel(head_ref, got_hbm, pick_hbm, *refs):
    w_refs, (out_hbm, scr, terms, stack, parts, got_ref, pick_ref, out_ref, sems, out_sems) = (
        refs[:-10],
        refs[-10:],
    )
    heads = len(w_refs)
    head = head_ref[0]
    reqs, lines, _ = scr.shape
    slots = lines // 2
    depth = stack.shape[1]
    loads = [pltpu.make_async_copy(got_hbm.at[:, 0:lines, :], parts, sems.at[0])]
    loads.append(
        pltpu.make_async_copy(w_refs[0].at[0, pl.ds(head * depth, depth), :], stack.at[0], sems.at[1])
    )
    for d in range(1, heads):
        loads.append(pltpu.make_async_copy(w_refs[d], stack.at[d], sems.at[1 + d]))
    loads.append(pltpu.make_async_copy(got_hbm.at[:, lines:, :], got_ref, sems.at[heads + 1]))
    loads.append(pltpu.make_async_copy(pick_hbm, pick_ref, sems.at[heads + 2]))
    for load in loads:
        load.start()
    loads[0].wait()
    scr[...] = parts[...].astype(F32)
    stats = scr[:, slots + 1, :]
    stats = jnp.concatenate([stats, stats], axis=0).T
    left = iota((1, 2 * reqs), 1) < reqs
    target = iota((reqs, 2 * reqs), 0).astype(F32)

    def item(g, i):
        first = stats[6 * g + i : 6 * g + i + 1, :]
        if g == slots:
            return jnp.where(left, first, 0.0)
        return jnp.where(left, first, stats[6 * g + 6 + i : 6 * g + 7 + i, :])

    groups = range(0, slots + 1, 2)
    picks = [(item(g, 5) == target) & (item(g, 1) > 0.0) for g in groups]
    gate = jnp.zeros(target.shape, F32)
    peak = jnp.full(target.shape, NEGATIVE, F32)
    for g, pick in zip(groups, picks):
        gate = gate + jnp.where(pick, item(g, 3) + item(g, 4), 0.0)
        peak = jnp.maximum(peak, jnp.where(pick, item(g, 0), NEGATIVE))
    gate = jnp.sum(gate, axis=1, keepdims=True)
    peak = jnp.max(peak, axis=1, keepdims=True)
    den = jnp.zeros(target.shape, F32)
    num = jnp.zeros((2 * reqs, HD), F32)
    for g, pick in zip(groups, picks):
        factor = jnp.where(pick, jnp.exp(item(g, 0) - peak), 0.0)
        den = den + factor * (item(g, 1) + item(g, 2))
        high = factor.astype(BF16)
        low = (factor - high.astype(F32)).astype(BF16)
        entries = jnp.concatenate([scr[:, g, :], scr[:, min(g + 1, slots), :]], axis=0).astype(BF16)
        num = num + dot(jnp.concatenate([high, low], axis=0), entries)
    den = jnp.sum(den, axis=1, keepdims=True)
    some = den > 0.0
    value = (num[:reqs] + num[reqs:]) / jnp.where(some, den, 1.0)
    weighted = jnp.where(some, gate * value, 0.0).astype(BF16)
    tiles = stack.shape[2] // HD
    for load in loads[1 : 1 + heads]:
        load.wait()
    for b in range(heads):
        part = dot(weighted, stack[b ^ head])
        for t in range(tiles):
            terms[:, b * tiles + t, :] = part[:, t * HD : (t + 1) * HD]
    terms_at = out_ref.shape[1] - heads * tiles
    out_ref[:, terms_at:, :] = terms[...].astype(BF16)
    held = reqs * slots
    local = pick_ref.shape[0] // reqs
    for load in loads[1 + heads :]:
        load.wait()
    table = jnp.concatenate(
        [
            got_ref[:, t * slots : (t + 1) * slots, :]
            .astype(F32)
            .reshape(held, HD)
            .astype(BF16)
            for t in range(terms_at // local)
        ],
        axis=1,
    )
    step = 16
    stores = []
    for c in range(0, reqs, step):
        rows = dot(pick_ref[c * local : (c + step) * local, :], table)
        for t in range(terms_at // local):
            out_ref[c : c + step, t * local : (t + 1) * local, :] = (
                rows[:, t * HD : (t + 1) * HD].reshape(step, local, HD).astype(BF16)
            )
        at = pl.ds(c, step)
        stores.append(pltpu.make_async_copy(out_ref.at[at], out_hbm.at[at], out_sems.at[c // step]))
        stores[-1].start()
    for store in stores:
        store.wait()


def route_kernel(new_ref, table_ref, count_ref, out_ref):
    max_new = new_ref.shape[0]
    per_new = table_ref.shape[0] // max_new
    shape = (out_ref.shape[0], new_ref.shape[1])
    slot = iota(shape, 0) // per_new
    quarter = iota(shape, 0) % per_new
    found = jnp.zeros(shape, jnp.int32)
    for i in range(max_new):
        filled = jnp.where(i * per_new < count_ref[...], new_ref[i : i + 1, :], -1)
        page = jnp.zeros(shape, jnp.int32)
        for w in range(per_new):
            page = jnp.where(quarter == w, table_ref[i * per_new + w : i * per_new + w + 1, :] + 1, page)
        found = jnp.where(filled == slot, page, found)
    source = jnp.sum(found, axis=1, keepdims=True) - 1
    out_ref[...] = jnp.where(source == iota(out_ref.shape, 1), 1.0, 0.0).astype(BF16)


def sum_kernel(shard_ref, got_hbm, *refs):
    out_refs, (quarters, got_ref, sem) = refs[:-3], refs[-3:]
    terms = got_ref.shape[1]
    load = pltpu.make_async_copy(got_hbm.at[:, got_hbm.shape[1] - terms :, :], got_ref, sem)
    load.start()
    load.wait()
    s = shard_ref[0]
    count = len(out_refs)
    heads = count
    columns = got_ref.shape[0] // EXPERTS
    got = got_ref[...].astype(F32)
    per = got.shape[1] // 2
    for z in range(columns // heads):
        total = jnp.zeros(got.shape[1:], F32)
        for e in range(EXPERTS):
            at = e * columns + z * heads
            total = total + jnp.sum(got[at : at + heads], axis=0)
        for i in range(2):
            quarters[2 * z + i] = total[i * per : (i + 1) * per]
    for t, out_ref in enumerate(out_refs):
        quarter = quarters[lax.rem(s + t, count)]
        for i in range(per):
            out_ref[:, i * HD : (i + 1) * HD] = quarter[i : i + 1, :]


def land_kernel(got_hbm, k_hbm, v_hbm, got_ref, k_ref, v_ref, sems, out_sems):
    total = got_ref.shape[0]
    tiles = k_ref.shape[2] // HD
    rows = total // 2
    loads = []
    for i in range(2):
        at = pl.ds(i * rows, rows)
        loads.append(pltpu.make_async_copy(got_hbm.at[at], got_ref.at[at], sems.at[i]))
        loads[i].start()
    n = k_ref.shape[0] * k_ref.shape[1]
    local = n // rows
    to = iota((n, n), 0)
    fro = iota((n, n), 1)
    perm = jnp.where((to // rows == fro % local) & (to % rows == fro // local), 1.0, 0.0).astype(BF16)
    stores = []
    for i, (ref, hbm) in enumerate(((k_ref, k_hbm), (v_ref, v_hbm))):
        base = i * rows
        loads[i].wait()
        flat = jnp.concatenate(
            [
                got_ref[base : base + rows, t * local : (t + 1) * local, :].reshape(n, HD)
                for t in range(tiles)
            ],
            axis=1,
        )
        ref[...] = dot(perm, flat).reshape(ref.shape).astype(BF16)
        stores.append(pltpu.make_async_copy(ref, hbm, out_sems.at[i]))
        stores[i].start()
    for store in stores:
        store.wait()


def shards(
    old_keys,
    old_values,
    keep_lists,
    drop_weights,
    request_pages,
    page_table,
    new_table,
    queries,
    new_keys,
    new_values,
    expert_ids,
    router_logits,
    out_weight,
):
    devices = lax.axis_size("pages")
    shard_count = lax.axis_size("expert")
    my = lax.axis_index("pages").astype(jnp.int32)
    slots, page_len, width = old_keys.shape
    rows = keep_lists.shape[1] + 1
    per_new = page_len // rows
    requests, max_pages = page_table.shape
    new_cap = 2 * (slots // per_new)
    local = new_cap * per_new
    heads = width // HD
    topk = queries.shape[1]
    lines = 2 * slots
    columns = devices // EXPERTS
    head = lax.rem(my, heads)
    shard = lax.axis_index("expert").astype(jnp.int32).reshape(1)
    table = page_table.T
    counts = request_pages.reshape(1, -1)

    outbox = pl.pallas_call(
        source_kernel,
        out_shape=jax.ShapeDtypeStruct((devices, lines + heads * slots, HD), BF16),
        in_specs=[SMEM] + [VMEM] * 5 + [ANY] * 2 + [VMEM] * 4,
        out_specs=ANY,
        scratch_shapes=[
            pltpu.VMEM((slots * rows, width), BF16),
            pltpu.VMEM((slots * rows, width), BF16),
            pltpu.VMEM((slots, HD), F32),
            pltpu.VMEM((requests, topk, width), F32),
            pltpu.VMEM((slots, page_len, width), BF16),
            pltpu.VMEM((slots, page_len, width), BF16),
            pltpu.VMEM((devices, lines + heads * slots, HD), BF16),
            pltpu.SemaphoreType.DMA((2 * slots,)),
            pltpu.SemaphoreType.DMA(()),
        ],
        name="source",
    )(
        my.reshape(1),
        table,
        counts,
        expert_ids.T,
        keep_lists,
        drop_weights,
        old_keys,
        old_values,
        queries,
        new_keys,
        new_values,
        router_logits,
    )
    inbox = lax.all_to_all(outbox, "pages", split_axis=0, concat_axis=0, tiled=True)

    weight = out_weight[0]
    weights = [out_weight]
    for d in range(1, heads):
        weights.append(
            lax.ppermute(
                lax.dynamic_slice_in_dim(weight, (head ^ d) * HD, HD, 0),
                "pages",
                [(p, p ^ d) for p in range(devices)],
            )
        )
    pick = pl.pallas_call(
        route_kernel,
        out_shape=jax.ShapeDtypeStruct((devices * local, devices * slots), BF16),
        in_specs=[VMEM] * 3,
        out_specs=VMEM,
        compiler_params=PARAMS,
        name="route",
    )(new_table.T, table, counts)
    inbox, pick, weights = lax.optimization_barrier((inbox, pick, weights))

    block_cols = out_weight.shape[2]
    terms = heads * block_cols // HD
    routed = pl.pallas_call(
        middle_kernel,
        out_shape=jax.ShapeDtypeStruct((devices, heads * local + terms, HD), BF16),
        in_specs=[SMEM] + [ANY] * (2 + heads),
        out_specs=ANY,
        scratch_shapes=[
            pltpu.VMEM((requests, lines, HD), F32),
            pltpu.VMEM((requests, terms, HD), F32),
            pltpu.VMEM((heads, HD, block_cols), BF16),
            pltpu.VMEM((devices, lines, HD), BF16),
            pltpu.VMEM((devices, heads * slots, HD), BF16),
            pltpu.VMEM((devices * local, devices * slots), BF16),
            pltpu.VMEM((devices, heads * local + terms, HD), BF16),
            pltpu.SemaphoreType.DMA((heads + 3,)),
            pltpu.SemaphoreType.DMA((devices // 16,)),
        ],
        compiler_params=PARAMS,
        name="middle",
    )(head.reshape(1), inbox, pick, *weights)
    landed = lax.all_to_all(routed, "pages", split_axis=0, concat_axis=0, tiled=True)

    quarters = pl.pallas_call(
        sum_kernel,
        out_shape=[jax.ShapeDtypeStruct((1, width), F32)] * shard_count,
        in_specs=[SMEM, ANY],
        out_specs=[VMEM] * shard_count,
        scratch_shapes=[
            pltpu.VMEM((shard_count, width // HD, HD), F32),
            pltpu.VMEM((devices, terms, HD), BF16),
            pltpu.SemaphoreType.DMA(()),
        ],
        compiler_params=PARAMS,
        name="sum",
    )(shard, landed)
    landed, quarters = lax.optimization_barrier((landed, quarters))
    moved = [quarters[0]]
    for t in range(1, shard_count):
        moved.append(
            lax.ppermute(quarters[t], "expert", [(i, (i + t) % shard_count) for i in range(shard_count)])
        )
    new_page = jax.ShapeDtypeStruct((new_cap, per_new * rows, width), BF16)
    compact_keys, compact_values = pl.pallas_call(
        land_kernel,
        out_shape=(new_page, new_page),
        in_specs=[ANY],
        out_specs=(ANY, ANY),
        scratch_shapes=[
            pltpu.VMEM((devices, heads * local + terms, HD), BF16),
            pltpu.VMEM(new_page.shape, BF16),
            pltpu.VMEM(new_page.shape, BF16),
            pltpu.SemaphoreType.DMA((2,)),
            pltpu.SemaphoreType.DMA((2,)),
        ],
        compiler_params=PARAMS,
        name="land",
    )(landed)
    mixed = sum(moved[1:], moved[0]).astype(BF16)
    return (compact_keys, compact_values, mixed)


def solution(mesh):
    in_specs = (
        P("pages", None, "expert"),
        P("pages", None, "expert"),
        P("pages", None),
        P("pages", None),
        P(),
        P(),
        P(),
        P(None, None, "expert"),
        P("pages", "expert"),
        P("pages", "expert"),
        P(),
        P("pages", None),
        P("pages", "expert", None),
    )
    out_specs = (P("pages", None, "expert"), P("pages", None, "expert"), P("pages", "expert"))
    return jax.shard_map(shards, mesh=mesh, in_specs=in_specs, out_specs=out_specs, check_vma=False)
```

```python
import math

import jax
import jax.numpy as jnp
from jax import lax
from jax.experimental import pallas as pl
from jax.experimental.pallas import tpu as pltpu
from jax.sharding import PartitionSpec as P

HD = 128
EXPERTS = 8
NEGATIVE = -1e30
F32 = jnp.float32
BF16 = jnp.bfloat16
VMEM = pl.BlockSpec(memory_space=pltpu.VMEM)
SMEM = pl.BlockSpec(memory_space=pltpu.SMEM)
ANY = pl.BlockSpec(memory_space=pl.ANY)
PARAMS = pltpu.CompilerParams(vmem_limit_bytes=28 << 20)
NT = (((1,), (1,)), ((), ()))


def iota(shape, dim):
    return lax.broadcasted_iota(jnp.int32, shape, dim)


def dot(a, b):
    return jnp.dot(a, b, preferred_element_type=F32)


def source_kernel(
    my_ref,
    table_ref,
    count_ref,
    ids_ref,
    keep_ref,
    drop_ref,
    k_ref,
    v_ref,
    q_ref,
    nk_ref,
    nv_ref,
    logit_ref,
    out_ref,
    kb,
    vb,
    keep_rows,
    q_rows,
):
    my = my_ref[0]
    slots, page_len, width = k_ref.shape
    keep_count = keep_ref.shape[1]
    rows = keep_count + 1
    heads = width // HD
    reqs, topk, _ = q_ref.shape
    keep_rows[...] = jnp.full(keep_rows.shape, -1.0, F32)
    keep_rows[:, 0:keep_count] = keep_ref[...].astype(F32)
    keep_columns = keep_rows[...].T[0:rows, :].astype(jnp.int32)
    q_rows[...] = q_ref[...].astype(F32)
    lane = iota((rows, page_len), 1)
    last = iota((rows, page_len), 0) == rows - 1
    for g in range(slots):
        onehot = jnp.where(keep_columns[:, g : g + 1] == lane, 1.0, 0.0)
        kept = jnp.max(onehot, axis=0, keepdims=True)
        coef = jnp.where(kept > 0.0, 0.0, drop_ref[g : g + 1, :].astype(F32))
        total = jnp.sum(coef, axis=1, keepdims=True)
        mat = jnp.where(last, coef, onehot).astype(BF16)
        denom = jnp.where(last[:, 0:1], total, 1.0)
        kb[g * rows : (g + 1) * rows, :] = (dot(mat, k_ref[g]) / denom).astype(BF16)
        vb[g * rows : (g + 1) * rows, :] = (dot(mat, v_ref[g]) / denom).astype(BF16)
    n = slots * rows
    ent = 2 * slots
    ent_row = iota((ent, reqs), 0)
    req_lane = iota((ent, reqs), 1)
    sel = jnp.where((ent_row == slots) & (req_lane == my), 1.0, 0.0)
    in_use = iota(table_ref.shape, 0) < count_ref[...]
    table = jnp.where(in_use, table_ref[...], -1)
    for g in range(slots):
        hit = jnp.where(table == my * slots + g, 1.0, 0.0)
        sel = jnp.where(ent_row == g, jnp.max(hit, axis=0, keepdims=True), sel)
    sel_b = sel.astype(BF16)
    same = lax.dot_general(sel_b, sel_b, NT, preferred_element_type=F32)
    q_lane = iota((ent, width), 1) // HD
    pieces = []
    for k in range(topk):
        group_query = dot(sel_b, q_rows[:, k, :].astype(BF16))
        for h in range(heads):
            pieces.append(jnp.where(q_lane == h, group_query, 0.0))
    queries = jnp.concatenate(pieces, axis=0)
    kh = topk * heads
    scale = 1.0 / math.sqrt(HD)
    scores = lax.dot_general(queries.astype(BF16), kb[...], NT, preferred_element_type=F32) * scale
    col = iota((kh * ent, n), 1)
    scores = scores + jnp.where(col % rows == rows - 1, math.log(page_len - rows + 1), 0.0)
    of_page = jnp.where(iota((ent, n), 1) // rows == iota((ent, n), 0), 1.0, 0.0).astype(BF16)
    shared = dot(same.astype(BF16), of_page)
    mask = jnp.concatenate([shared] * kh, axis=0) > 0.5
    scores = jnp.where(mask, scores, NEGATIVE)
    is_own = iota((kh * ent, 1), 0) % ent == slots
    own = jnp.sum(queries * nk_ref[...].astype(F32), axis=1, keepdims=True) * scale
    own = jnp.where(is_own, own, NEGATIVE)
    peak = jnp.maximum(jnp.max(scores, axis=1, keepdims=True), own)
    shift = peak.astype(BF16).astype(F32)
    probs = jnp.where(mask, jnp.exp(scores - shift), 0.0)
    own_prob = jnp.where(is_own, jnp.exp(own - shift), 0.0)
    den = jnp.sum(probs, axis=1, keepdims=True) + own_prob
    num = dot(probs.astype(BF16), vb[...])
    num = num + own_prob.astype(BF16).astype(F32) * nv_ref[...].astype(F32)
    high = den.astype(BF16).astype(F32)
    low = den - high
    er = iota((ent, ent), 0)
    ec = iota((ent, ent), 1)
    before = jnp.sum(jnp.where((ec < er) | (ec == slots), same, 0.0), axis=1, keepdims=True)
    row = ent_row[:, 0:1]
    first = (row == slots) | ((row < slots) & (before < 0.5))
    request = jnp.sum(jnp.where(sel > 0.5, req_lane.astype(F32), 0.0), axis=1, keepdims=True)
    expert = [
        jnp.sum(jnp.where(sel > 0.5, ids_ref[k : k + 1, :].astype(F32), 0.0), axis=1, keepdims=True)
        for k in range(topk)
    ]
    expert_lane = iota((1, EXPERTS), 1).astype(F32)
    logit = [
        jnp.sum(
            jnp.where(expert_lane == expert[k][slots : slots + 1, :], logit_ref[...], 0.0),
            axis=1,
            keepdims=True,
        )
        for k in range(topk)
    ]
    top = logit[0]
    for k in range(1, topk):
        top = jnp.maximum(top, logit[k])
    terms = [jnp.exp(logit[k] - top) for k in range(topk)]
    term_sum = terms[0]
    for k in range(1, topk):
        term_sum = term_sum + terms[k]
    stat_lane = iota((ent, HD), 1)
    by_choice = []
    for k in range(topk):
        gate = jnp.where(row == slots, terms[k] / term_sum, 0.0)
        gate_high = gate.astype(BF16).astype(F32)
        stats = jnp.where(stat_lane == 3 * heads, gate_high, 0.0)
        stats = jnp.where(stat_lane == 3 * heads + 1, gate - gate_high, stats)
        stats = jnp.where(stat_lane == 3 * heads + 2, request, stats)
        lanes = []
        for h in range(heads):
            at = slice((k * heads + h) * ent, (k * heads + h + 1) * ent)
            lanes.append(num[at, h * HD : (h + 1) * HD])
            for i, stat in enumerate((shift, high, low)):
                stats = jnp.where(stat_lane == 3 * h + i, stat[at, :], stats)
        by_choice.append(jnp.concatenate(lanes + [stats], axis=1))
    parts = []
    for e in range(EXPERTS):
        part = jnp.zeros(by_choice[0].shape, F32)
        for k in range(topk):
            part = jnp.where(first & (expert[k] == e), by_choice[k], part)
        parts.append(part)
    entries = jnp.concatenate(parts, axis=0)
    stats = entries[:, width:].astype(BF16)
    devices = out_ref.shape[0]
    lines = out_ref.shape[1] - heads * slots
    columns = devices // EXPERTS
    to = iota((EXPERTS * lines, EXPERTS * ent), 0)
    fro = iota((EXPERTS * lines, EXPERTS * ent), 1)
    flat = (to // lines == fro // ent) & (to % lines == slots + 1)
    flat = jnp.where(flat, 1.0, 0.0).astype(BF16)
    square = iota((HD, HD), 0)
    item = iota((HD, HD), 1) % 6
    mine = iota((EXPERTS * ent, HD), 1) // 6 == iota((EXPERTS * ent, HD), 0) % ent
    for h in range(heads):
        origin = jnp.where(item < 3, 3 * h + item, 3 * heads + item - 3)
        spread = dot(stats, jnp.where(square == origin, 1.0, 0.0).astype(BF16))
        line = dot(flat, jnp.where(mine, spread, 0.0).astype(BF16))
        sent = (entries[:, h * HD : (h + 1) * HD] + line).astype(BF16)
        for e in range(EXPERTS):
            for z in range(columns // heads):
                out_ref[e * columns + z * heads + h, 0:lines, :] = sent[e * lines : (e + 1) * lines, :]
    to = iota((n, n), 0)
    fro = iota((n, n), 1)
    perm = jnp.where((to % slots == fro // rows) & (to // slots == fro % rows), 1.0, 0.0).astype(BF16)
    for base, blocks in ((0, kb), (rows, vb)):
        spread = dot(perm, blocks[...])
        for t in range(heads):
            at = slice(lines + t * slots, lines + (t + 1) * slots)
            out_ref[base : base + rows, at, :] = (
                spread[:, t * HD : (t + 1) * HD].reshape(rows, slots, HD).astype(BF16)
            )


def middle_kernel(head_ref, got_hbm, pick_hbm, *refs):
    w_refs, (out_hbm, scr, terms, stack, parts, got_ref, pick_ref, out_ref, sems, out_sems) = (
        refs[:-10],
        refs[-10:],
    )
    heads = len(w_refs)
    head = head_ref[0]
    reqs, lines, _ = scr.shape
    slots = lines // 2
    depth = stack.shape[1]
    loads = [pltpu.make_async_copy(got_hbm.at[:, 0:lines, :], parts, sems.at[0])]
    loads.append(
        pltpu.make_async_copy(w_refs[0].at[0, pl.ds(head * depth, depth), :], stack.at[0], sems.at[1])
    )
    for d in range(1, heads):
        loads.append(pltpu.make_async_copy(w_refs[d], stack.at[d], sems.at[1 + d]))
    loads.append(pltpu.make_async_copy(got_hbm.at[:, lines:, :], got_ref, sems.at[heads + 1]))
    loads.append(pltpu.make_async_copy(pick_hbm, pick_ref, sems.at[heads + 2]))
    for load in loads:
        load.start()
    loads[0].wait()
    scr[...] = parts[...].astype(F32)
    stats = scr[:, slots + 1, :]
    stats = jnp.concatenate([stats, stats], axis=0).T
    left = iota((1, 2 * reqs), 1) < reqs
    target = iota((reqs, 2 * reqs), 0).astype(F32)

    def item(g, i):
        first = stats[6 * g + i : 6 * g + i + 1, :]
        if g == slots:
            return jnp.where(left, first, 0.0)
        return jnp.where(left, first, stats[6 * g + 6 + i : 6 * g + 7 + i, :])

    groups = range(0, slots + 1, 2)
    picks = [(item(g, 5) == target) & (item(g, 1) > 0.0) for g in groups]
    gate = jnp.zeros(target.shape, F32)
    peak = jnp.full(target.shape, NEGATIVE, F32)
    for g, pick in zip(groups, picks):
        gate = gate + jnp.where(pick, item(g, 3) + item(g, 4), 0.0)
        peak = jnp.maximum(peak, jnp.where(pick, item(g, 0), NEGATIVE))
    gate = jnp.sum(gate, axis=1, keepdims=True)
    peak = jnp.max(peak, axis=1, keepdims=True)
    den = jnp.zeros(target.shape, F32)
    num = jnp.zeros((2 * reqs, HD), F32)
    for g, pick in zip(groups, picks):
        factor = jnp.where(pick, jnp.exp(item(g, 0) - peak), 0.0)
        den = den + factor * (item(g, 1) + item(g, 2))
        high = factor.astype(BF16)
        low = (factor - high.astype(F32)).astype(BF16)
        entries = jnp.concatenate([scr[:, g, :], scr[:, min(g + 1, slots), :]], axis=0).astype(BF16)
        num = num + dot(jnp.concatenate([high, low], axis=0), entries)
    den = jnp.sum(den, axis=1, keepdims=True)
    some = den > 0.0
    value = (num[:reqs] + num[reqs:]) / jnp.where(some, den, 1.0)
    weighted = jnp.where(some, gate * value, 0.0).astype(BF16)
    tiles = stack.shape[2] // HD
    for load in loads[1 : 1 + heads]:
        load.wait()
    for b in range(heads):
        part = dot(weighted, stack[b ^ head])
        for t in range(tiles):
            terms[:, b * tiles + t, :] = part[:, t * HD : (t + 1) * HD]
    terms_at = out_ref.shape[1] - heads * tiles
    out_ref[:, terms_at:, :] = terms[...].astype(BF16)
    held = reqs * slots
    local = pick_ref.shape[0] // reqs
    for load in loads[1 + heads :]:
        load.wait()
    table = jnp.concatenate(
        [
            got_ref[:, t * slots : (t + 1) * slots, :]
            .astype(F32)
            .reshape(held, HD)
            .astype(BF16)
            for t in range(terms_at // local)
        ],
        axis=1,
    )
    step = 16
    stores = []
    for c in range(0, reqs, step):
        rows = dot(pick_ref[c * local : (c + step) * local, :], table)
        for t in range(terms_at // local):
            out_ref[c : c + step, t * local : (t + 1) * local, :] = (
                rows[:, t * HD : (t + 1) * HD].reshape(step, local, HD).astype(BF16)
            )
        at = pl.ds(c, step)
        stores.append(pltpu.make_async_copy(out_ref.at[at], out_hbm.at[at], out_sems.at[c // step]))
        stores[-1].start()
    for store in stores:
        store.wait()


def route_kernel(new_ref, table_ref, count_ref, out_ref):
    max_new = new_ref.shape[0]
    per_new = table_ref.shape[0] // max_new
    shape = (out_ref.shape[0], new_ref.shape[1])
    slot = iota(shape, 0) // per_new
    quarter = iota(shape, 0) % per_new
    found = jnp.zeros(shape, jnp.int32)
    for i in range(max_new):
        filled = jnp.where(i * per_new < count_ref[...], new_ref[i : i + 1, :], -1)
        page = jnp.zeros(shape, jnp.int32)
        for w in range(per_new):
            page = jnp.where(quarter == w, table_ref[i * per_new + w : i * per_new + w + 1, :] + 1, page)
        found = jnp.where(filled == slot, page, found)
    source = jnp.sum(found, axis=1, keepdims=True) - 1
    out_ref[...] = jnp.where(source == iota(out_ref.shape, 1), 1.0, 0.0).astype(BF16)


def sum_kernel(shard_ref, got_hbm, *refs):
    out_refs, (quarters, got_ref, sem) = refs[:-3], refs[-3:]
    terms = got_ref.shape[1]
    load = pltpu.make_async_copy(got_hbm.at[:, got_hbm.shape[1] - terms :, :], got_ref, sem)
    load.start()
    load.wait()
    s = shard_ref[0]
    count = len(out_refs)
    heads = count
    columns = got_ref.shape[0] // EXPERTS
    got = got_ref[...].astype(F32)
    per = got.shape[1] // 2
    for z in range(columns // heads):
        total = jnp.zeros(got.shape[1:], F32)
        for e in range(EXPERTS):
            at = e * columns + z * heads
            total = total + jnp.sum(got[at : at + heads], axis=0)
        for i in range(2):
            quarters[2 * z + i] = total[i * per : (i + 1) * per]
    for t, out_ref in enumerate(out_refs):
        quarter = quarters[lax.rem(s + t, count)]
        for i in range(per):
            out_ref[:, i * HD : (i + 1) * HD] = quarter[i : i + 1, :]


def land_kernel(got_hbm, k_hbm, v_hbm, got_ref, k_ref, v_ref, sems, out_sems):
    total = got_ref.shape[0]
    tiles = k_ref.shape[2] // HD
    rows = total // 2
    loads = []
    for i in range(2):
        at = pl.ds(i * rows, rows)
        loads.append(pltpu.make_async_copy(got_hbm.at[at], got_ref.at[at], sems.at[i]))
        loads[i].start()
    n = k_ref.shape[0] * k_ref.shape[1]
    local = n // rows
    to = iota((n, n), 0)
    fro = iota((n, n), 1)
    perm = jnp.where((to // rows == fro % local) & (to % rows == fro // local), 1.0, 0.0).astype(BF16)
    stores = []
    for i, (ref, hbm) in enumerate(((k_ref, k_hbm), (v_ref, v_hbm))):
        base = i * rows
        loads[i].wait()
        flat = jnp.concatenate(
            [
                got_ref[base : base + rows, t * local : (t + 1) * local, :].reshape(n, HD)
                for t in range(tiles)
            ],
            axis=1,
        )
        ref[...] = dot(perm, flat).reshape(ref.shape).astype(BF16)
        stores.append(pltpu.make_async_copy(ref, hbm, out_sems.at[i]))
        stores[i].start()
    for store in stores:
        store.wait()


def shards(
    old_keys,
    old_values,
    keep_lists,
    drop_weights,
    request_pages,
    page_table,
    new_table,
    queries,
    new_keys,
    new_values,
    expert_ids,
    router_logits,
    out_weight,
):
    devices = lax.axis_size("pages")
    shard_count = lax.axis_size("expert")
    my = lax.axis_index("pages").astype(jnp.int32)
    slots, page_len, width = old_keys.shape
    rows = keep_lists.shape[1] + 1
    per_new = page_len // rows
    requests, max_pages = page_table.shape
    new_cap = 2 * (slots // per_new)
    local = new_cap * per_new
    heads = width // HD
    topk = queries.shape[1]
    lines = 2 * slots
    columns = devices // EXPERTS
    head = lax.rem(my, heads)
    shard = lax.axis_index("expert").astype(jnp.int32).reshape(1)
    table = page_table.T
    counts = request_pages.reshape(1, -1)

    pieces = [
        lax.dynamic_slice_in_dim(out_weight[0], (head ^ d) * HD, HD, 0) for d in range(1, heads)
    ]
    table, pieces = lax.optimization_barrier((table, pieces))
    weights = [
        lax.ppermute(piece, "pages", [(p, p ^ d) for p in range(devices)])
        for d, piece in enumerate(pieces, 1)
    ]
    outbox = pl.pallas_call(
        source_kernel,
        out_shape=jax.ShapeDtypeStruct((devices, lines + heads * slots, HD), BF16),
        in_specs=[SMEM] + [VMEM] * 11,
        out_specs=VMEM,
        scratch_shapes=[
            pltpu.VMEM((slots * rows, width), BF16),
            pltpu.VMEM((slots * rows, width), BF16),
            pltpu.VMEM((slots, HD), F32),
            pltpu.VMEM((requests, topk, width), F32),
        ],
        name="source",
    )(
        my.reshape(1),
        table,
        counts,
        expert_ids.T,
        keep_lists,
        drop_weights,
        old_keys,
        old_values,
        queries,
        new_keys,
        new_values,
        router_logits,
    )
    outbox, weights = lax.optimization_barrier((outbox, weights))
    inbox = lax.all_to_all(outbox, "pages", split_axis=0, concat_axis=0, tiled=True)

    pick = pl.pallas_call(
        route_kernel,
        out_shape=jax.ShapeDtypeStruct((devices * local, devices * slots), BF16),
        in_specs=[VMEM] * 3,
        out_specs=VMEM,
        compiler_params=PARAMS,
        name="route",
    )(new_table.T, table, counts)
    inbox, pick = lax.optimization_barrier((inbox, pick))

    block_cols = out_weight.shape[2]
    terms = heads * block_cols // HD
    routed = pl.pallas_call(
        middle_kernel,
        out_shape=jax.ShapeDtypeStruct((devices, heads * local + terms, HD), BF16),
        in_specs=[SMEM] + [ANY] * (2 + heads),
        out_specs=ANY,
        scratch_shapes=[
            pltpu.VMEM((requests, lines, HD), F32),
            pltpu.VMEM((requests, terms, HD), F32),
            pltpu.VMEM((heads, HD, block_cols), BF16),
            pltpu.VMEM((devices, lines, HD), BF16),
            pltpu.VMEM((devices, heads * slots, HD), BF16),
            pltpu.VMEM((devices * local, devices * slots), BF16),
            pltpu.VMEM((devices, heads * local + terms, HD), BF16),
            pltpu.SemaphoreType.DMA((heads + 3,)),
            pltpu.SemaphoreType.DMA((devices // 16,)),
        ],
        compiler_params=PARAMS,
        name="middle",
    )(head.reshape(1), inbox, pick, out_weight, *weights)
    landed = lax.all_to_all(routed, "pages", split_axis=0, concat_axis=0, tiled=True)

    quarters = pl.pallas_call(
        sum_kernel,
        out_shape=[jax.ShapeDtypeStruct((1, width), F32)] * shard_count,
        in_specs=[SMEM, ANY],
        out_specs=[VMEM] * shard_count,
        scratch_shapes=[
            pltpu.VMEM((shard_count, width // HD, HD), F32),
            pltpu.VMEM((devices, terms, HD), BF16),
            pltpu.SemaphoreType.DMA(()),
        ],
        compiler_params=PARAMS,
        name="sum",
    )(shard, landed)
    landed, quarters = lax.optimization_barrier((landed, quarters))
    moved = [quarters[0]]
    for t in range(1, shard_count):
        moved.append(
            lax.ppermute(quarters[t], "expert", [(i, (i + t) % shard_count) for i in range(shard_count)])
        )
    new_page = jax.ShapeDtypeStruct((new_cap, per_new * rows, width), BF16)
    compact_keys, compact_values = pl.pallas_call(
        land_kernel,
        out_shape=(new_page, new_page),
        in_specs=[ANY],
        out_specs=(ANY, ANY),
        scratch_shapes=[
            pltpu.VMEM((devices, heads * local + terms, HD), BF16),
            pltpu.VMEM(new_page.shape, BF16),
            pltpu.VMEM(new_page.shape, BF16),
            pltpu.SemaphoreType.DMA((2,)),
            pltpu.SemaphoreType.DMA((2,)),
        ],
        compiler_params=PARAMS,
        name="land",
    )(landed)
    mixed = sum(moved[1:], moved[0]).astype(BF16)
    return (compact_keys, compact_values, mixed)


def solution(mesh):
    in_specs = (
        P("pages", None, "expert"),
        P("pages", None, "expert"),
        P("pages", None),
        P("pages", None),
        P(),
        P(),
        P(),
        P(None, None, "expert"),
        P("pages", "expert"),
        P("pages", "expert"),
        P(),
        P("pages", None),
        P("pages", "expert", None),
    )
    out_specs = (P("pages", None, "expert"), P("pages", None, "expert"), P("pages", "expert"))
    return jax.shard_map(shards, mesh=mesh, in_specs=in_specs, out_specs=out_specs, check_vma=False)
```

```python
import math

import jax
import jax.numpy as jnp
from jax import lax
from jax.experimental import pallas as pl
from jax.experimental.pallas import tpu as pltpu
from jax.sharding import PartitionSpec as P

HD = 128
EXPERTS = 8
NEGATIVE = -1e30
F32 = jnp.float32
BF16 = jnp.bfloat16
VMEM = pl.BlockSpec(memory_space=pltpu.VMEM)
SMEM = pl.BlockSpec(memory_space=pltpu.SMEM)
ANY = pl.BlockSpec(memory_space=pl.ANY)
PARAMS = pltpu.CompilerParams(vmem_limit_bytes=28 << 20)
NT = (((1,), (1,)), ((), ()))


def iota(shape, dim):
    return lax.broadcasted_iota(jnp.int32, shape, dim)


def over(x, n):
    return lax.shift_right_logical(x, n.bit_length() - 1) if n & (n - 1) == 0 else x // n


def rest(x, n):
    return x & (n - 1) if n & (n - 1) == 0 else x % n


def dot(a, b):
    return jnp.dot(a, b, preferred_element_type=F32)


def source_kernel(
    my_ref,
    table_ref,
    count_ref,
    ids_ref,
    keep_ref,
    drop_ref,
    k_ref,
    v_ref,
    q_ref,
    nk_ref,
    nv_ref,
    logit_ref,
    out_ref,
    kb,
    vb,
    keep_rows,
    q_rows,
):
    my = my_ref[0]
    slots, page_len, width = k_ref.shape
    keep_count = keep_ref.shape[1]
    rows = keep_count + 1
    heads = width // HD
    reqs, topk, _ = q_ref.shape
    keep_rows[...] = jnp.full(keep_rows.shape, -1.0, F32)
    keep_rows[:, 0:keep_count] = keep_ref[...].astype(F32)
    keep_columns = keep_rows[...].T[0:rows, :].astype(jnp.int32)
    q_rows[...] = q_ref[...].astype(F32)
    lane = iota((rows, page_len), 1)
    last = iota((rows, page_len), 0) == rows - 1
    for g in range(slots):
        onehot = jnp.where(keep_columns[:, g : g + 1] == lane, 1.0, 0.0)
        kept = jnp.max(onehot, axis=0, keepdims=True)
        coef = jnp.where(kept > 0.0, 0.0, drop_ref[g : g + 1, :].astype(F32))
        total = jnp.sum(coef, axis=1, keepdims=True)
        mat = jnp.where(last, coef, onehot).astype(BF16)
        denom = jnp.where(last[rows - 8 :, 0:1], total, 1.0)
        for ref, blocks in ((k_ref, kb), (v_ref, vb)):
            block = dot(mat, ref[g])
            block = jnp.concatenate([block[: rows - 8], block[rows - 8 :] / denom], axis=0)
            blocks[g * rows : (g + 1) * rows, :] = block.astype(BF16)
    n = slots * rows
    ent = 2 * slots
    ent_row = iota((ent, reqs), 0)
    req_lane = iota((ent, reqs), 1)
    sel = jnp.where((ent_row == slots) & (req_lane == my), 1.0, 0.0)
    in_use = iota(table_ref.shape, 0) < count_ref[...]
    table = jnp.where(in_use, table_ref[...], -1)
    for g in range(slots):
        hit = jnp.where(table == my * slots + g, 1.0, 0.0)
        sel = jnp.where(ent_row == g, jnp.max(hit, axis=0, keepdims=True), sel)
    sel_b = sel.astype(BF16)
    same = lax.dot_general(sel_b, sel_b, NT, preferred_element_type=F32)
    q_lane = over(iota((ent, width), 1), HD)
    pieces = []
    for k in range(topk):
        group_query = dot(sel_b, q_rows[:, k, :].astype(BF16))
        for h in range(heads):
            pieces.append(jnp.where(q_lane == h, group_query, 0.0))
    queries = jnp.concatenate(pieces, axis=0)
    kh = topk * heads
    scale = 1.0 / math.sqrt(HD)
    scores = lax.dot_general(queries.astype(BF16), kb[...], NT, preferred_element_type=F32) * scale
    col = iota((kh * ent, n), 1)
    scores = scores + jnp.where(rest(col, rows) == rows - 1, math.log(page_len - rows + 1), 0.0)
    of_page = jnp.where(over(iota((ent, n), 1), rows) == iota((ent, n), 0), 1.0, 0.0).astype(BF16)
    shared = dot(same.astype(BF16), of_page)
    mask = jnp.concatenate([shared] * kh, axis=0) > 0.5
    scores = jnp.where(mask, scores, NEGATIVE)
    is_own = rest(iota((kh * ent, 1), 0), ent) == slots
    own = jnp.sum(queries * nk_ref[...].astype(F32), axis=1, keepdims=True) * scale
    own = jnp.where(is_own, own, NEGATIVE)
    peak = jnp.maximum(jnp.max(scores, axis=1, keepdims=True), own)
    shift = peak.astype(BF16).astype(F32)
    probs = jnp.where(mask, jnp.exp(scores - shift), 0.0)
    own_prob = jnp.where(is_own, jnp.exp(own - shift), 0.0)
    den = jnp.sum(probs, axis=1, keepdims=True) + own_prob
    num = dot(probs.astype(BF16), vb[...])
    num = num + own_prob.astype(BF16).astype(F32) * nv_ref[...].astype(F32)
    high = den.astype(BF16).astype(F32)
    low = den - high
    er = iota((ent, ent), 0)
    ec = iota((ent, ent), 1)
    before = jnp.sum(jnp.where((ec < er) | (ec == slots), same, 0.0), axis=1, keepdims=True)
    row = ent_row[:, 0:1]
    first = (row == slots) | ((row < slots) & (before < 0.5))
    request = jnp.sum(jnp.where(sel > 0.5, req_lane.astype(F32), 0.0), axis=1, keepdims=True)
    expert = [
        jnp.sum(jnp.where(sel > 0.5, ids_ref[k : k + 1, :].astype(F32), 0.0), axis=1, keepdims=True)
        for k in range(topk)
    ]
    expert_lane = iota((1, EXPERTS), 1).astype(F32)
    logit = [
        jnp.sum(
            jnp.where(expert_lane == expert[k][slots : slots + 1, :], logit_ref[...], 0.0),
            axis=1,
            keepdims=True,
        )
        for k in range(topk)
    ]
    top = logit[0]
    for k in range(1, topk):
        top = jnp.maximum(top, logit[k])
    terms = [jnp.exp(logit[k] - top) for k in range(topk)]
    term_sum = terms[0]
    for k in range(1, topk):
        term_sum = term_sum + terms[k]
    stat_lane = iota((ent, HD), 1)
    by_choice = []
    for k in range(topk):
        gate = jnp.where(row == slots, terms[k] / term_sum, 0.0)
        gate_high = gate.astype(BF16).astype(F32)
        stats = jnp.where(stat_lane == 3 * heads, gate_high, 0.0)
        stats = jnp.where(stat_lane == 3 * heads + 1, gate - gate_high, stats)
        stats = jnp.where(stat_lane == 3 * heads + 2, request, stats)
        lanes = []
        for h in range(heads):
            at = slice((k * heads + h) * ent, (k * heads + h + 1) * ent)
            lanes.append(num[at, h * HD : (h + 1) * HD])
            for i, stat in enumerate((shift, high, low)):
                stats = jnp.where(stat_lane == 3 * h + i, stat[at, :], stats)
        by_choice.append(jnp.concatenate(lanes + [stats], axis=1))
    parts = []
    for e in range(EXPERTS):
        part = jnp.zeros(by_choice[0].shape, F32)
        for k in range(topk):
            part = jnp.where(first & (expert[k] == e), by_choice[k], part)
        parts.append(part)
    entries = jnp.concatenate(parts, axis=0)
    stats = entries[:, width:].astype(BF16)
    devices = out_ref.shape[0]
    lines = out_ref.shape[1] - heads * slots
    columns = devices // EXPERTS
    to = iota((EXPERTS * lines, EXPERTS * ent), 0)
    fro = iota((EXPERTS * lines, EXPERTS * ent), 1)
    flat = (over(to, lines) == over(fro, ent)) & (rest(to, lines) == slots + 1)
    flat = jnp.where(flat, 1.0, 0.0).astype(BF16)
    square = iota((HD, HD), 0)
    item = iota((HD, HD), 1) % 6
    mine = iota((EXPERTS * ent, HD), 1) // 6 == rest(iota((EXPERTS * ent, HD), 0), ent)
    for h in range(heads):
        origin = jnp.where(item < 3, 3 * h + item, 3 * heads + item - 3)
        spread = dot(stats, jnp.where(square == origin, 1.0, 0.0).astype(BF16))
        line = dot(flat, jnp.where(mine, spread, 0.0).astype(BF16))
        sent = (entries[:, h * HD : (h + 1) * HD] + line).astype(BF16)
        for e in range(EXPERTS):
            for z in range(columns // heads):
                out_ref[e * columns + z * heads + h, 0:lines, :] = sent[e * lines : (e + 1) * lines, :]
    to = iota((n, n), 0)
    fro = iota((n, n), 1)
    perm = jnp.where((rest(to, slots) == over(fro, rows)) & (over(to, slots) == rest(fro, rows)), 1.0, 0.0).astype(BF16)
    for base, blocks in ((0, kb), (rows, vb)):
        spread = dot(perm, blocks[...])
        for t in range(heads):
            at = slice(lines + t * slots, lines + (t + 1) * slots)
            out_ref[base : base + rows, at, :] = (
                spread[:, t * HD : (t + 1) * HD].reshape(rows, slots, HD).astype(BF16)
            )


def middle_kernel(head_ref, got_hbm, pick_hbm, *refs):
    w_refs, (out_hbm, scr, terms, stack, parts, got_ref, pick_ref, out_ref, sems, out_sems) = (
        refs[:-10],
        refs[-10:],
    )
    heads = len(w_refs)
    head = head_ref[0]
    reqs, lines, _ = scr.shape
    slots = lines // 2
    depth = stack.shape[1]
    loads = [pltpu.make_async_copy(got_hbm.at[:, 0:lines, :], parts, sems.at[0])]
    loads.append(
        pltpu.make_async_copy(w_refs[0].at[0, pl.ds(head * depth, depth), :], stack.at[0], sems.at[1])
    )
    for d in range(1, heads):
        loads.append(pltpu.make_async_copy(w_refs[d], stack.at[d], sems.at[1 + d]))
    loads.append(pltpu.make_async_copy(got_hbm.at[:, lines:, :], got_ref, sems.at[heads + 1]))
    loads.append(pltpu.make_async_copy(pick_hbm, pick_ref, sems.at[heads + 2]))
    for load in loads:
        load.start()
    loads[0].wait()
    scr[...] = parts[...].astype(F32)
    stats = scr[:, slots + 1, :]
    stats = jnp.concatenate([stats, stats], axis=0).T
    left = iota((1, 2 * reqs), 1) < reqs
    target = iota((reqs, 2 * reqs), 0).astype(F32)

    def item(g, i):
        first = stats[6 * g + i : 6 * g + i + 1, :]
        if g == slots:
            return jnp.where(left, first, 0.0)
        return jnp.where(left, first, stats[6 * g + 6 + i : 6 * g + 7 + i, :])

    groups = range(0, slots + 1, 2)
    picks = [(item(g, 5) == target) & (item(g, 1) > 0.0) for g in groups]
    gate = jnp.zeros(target.shape, F32)
    peak = jnp.full(target.shape, NEGATIVE, F32)
    for g, pick in zip(groups, picks):
        gate = gate + jnp.where(pick, item(g, 3) + item(g, 4), 0.0)
        peak = jnp.maximum(peak, jnp.where(pick, item(g, 0), NEGATIVE))
    gate = jnp.sum(gate, axis=1, keepdims=True)
    peak = jnp.max(peak, axis=1, keepdims=True)
    den = jnp.zeros(target.shape, F32)
    num = jnp.zeros((2 * reqs, HD), F32)
    for g, pick in zip(groups, picks):
        factor = jnp.where(pick, jnp.exp(item(g, 0) - peak), 0.0)
        den = den + factor * (item(g, 1) + item(g, 2))
        high = factor.astype(BF16)
        low = (factor - high.astype(F32)).astype(BF16)
        entries = jnp.concatenate([scr[:, g, :], scr[:, min(g + 1, slots), :]], axis=0).astype(BF16)
        num = num + dot(jnp.concatenate([high, low], axis=0), entries)
    den = jnp.sum(den, axis=1, keepdims=True)
    some = den > 0.0
    value = (num[:reqs] + num[reqs:]) / jnp.where(some, den, 1.0)
    weighted = jnp.where(some, gate * value, 0.0).astype(BF16)
    tiles = stack.shape[2] // HD
    for load in loads[1 : 1 + heads]:
        load.wait()
    for b in range(heads):
        part = dot(weighted, stack[b ^ head])
        for t in range(tiles):
            terms[:, b * tiles + t, :] = part[:, t * HD : (t + 1) * HD]
    terms_at = out_ref.shape[1] - heads * tiles
    out_ref[:, terms_at:, :] = terms[...].astype(BF16)
    held = reqs * slots
    local = pick_ref.shape[0] // reqs
    for load in loads[1 + heads :]:
        load.wait()
    table = jnp.concatenate(
        [
            got_ref[:, t * slots : (t + 1) * slots, :]
            .astype(F32)
            .reshape(held, HD)
            .astype(BF16)
            for t in range(terms_at // local)
        ],
        axis=1,
    )
    step = 16
    stores = []
    for c in range(0, reqs, step):
        rows = dot(pick_ref[c * local : (c + step) * local, :], table)
        for t in range(terms_at // local):
            out_ref[c : c + step, t * local : (t + 1) * local, :] = (
                rows[:, t * HD : (t + 1) * HD].reshape(step, local, HD).astype(BF16)
            )
        at = pl.ds(c, step)
        stores.append(pltpu.make_async_copy(out_ref.at[at], out_hbm.at[at], out_sems.at[c // step]))
        stores[-1].start()
    for store in stores:
        store.wait()


def route_kernel(new_ref, table_ref, count_ref, out_ref):
    max_new = new_ref.shape[0]
    per_new = table_ref.shape[0] // max_new
    shape = (out_ref.shape[0], new_ref.shape[1])
    slot = over(iota(shape, 0), per_new)
    quarter = rest(iota(shape, 0), per_new)
    found = jnp.zeros(shape, jnp.int32)
    for i in range(max_new):
        filled = jnp.where(i * per_new < count_ref[...], new_ref[i : i + 1, :], -1)
        page = jnp.zeros(shape, jnp.int32)
        for w in range(per_new):
            page = jnp.where(quarter == w, table_ref[i * per_new + w : i * per_new + w + 1, :] + 1, page)
        found = jnp.where(filled == slot, page, found)
    source = jnp.sum(found, axis=1, keepdims=True) - 1
    out_ref[...] = jnp.where(source == iota(out_ref.shape, 1), 1.0, 0.0).astype(BF16)


def sum_kernel(shard_ref, got_hbm, *refs):
    out_refs, (quarters, got_ref, sem) = refs[:-3], refs[-3:]
    terms = got_ref.shape[1]
    load = pltpu.make_async_copy(got_hbm.at[:, got_hbm.shape[1] - terms :, :], got_ref, sem)
    load.start()
    load.wait()
    s = shard_ref[0]
    count = len(out_refs)
    heads = count
    columns = got_ref.shape[0] // EXPERTS
    got = got_ref[...].astype(F32)
    per = got.shape[1] // 2
    for z in range(columns // heads):
        total = jnp.zeros(got.shape[1:], F32)
        for e in range(EXPERTS):
            at = e * columns + z * heads
            total = total + jnp.sum(got[at : at + heads], axis=0)
        for i in range(2):
            quarters[2 * z + i] = total[i * per : (i + 1) * per]
    for t, out_ref in enumerate(out_refs):
        quarter = quarters[lax.rem(s + t, count)]
        for i in range(per):
            out_ref[:, i * HD : (i + 1) * HD] = quarter[i : i + 1, :]


def land_kernel(got_hbm, k_hbm, v_hbm, got_ref, k_ref, v_ref, sems, out_sems):
    total = got_ref.shape[0]
    tiles = k_ref.shape[2] // HD
    rows = total // 2
    loads = []
    for i in range(2):
        at = pl.ds(i * rows, rows)
        loads.append(pltpu.make_async_copy(got_hbm.at[at], got_ref.at[at], sems.at[i]))
        loads[i].start()
    n = k_ref.shape[0] * k_ref.shape[1]
    local = n // rows
    to = iota((n, n), 0)
    fro = iota((n, n), 1)
    perm = jnp.where((over(to, rows) == rest(fro, local)) & (rest(to, rows) == over(fro, local)), 1.0, 0.0).astype(BF16)
    stores = []
    for i, (ref, hbm) in enumerate(((k_ref, k_hbm), (v_ref, v_hbm))):
        base = i * rows
        loads[i].wait()
        flat = jnp.concatenate(
            [
                got_ref[base : base + rows, t * local : (t + 1) * local, :].reshape(n, HD)
                for t in range(tiles)
            ],
            axis=1,
        )
        ref[...] = dot(perm, flat).reshape(ref.shape).astype(BF16)
        stores.append(pltpu.make_async_copy(ref, hbm, out_sems.at[i]))
        stores[i].start()
    for store in stores:
        store.wait()


def shards(
    old_keys,
    old_values,
    keep_lists,
    drop_weights,
    request_pages,
    page_table,
    new_table,
    queries,
    new_keys,
    new_values,
    expert_ids,
    router_logits,
    out_weight,
):
    devices = lax.axis_size("pages")
    shard_count = lax.axis_size("expert")
    my = lax.axis_index("pages").astype(jnp.int32)
    slots, page_len, width = old_keys.shape
    rows = keep_lists.shape[1] + 1
    per_new = page_len // rows
    requests, max_pages = page_table.shape
    new_cap = 2 * (slots // per_new)
    local = new_cap * per_new
    heads = width // HD
    topk = queries.shape[1]
    lines = 2 * slots
    columns = devices // EXPERTS
    head = lax.rem(my, heads)
    shard = lax.axis_index("expert").astype(jnp.int32).reshape(1)
    table = page_table.T
    counts = request_pages.reshape(1, -1)

    outbox = pl.pallas_call(
        source_kernel,
        out_shape=jax.ShapeDtypeStruct((devices, lines + heads * slots, HD), BF16),
        in_specs=[SMEM] + [VMEM] * 11,
        out_specs=VMEM,
        scratch_shapes=[
            pltpu.VMEM((slots * rows, width), BF16),
            pltpu.VMEM((slots * rows, width), BF16),
            pltpu.VMEM((slots, HD), F32),
            pltpu.VMEM((requests, topk, width), F32),
        ],
        name="source",
    )(
        my.reshape(1),
        table,
        counts,
        expert_ids.T,
        keep_lists,
        drop_weights,
        old_keys,
        old_values,
        queries,
        new_keys,
        new_values,
        router_logits,
    )
    inbox = lax.all_to_all(outbox, "pages", split_axis=0, concat_axis=0, tiled=True)

    weight, _ = lax.optimization_barrier((out_weight[0], outbox))
    pieces = [lax.dynamic_slice_in_dim(weight, (head ^ d) * HD, HD, 0) for d in range(1, heads)]
    weights = [
        lax.ppermute(piece, "pages", [(p, p ^ d) for p in range(devices)])
        for d, piece in enumerate(pieces, 1)
    ]
    pick = pl.pallas_call(
        route_kernel,
        out_shape=jax.ShapeDtypeStruct((devices * local, devices * slots), BF16),
        in_specs=[VMEM] * 3,
        out_specs=VMEM,
        compiler_params=PARAMS,
        name="route",
    )(new_table.T, table, counts)
    inbox, pick, weights = lax.optimization_barrier((inbox, pick, weights))

    block_cols = out_weight.shape[2]
    terms = heads * block_cols // HD
    routed = pl.pallas_call(
        middle_kernel,
        out_shape=jax.ShapeDtypeStruct((devices, heads * local + terms, HD), BF16),
        in_specs=[SMEM] + [ANY] * (2 + heads),
        out_specs=ANY,
        scratch_shapes=[
            pltpu.VMEM((requests, lines, HD), F32),
            pltpu.VMEM((requests, terms, HD), F32),
            pltpu.VMEM((heads, HD, block_cols), BF16),
            pltpu.VMEM((devices, lines, HD), BF16),
            pltpu.VMEM((devices, heads * slots, HD), BF16),
            pltpu.VMEM((devices * local, devices * slots), BF16),
            pltpu.VMEM((devices, heads * local + terms, HD), BF16),
            pltpu.SemaphoreType.DMA((heads + 3,)),
            pltpu.SemaphoreType.DMA((devices // 16,)),
        ],
        compiler_params=PARAMS,
        name="middle",
    )(head.reshape(1), inbox, pick, out_weight, *weights)
    landed = lax.all_to_all(routed, "pages", split_axis=0, concat_axis=0, tiled=True)

    quarters = pl.pallas_call(
        sum_kernel,
        out_shape=[jax.ShapeDtypeStruct((1, width), F32)] * shard_count,
        in_specs=[SMEM, ANY],
        out_specs=[VMEM] * shard_count,
        scratch_shapes=[
            pltpu.VMEM((shard_count, width // HD, HD), F32),
            pltpu.VMEM((devices, terms, HD), BF16),
            pltpu.SemaphoreType.DMA(()),
        ],
        compiler_params=PARAMS,
        name="sum",
    )(shard, landed)
    landed, quarters = lax.optimization_barrier((landed, quarters))
    moved = [quarters[0]]
    for t in range(1, shard_count):
        moved.append(
            lax.ppermute(quarters[t], "expert", [(i, (i + t) % shard_count) for i in range(shard_count)])
        )
    new_page = jax.ShapeDtypeStruct((new_cap, per_new * rows, width), BF16)
    compact_keys, compact_values = pl.pallas_call(
        land_kernel,
        out_shape=(new_page, new_page),
        in_specs=[ANY],
        out_specs=(ANY, ANY),
        scratch_shapes=[
            pltpu.VMEM((devices, heads * local + terms, HD), BF16),
            pltpu.VMEM(new_page.shape, BF16),
            pltpu.VMEM(new_page.shape, BF16),
            pltpu.SemaphoreType.DMA((2,)),
            pltpu.SemaphoreType.DMA((2,)),
        ],
        compiler_params=PARAMS,
        name="land",
    )(landed)
    mixed = sum(moved[1:], moved[0]).astype(BF16)
    return (compact_keys, compact_values, mixed)


def solution(mesh):
    in_specs = (
        P("pages", None, "expert"),
        P("pages", None, "expert"),
        P("pages", None),
        P("pages", None),
        P(),
        P(),
        P(),
        P(None, None, "expert"),
        P("pages", "expert"),
        P("pages", "expert"),
        P(),
        P("pages", None),
        P("pages", "expert", None),
    )
    out_specs = (P("pages", None, "expert"), P("pages", None, "expert"), P("pages", "expert"))
    return jax.shard_map(shards, mesh=mesh, in_specs=in_specs, out_specs=out_specs, check_vma=False)
```

```python
import functools
import math

import jax
import jax.numpy as jnp
from jax import lax
from jax.experimental import pallas as pl
from jax.experimental.pallas import tpu as pltpu
from jax.sharding import PartitionSpec as P

HD = 128
EXPERTS = 8
NEGATIVE = -1e30
F32 = jnp.float32
BF16 = jnp.bfloat16
VMEM = pl.BlockSpec(memory_space=pltpu.VMEM)
SMEM = pl.BlockSpec(memory_space=pltpu.SMEM)
ANY = pl.BlockSpec(memory_space=pl.ANY)
PARAMS = pltpu.CompilerParams(vmem_limit_bytes=28 << 20)
NT = (((1,), (1,)), ((), ()))


def iota(shape, dim):
    return lax.broadcasted_iota(jnp.int32, shape, dim)


def over(x, n):
    return lax.shift_right_logical(x, n.bit_length() - 1) if n & (n - 1) == 0 else x // n


def rest(x, n):
    return x & (n - 1) if n & (n - 1) == 0 else x % n


def dot(a, b):
    return jnp.dot(a, b, preferred_element_type=F32)


def source_kernel(
    my_ref,
    table_ref,
    count_ref,
    ids_ref,
    keep_ref,
    drop_ref,
    k_ref,
    v_ref,
    q_ref,
    nk_ref,
    nv_ref,
    logit_ref,
    out_ref,
    kb,
    vb,
    keep_rows,
    q_rows,
):
    my = my_ref[0]
    slots, page_len, width = k_ref.shape
    keep_count = keep_ref.shape[1]
    rows = keep_count + 1
    heads = width // HD
    reqs, topk, _ = q_ref.shape
    keep_rows[...] = jnp.full(keep_rows.shape, -1.0, F32)
    keep_rows[:, 0:keep_count] = keep_ref[...].astype(F32)
    keep_columns = keep_rows[...].T[0:rows, :].astype(jnp.int32)
    q_rows[...] = q_ref[...].astype(F32)
    lane = iota((rows, page_len), 1)
    last = iota((rows, page_len), 0) == rows - 1
    for g in range(slots):
        onehot = jnp.where(keep_columns[:, g : g + 1] == lane, 1.0, 0.0)
        kept = jnp.max(onehot, axis=0, keepdims=True)
        coef = jnp.where(kept > 0.0, 0.0, drop_ref[g : g + 1, :].astype(F32))
        total = jnp.sum(coef, axis=1, keepdims=True)
        mat = jnp.where(last, coef, onehot).astype(BF16)
        denom = jnp.where(last[rows - 8 :, 0:1], total, 1.0)
        for ref, blocks in ((k_ref, kb), (v_ref, vb)):
            block = dot(mat, ref[g])
            block = jnp.concatenate([block[: rows - 8], block[rows - 8 :] / denom], axis=0)
            blocks[g * rows : (g + 1) * rows, :] = block.astype(BF16)
    n = slots * rows
    ent = 2 * slots
    ent_row = iota((ent, reqs), 0)
    req_lane = iota((ent, reqs), 1)
    sel = jnp.where((ent_row == slots) & (req_lane == my), 1.0, 0.0)
    in_use = iota(table_ref.shape, 0) < count_ref[...]
    table = jnp.where(in_use, table_ref[...], -1)
    for g in range(slots):
        hit = jnp.where(table == my * slots + g, 1.0, 0.0)
        sel = jnp.where(ent_row == g, jnp.max(hit, axis=0, keepdims=True), sel)
    sel_b = sel.astype(BF16)
    same = lax.dot_general(sel_b, sel_b, NT, preferred_element_type=F32)
    q_lane = over(iota((ent, width), 1), HD)
    pieces = []
    for k in range(topk):
        group_query = dot(sel_b, q_rows[:, k, :].astype(BF16))
        for h in range(heads):
            pieces.append(jnp.where(q_lane == h, group_query, 0.0))
    queries = jnp.concatenate(pieces, axis=0)
    kh = topk * heads
    scale = 1.0 / math.sqrt(HD)
    scores = lax.dot_general(queries.astype(BF16), kb[...], NT, preferred_element_type=F32) * scale
    col = iota((kh * ent, n), 1)
    scores = scores + jnp.where(rest(col, rows) == rows - 1, math.log(page_len - rows + 1), 0.0)
    of_page = jnp.where(over(iota((ent, n), 1), rows) == iota((ent, n), 0), 1.0, 0.0).astype(BF16)
    shared = dot(same.astype(BF16), of_page)
    mask = jnp.concatenate([shared] * kh, axis=0) > 0.5
    scores = jnp.where(mask, scores, NEGATIVE)
    is_own = rest(iota((kh * ent, 1), 0), ent) == slots
    own = jnp.sum(queries * nk_ref[...].astype(F32), axis=1, keepdims=True) * scale
    own = jnp.where(is_own, own, NEGATIVE)
    peak = jnp.maximum(jnp.max(scores, axis=1, keepdims=True), own)
    shift = peak.astype(BF16).astype(F32)
    probs = jnp.where(mask, jnp.exp(scores - shift), 0.0)
    own_prob = jnp.where(is_own, jnp.exp(own - shift), 0.0)
    den = jnp.sum(probs, axis=1, keepdims=True) + own_prob
    num = dot(probs.astype(BF16), vb[...])
    num = num + own_prob.astype(BF16).astype(F32) * nv_ref[...].astype(F32)
    high = den.astype(BF16).astype(F32)
    low = den - high
    er = iota((ent, ent), 0)
    ec = iota((ent, ent), 1)
    before = jnp.sum(jnp.where((ec < er) | (ec == slots), same, 0.0), axis=1, keepdims=True)
    row = ent_row[:, 0:1]
    first = (row == slots) | ((row < slots) & (before < 0.5))
    request = jnp.sum(jnp.where(sel > 0.5, req_lane.astype(F32), 0.0), axis=1, keepdims=True)
    expert = [
        jnp.sum(jnp.where(sel > 0.5, ids_ref[k : k + 1, :].astype(F32), 0.0), axis=1, keepdims=True)
        for k in range(topk)
    ]
    expert_lane = iota((1, EXPERTS), 1).astype(F32)
    logit = [
        jnp.sum(
            jnp.where(expert_lane == expert[k][slots : slots + 1, :], logit_ref[...], 0.0),
            axis=1,
            keepdims=True,
        )
        for k in range(topk)
    ]
    top = logit[0]
    for k in range(1, topk):
        top = jnp.maximum(top, logit[k])
    terms = [jnp.exp(logit[k] - top) for k in range(topk)]
    term_sum = terms[0]
    for k in range(1, topk):
        term_sum = term_sum + terms[k]
    stat_lane = iota((ent, HD), 1)
    by_choice = []
    for k in range(topk):
        gate = jnp.where(row == slots, terms[k] / term_sum, 0.0)
        gate_high = gate.astype(BF16).astype(F32)
        stats = jnp.where(stat_lane == 3 * heads, gate_high, 0.0)
        stats = jnp.where(stat_lane == 3 * heads + 1, gate - gate_high, stats)
        stats = jnp.where(stat_lane == 3 * heads + 2, request, stats)
        lanes = []
        for h in range(heads):
            at = slice((k * heads + h) * ent, (k * heads + h + 1) * ent)
            lanes.append(num[at, h * HD : (h + 1) * HD])
            for i, stat in enumerate((shift, high, low)):
                stats = jnp.where(stat_lane == 3 * h + i, stat[at, :], stats)
        by_choice.append(jnp.concatenate(lanes + [stats], axis=1))
    parts = []
    for e in range(EXPERTS):
        part = jnp.zeros(by_choice[0].shape, F32)
        for k in range(topk):
            part = jnp.where(first & (expert[k] == e), by_choice[k], part)
        parts.append(part)
    entries = jnp.concatenate(parts, axis=0)
    stats = entries[:, width:].astype(BF16)
    devices = out_ref.shape[0]
    lines = out_ref.shape[1] - heads * slots
    columns = devices // EXPERTS
    to = iota((EXPERTS * lines, EXPERTS * ent), 0)
    fro = iota((EXPERTS * lines, EXPERTS * ent), 1)
    flat = (over(to, lines) == over(fro, ent)) & (rest(to, lines) == slots + 1)
    flat = jnp.where(flat, 1.0, 0.0).astype(BF16)
    square = iota((HD, HD), 0)
    item = iota((HD, HD), 1) % 6
    mine = iota((EXPERTS * ent, HD), 1) // 6 == rest(iota((EXPERTS * ent, HD), 0), ent)
    for h in range(heads):
        origin = jnp.where(item < 3, 3 * h + item, 3 * heads + item - 3)
        spread = dot(stats, jnp.where(square == origin, 1.0, 0.0).astype(BF16))
        line = dot(flat, jnp.where(mine, spread, 0.0).astype(BF16))
        sent = (entries[:, h * HD : (h + 1) * HD] + line).astype(BF16)
        for e in range(EXPERTS):
            for z in range(columns // heads):
                out_ref[e * columns + z * heads + h, 0:lines, :] = sent[e * lines : (e + 1) * lines, :]
    to = iota((n, n), 0)
    fro = iota((n, n), 1)
    perm = jnp.where((rest(to, slots) == over(fro, rows)) & (over(to, slots) == rest(fro, rows)), 1.0, 0.0).astype(BF16)
    for base, blocks in ((0, kb), (rows, vb)):
        spread = dot(perm, blocks[...])
        for t in range(heads):
            at = slice(lines + t * slots, lines + (t + 1) * slots)
            out_ref[base : base + rows, at, :] = (
                spread[:, t * HD : (t + 1) * HD].reshape(rows, slots, HD).astype(BF16)
            )


def expert_kernel(at_ref, got_hbm, *refs):
    scr, halves, stack, parts, sems = refs[-5:]
    heads = stack.shape[0]
    w_refs, out_refs = refs[:heads], refs[heads:-5]
    page = at_ref[0]
    shard = at_ref[1]
    head = page & (heads - 1)
    group = lax.shift_right_logical(page, 2) & 1
    reqs, lines, _ = scr.shape
    slots = lines // 2
    depth = stack.shape[1]
    loads = [pltpu.make_async_copy(got_hbm.at[:, 0:lines, :], parts, sems.at[0])]
    loads.append(
        pltpu.make_async_copy(w_refs[0].at[0, pl.ds(head * depth, depth), :], stack.at[0], sems.at[1])
    )
    for d in range(1, heads):
        loads.append(pltpu.make_async_copy(w_refs[d], stack.at[d], sems.at[1 + d]))
    for load in loads:
        load.start()
    loads[0].wait()
    scr[...] = parts[...].astype(F32)
    stats = scr[:, slots + 1, :]
    stats = jnp.concatenate([stats, stats], axis=0).T
    left = iota((1, 2 * reqs), 1) < reqs
    order = iota((reqs, 2 * reqs), 0)
    target = (rest(order, reqs // 2) * 2 + over(order, reqs // 2)).astype(F32)

    def item(g, i):
        first = stats[6 * g + i : 6 * g + i + 1, :]
        if g == slots:
            return jnp.where(left, first, 0.0)
        return jnp.where(left, first, stats[6 * g + 6 + i : 6 * g + 7 + i, :])

    groups = range(0, slots + 1, 2)
    picks = [(item(g, 5) == target) & (item(g, 1) > 0.0) for g in groups]
    gate = jnp.zeros(target.shape, F32)
    peak = jnp.full(target.shape, NEGATIVE, F32)
    for g, pick in zip(groups, picks):
        gate = gate + jnp.where(pick, item(g, 3) + item(g, 4), 0.0)
        peak = jnp.maximum(peak, jnp.where(pick, item(g, 0), NEGATIVE))
    gate = jnp.sum(gate, axis=1, keepdims=True)
    peak = jnp.max(peak, axis=1, keepdims=True)
    den = jnp.zeros(target.shape, F32)
    num = jnp.zeros((2 * reqs, HD), F32)
    for g, pick in zip(groups, picks):
        factor = jnp.where(pick, jnp.exp(item(g, 0) - peak), 0.0)
        den = den + factor * (item(g, 1) + item(g, 2))
        high = factor.astype(BF16)
        low = (factor - high.astype(F32)).astype(BF16)
        entries = jnp.concatenate([scr[:, g, :], scr[:, min(g + 1, slots), :]], axis=0).astype(BF16)
        num = num + dot(jnp.concatenate([high, low], axis=0), entries)
    den = jnp.sum(den, axis=1, keepdims=True)
    some = den > 0.0
    value = (num[:reqs] + num[reqs:]) / jnp.where(some, den, 1.0)
    weighted = jnp.where(some, gate * value, 0.0).astype(BF16)
    for load in loads[1:]:
        load.wait()
    cols = stack.shape[2]
    for b in range(heads):
        at = slice(b % 2 * cols, (b % 2 + 1) * cols)
        halves[b // 2, :, at] = dot(weighted, stack[b ^ head])
    for t, out_ref in enumerate(out_refs):
        part = halves[(shard + t) & 1]
        if t == 0:
            part = jnp.where(lax.shift_right_logical(shard, 1) == group, part, 0.0)
        out_ref[...] = part.astype(BF16)


def stage_kernel(at_ref, *refs, count):
    in_refs, out_refs, (total,) = refs[: -count - 1], refs[-count - 1 : -1], refs[-1:]
    value = in_refs[0][...].astype(F32)
    for ref in in_refs[1:]:
        value = value + ref[...].astype(F32)
    total[...] = value
    rows = value.shape[0] // count
    for t, out_ref in enumerate(out_refs):
        at = ((at_ref[0] + t) & (count - 1)) * rows
        if rows % 8 == 0:
            at = pl.multiple_of(at, 8)
        out_ref[...] = total[pl.ds(at, rows), :]


def relay_kernel(got_hbm, pick_hbm, out_hbm, got_ref, pick_ref, out_ref, sems, out_sems):
    reqs, width, _ = got_ref.shape
    slots = width // 4
    lines = got_hbm.shape[1] - width
    loads = [
        pltpu.make_async_copy(got_hbm.at[:, lines:, :], got_ref, sems.at[0]),
        pltpu.make_async_copy(pick_hbm, pick_ref, sems.at[1]),
    ]
    for load in loads:
        load.start()
    for load in loads:
        load.wait()
    terms_at = out_ref.shape[1]
    held = reqs * slots
    local = pick_ref.shape[0] // reqs
    table = jnp.concatenate(
        [
            got_ref[:, t * slots : (t + 1) * slots, :]
            .astype(F32)
            .reshape(held, HD)
            .astype(BF16)
            for t in range(terms_at // local)
        ],
        axis=1,
    )
    step = 16
    stores = []
    for c in range(0, reqs, step):
        rows = dot(pick_ref[c * local : (c + step) * local, :], table)
        for t in range(terms_at // local):
            out_ref[c : c + step, t * local : (t + 1) * local, :] = (
                rows[:, t * HD : (t + 1) * HD].reshape(step, local, HD).astype(BF16)
            )
        at = pl.ds(c, step)
        stores.append(pltpu.make_async_copy(out_ref.at[at], out_hbm.at[at], out_sems.at[c // step]))
        stores[-1].start()
    for store in stores:
        store.wait()


def route_kernel(new_ref, table_ref, count_ref, out_ref):
    max_new = new_ref.shape[0]
    per_new = table_ref.shape[0] // max_new
    shape = (out_ref.shape[0], new_ref.shape[1])
    slot = over(iota(shape, 0), per_new)
    quarter = rest(iota(shape, 0), per_new)
    found = jnp.zeros(shape, jnp.int32)
    for i in range(max_new):
        filled = jnp.where(i * per_new < count_ref[...], new_ref[i : i + 1, :], -1)
        page = jnp.zeros(shape, jnp.int32)
        for w in range(per_new):
            page = jnp.where(quarter == w, table_ref[i * per_new + w : i * per_new + w + 1, :] + 1, page)
        found = jnp.where(filled == slot, page, found)
    source = jnp.sum(found, axis=1, keepdims=True) - 1
    out_ref[...] = jnp.where(source == iota(out_ref.shape, 1), 1.0, 0.0).astype(BF16)


def land_kernel(got_hbm, k_hbm, v_hbm, got_ref, k_ref, v_ref, sems, out_sems):
    total = got_ref.shape[0]
    tiles = k_ref.shape[2] // HD
    rows = total // 2
    loads = []
    for i in range(2):
        at = pl.ds(i * rows, rows)
        loads.append(pltpu.make_async_copy(got_hbm.at[at], got_ref.at[at], sems.at[i]))
        loads[i].start()
    n = k_ref.shape[0] * k_ref.shape[1]
    local = n // rows
    to = iota((n, n), 0)
    fro = iota((n, n), 1)
    perm = jnp.where((over(to, rows) == rest(fro, local)) & (rest(to, rows) == over(fro, local)), 1.0, 0.0).astype(BF16)
    stores = []
    for i, (ref, hbm) in enumerate(((k_ref, k_hbm), (v_ref, v_hbm))):
        base = i * rows
        loads[i].wait()
        flat = jnp.concatenate(
            [
                got_ref[base : base + rows, t * local : (t + 1) * local, :].reshape(n, HD)
                for t in range(tiles)
            ],
            axis=1,
        )
        ref[...] = dot(perm, flat).reshape(ref.shape).astype(BF16)
        stores.append(pltpu.make_async_copy(ref, hbm, out_sems.at[i]))
        stores[i].start()
    for store in stores:
        store.wait()


def shards(
    old_keys,
    old_values,
    keep_lists,
    drop_weights,
    request_pages,
    page_table,
    new_table,
    queries,
    new_keys,
    new_values,
    expert_ids,
    router_logits,
    out_weight,
):
    devices = lax.axis_size("pages")
    shard_count = lax.axis_size("expert")
    my = lax.axis_index("pages").astype(jnp.int32)
    slots, page_len, width = old_keys.shape
    rows = keep_lists.shape[1] + 1
    per_new = page_len // rows
    requests, max_pages = page_table.shape
    new_cap = 2 * (slots // per_new)
    local = new_cap * per_new
    heads = width // HD
    topk = queries.shape[1]
    lines = 2 * slots
    columns = devices // EXPERTS
    head = lax.rem(my, heads)
    shard = lax.axis_index("expert").astype(jnp.int32)
    table = page_table.T
    counts = request_pages.reshape(1, -1)

    outbox = pl.pallas_call(
        source_kernel,
        out_shape=jax.ShapeDtypeStruct((devices, lines + heads * slots, HD), BF16),
        in_specs=[SMEM] + [VMEM] * 11,
        out_specs=VMEM,
        scratch_shapes=[
            pltpu.VMEM((slots * rows, width), BF16),
            pltpu.VMEM((slots * rows, width), BF16),
            pltpu.VMEM((slots, HD), F32),
            pltpu.VMEM((requests, topk, width), F32),
        ],
        name="source",
    )(
        my.reshape(1),
        table,
        counts,
        expert_ids.T,
        keep_lists,
        drop_weights,
        old_keys,
        old_values,
        queries,
        new_keys,
        new_values,
        router_logits,
    )
    inbox = lax.all_to_all(outbox, "pages", split_axis=0, concat_axis=0, tiled=True)

    weight, _ = lax.optimization_barrier((out_weight[0], outbox))
    pieces = [lax.dynamic_slice_in_dim(weight, (head ^ d) * HD, HD, 0) for d in range(1, heads)]
    weights = [
        lax.ppermute(piece, "pages", [(p, p ^ d) for p in range(devices)])
        for d, piece in enumerate(pieces, 1)
    ]
    pick = pl.pallas_call(
        route_kernel,
        out_shape=jax.ShapeDtypeStruct((devices * local, devices * slots), BF16),
        in_specs=[VMEM] * 3,
        out_specs=VMEM,
        compiler_params=PARAMS,
        name="route",
    )(new_table.T, table, counts)
    inbox, pick, weights = lax.optimization_barrier((inbox, pick, weights))

    routed = pl.pallas_call(
        relay_kernel,
        out_shape=jax.ShapeDtypeStruct((devices, heads * local, HD), BF16),
        in_specs=[ANY, ANY],
        out_specs=ANY,
        scratch_shapes=[
            pltpu.VMEM((devices, heads * slots, HD), BF16),
            pltpu.VMEM((devices * local, devices * slots), BF16),
            pltpu.VMEM((devices, heads * local, HD), BF16),
            pltpu.SemaphoreType.DMA((2,)),
            pltpu.SemaphoreType.DMA((devices // 16,)),
        ],
        compiler_params=PARAMS,
        name="relay",
    )(inbox, pick)
    landed = lax.all_to_all(routed, "pages", split_axis=0, concat_axis=0, tiled=True)

    inbox, _ = lax.optimization_barrier((inbox, routed))
    block_cols = out_weight.shape[2]
    deep = columns
    tall = devices // (2 * deep)
    parts = pl.pallas_call(
        expert_kernel,
        out_shape=[jax.ShapeDtypeStruct((requests, width), BF16)] * shard_count,
        in_specs=[SMEM, ANY] + [ANY] * heads,
        out_specs=[VMEM] * shard_count,
        scratch_shapes=[
            pltpu.VMEM((requests, lines, HD), F32),
            pltpu.VMEM((2, requests, width), F32),
            pltpu.VMEM((heads, HD, block_cols), BF16),
            pltpu.VMEM((devices, lines, HD), BF16),
            pltpu.SemaphoreType.DMA((heads + 1,)),
        ],
        compiler_params=PARAMS,
        name="expert",
    )(jnp.stack([my, shard]), inbox, out_weight, *weights)

    def holds(p, q):
        return p // heads % 2 == q // 2

    def stage(arrays, count, place, name):
        rows, cols = arrays[0].shape
        return pl.pallas_call(
            functools.partial(stage_kernel, count=count),
            out_shape=[jax.ShapeDtypeStruct((rows // count, cols), F32)] * count,
            in_specs=[SMEM] + [VMEM] * len(arrays),
            out_specs=[VMEM] * count,
            scratch_shapes=[pltpu.VMEM((rows, cols), F32)],
            compiler_params=PARAMS,
            name=name,
        )(place.reshape(1), *arrays)

    arrived = [parts[0]]
    for t in range(1, shard_count):
        moves = []
        for p in range(devices):
            for s in range(shard_count):
                q = (s + t) % shard_count
                if holds(p, q):
                    moves.append((p * shard_count + s, p * shard_count + q))
        arrived.append(lax.ppermute(parts[t], ("pages", "expert"), moves))

    def send(arrays, target):
        result = [arrays[0]]
        for t in range(1, len(arrays)):
            moves = [
                (p * shard_count + q, target(p, t) * shard_count + q)
                for p in range(devices)
                for q in range(shard_count)
                if holds(p, q)
            ]
            result.append(lax.ppermute(arrays[t], ("pages", "expert"), moves))
        return result

    parts = stage(arrived, 2, my & 1, "by_core")
    arrived = send(parts, lambda p, t: p ^ t)
    parts = stage(arrived, tall, lax.shift_right_logical(my, 4), "by_y")
    arrived = send(parts, lambda p, t: (p + 2 * deep * t) % devices)
    parts = stage(arrived, deep, lax.shift_right_logical(my, 1) & (deep - 1), "by_z")
    landed, _ = lax.optimization_barrier((landed, parts))
    arrived = send(
        parts, lambda p, t: p // (2 * deep) * 2 * deep + (p + 2 * t) % (2 * deep)
    )
    mixed = sum(arrived[1:], arrived[0]).astype(BF16)
    new_page = jax.ShapeDtypeStruct((new_cap, per_new * rows, width), BF16)
    compact_keys, compact_values = pl.pallas_call(
        land_kernel,
        out_shape=(new_page, new_page),
        in_specs=[ANY],
        out_specs=(ANY, ANY),
        scratch_shapes=[
            pltpu.VMEM((devices, heads * local, HD), BF16),
            pltpu.VMEM(new_page.shape, BF16),
            pltpu.VMEM(new_page.shape, BF16),
            pltpu.SemaphoreType.DMA((2,)),
            pltpu.SemaphoreType.DMA((2,)),
        ],
        compiler_params=PARAMS,
        name="land",
    )(landed)
    return (compact_keys, compact_values, mixed)


def solution(mesh):
    in_specs = (
        P("pages", None, "expert"),
        P("pages", None, "expert"),
        P("pages", None),
        P("pages", None),
        P(),
        P(),
        P(),
        P(None, None, "expert"),
        P("pages", "expert"),
        P("pages", "expert"),
        P(),
        P("pages", None),
        P("pages", "expert", None),
    )
    out_specs = (P("pages", None, "expert"), P("pages", None, "expert"), P("pages", "expert"))
    return jax.shard_map(shards, mesh=mesh, in_specs=in_specs, out_specs=out_specs, check_vma=False)
```

```python
import functools
import math

import jax
import jax.numpy as jnp
from jax import lax
from jax.experimental import pallas as pl
from jax.experimental.pallas import tpu as pltpu
from jax.sharding import PartitionSpec as P

HD = 128
EXPERTS = 8
NEGATIVE = -1e30
F32 = jnp.float32
BF16 = jnp.bfloat16
VMEM = pl.BlockSpec(memory_space=pltpu.VMEM)
SMEM = pl.BlockSpec(memory_space=pltpu.SMEM)
ANY = pl.BlockSpec(memory_space=pl.ANY)
PARAMS = pltpu.CompilerParams(vmem_limit_bytes=28 << 20)
NT = (((1,), (1,)), ((), ()))


def iota(shape, dim):
    return lax.broadcasted_iota(jnp.int32, shape, dim)


def over(x, n):
    return lax.shift_right_logical(x, n.bit_length() - 1) if n & (n - 1) == 0 else x // n


def rest(x, n):
    return x & (n - 1) if n & (n - 1) == 0 else x % n


def dot(a, b):
    return jnp.dot(a, b, preferred_element_type=F32)


def source_kernel(
    my_ref,
    table_ref,
    count_ref,
    ids_ref,
    keep_ref,
    drop_ref,
    k_hbm,
    v_hbm,
    q_ref,
    nk_ref,
    nv_ref,
    logit_ref,
    out_hbm,
    kb,
    vb,
    keep_rows,
    q_rows,
    k_ref,
    v_ref,
    row_ref,
    part_ref,
    mats,
    sems,
):
    loads = [
        pltpu.make_async_copy(k_hbm, k_ref, sems.at[0]),
        pltpu.make_async_copy(v_hbm, v_ref, sems.at[1]),
    ]
    for load in loads:
        load.start()
    my = my_ref[0]
    slots, page_len, width = k_ref.shape
    lines = part_ref.shape[1]
    keep_count = keep_ref.shape[1]
    rows = keep_count + 1
    heads = width // HD
    reqs, topk, _ = q_ref.shape
    keep_rows[...] = jnp.full(keep_rows.shape, -1.0, F32)
    keep_rows[:, 0:keep_count] = keep_ref[...].astype(F32)
    keep_columns = keep_rows[...].T[0:rows, :].astype(jnp.int32)
    q_rows[...] = q_ref[...].astype(F32)
    lane = iota((rows, page_len), 1)
    last = iota((rows, page_len), 0) == rows - 1
    totals = []
    for g in range(slots):
        onehot = jnp.where(keep_columns[:, g : g + 1] == lane, 1.0, 0.0)
        kept = jnp.max(onehot, axis=0, keepdims=True)
        coef = jnp.where(kept > 0.0, 0.0, drop_ref[g : g + 1, :].astype(F32))
        total = jnp.sum(coef, axis=1, keepdims=True)
        mats[g] = jnp.where(last, coef, onehot).astype(BF16)
        totals.append(jnp.where(last[rows - 8 :, 0:1], total, 1.0))
    n = slots * rows
    to = iota((n, n), 0)
    fro = iota((n, n), 1)
    perm = (rest(to, slots) == over(fro, rows)) & (over(to, slots) == rest(fro, rows))
    perm = jnp.where(perm, 1.0, 0.0).astype(BF16)
    for i, (ref, blocks) in enumerate(((k_ref, kb), (v_ref, vb))):
        loads[i].wait()
        for g in range(slots):
            block = dot(mats[g], ref[g])
            block = jnp.concatenate([block[: rows - 8], block[rows - 8 :] / totals[g]], axis=0)
            blocks[g * rows : (g + 1) * rows, :] = block.astype(BF16)
        spread = dot(perm, blocks[...])
        for t in range(heads):
            row_ref[i * rows : (i + 1) * rows, t * slots : (t + 1) * slots, :] = (
                spread[:, t * HD : (t + 1) * HD].reshape(rows, slots, HD).astype(BF16)
            )
    row_store = pltpu.make_async_copy(row_ref, out_hbm.at[:, lines:, :], sems.at[2])
    row_store.start()
    ent = 2 * slots
    ent_row = iota((ent, reqs), 0)
    req_lane = iota((ent, reqs), 1)
    sel = jnp.where((ent_row == slots) & (req_lane == my), 1.0, 0.0)
    in_use = iota(table_ref.shape, 0) < count_ref[...]
    table = jnp.where(in_use, table_ref[...], -1)
    for g in range(slots):
        hit = jnp.where(table == my * slots + g, 1.0, 0.0)
        sel = jnp.where(ent_row == g, jnp.max(hit, axis=0, keepdims=True), sel)
    sel_b = sel.astype(BF16)
    same = lax.dot_general(sel_b, sel_b, NT, preferred_element_type=F32)
    q_lane = over(iota((ent, width), 1), HD)
    pieces = []
    for k in range(topk):
        group_query = dot(sel_b, q_rows[:, k, :].astype(BF16))
        for h in range(heads):
            pieces.append(jnp.where(q_lane == h, group_query, 0.0))
    queries = jnp.concatenate(pieces, axis=0)
    kh = topk * heads
    scale = 1.0 / math.sqrt(HD)
    scores = lax.dot_general(queries.astype(BF16), kb[...], NT, preferred_element_type=F32) * scale
    col = iota((kh * ent, n), 1)
    scores = scores + jnp.where(rest(col, rows) == rows - 1, math.log(page_len - rows + 1), 0.0)
    of_page = jnp.where(over(iota((ent, n), 1), rows) == iota((ent, n), 0), 1.0, 0.0).astype(BF16)
    shared = dot(same.astype(BF16), of_page)
    mask = jnp.concatenate([shared] * kh, axis=0) > 0.5
    scores = jnp.where(mask, scores, NEGATIVE)
    is_own = rest(iota((kh * ent, 1), 0), ent) == slots
    own = jnp.sum(queries * nk_ref[...].astype(F32), axis=1, keepdims=True) * scale
    own = jnp.where(is_own, own, NEGATIVE)
    peak = jnp.maximum(jnp.max(scores, axis=1, keepdims=True), own)
    shift = peak.astype(BF16).astype(F32)
    probs = jnp.where(mask, jnp.exp(scores - shift), 0.0)
    own_prob = jnp.where(is_own, jnp.exp(own - shift), 0.0)
    den = jnp.sum(probs, axis=1, keepdims=True) + own_prob
    num = dot(probs.astype(BF16), vb[...])
    num = num + own_prob.astype(BF16).astype(F32) * nv_ref[...].astype(F32)
    high = den.astype(BF16).astype(F32)
    low = den - high
    er = iota((ent, ent), 0)
    ec = iota((ent, ent), 1)
    before = jnp.sum(jnp.where((ec < er) | (ec == slots), same, 0.0), axis=1, keepdims=True)
    row = ent_row[:, 0:1]
    first = (row == slots) | ((row < slots) & (before < 0.5))
    request = jnp.sum(jnp.where(sel > 0.5, req_lane.astype(F32), 0.0), axis=1, keepdims=True)
    expert = [
        jnp.sum(jnp.where(sel > 0.5, ids_ref[k : k + 1, :].astype(F32), 0.0), axis=1, keepdims=True)
        for k in range(topk)
    ]
    expert_lane = iota((1, EXPERTS), 1).astype(F32)
    logit = [
        jnp.sum(
            jnp.where(expert_lane == expert[k][slots : slots + 1, :], logit_ref[...], 0.0),
            axis=1,
            keepdims=True,
        )
        for k in range(topk)
    ]
    top = logit[0]
    for k in range(1, topk):
        top = jnp.maximum(top, logit[k])
    terms = [jnp.exp(logit[k] - top) for k in range(topk)]
    term_sum = terms[0]
    for k in range(1, topk):
        term_sum = term_sum + terms[k]
    stat_lane = iota((ent, HD), 1)
    by_choice = []
    for k in range(topk):
        gate = jnp.where(row == slots, terms[k] / term_sum, 0.0)
        gate_high = gate.astype(BF16).astype(F32)
        stats = jnp.where(stat_lane == 3 * heads, gate_high, 0.0)
        stats = jnp.where(stat_lane == 3 * heads + 1, gate - gate_high, stats)
        stats = jnp.where(stat_lane == 3 * heads + 2, request, stats)
        lanes = []
        for h in range(heads):
            at = slice((k * heads + h) * ent, (k * heads + h + 1) * ent)
            lanes.append(num[at, h * HD : (h + 1) * HD])
            for i, stat in enumerate((shift, high, low)):
                stats = jnp.where(stat_lane == 3 * h + i, stat[at, :], stats)
        by_choice.append(jnp.concatenate(lanes + [stats], axis=1))
    parts = []
    for e in range(EXPERTS):
        part = jnp.zeros(by_choice[0].shape, F32)
        for k in range(topk):
            part = jnp.where(first & (expert[k] == e), by_choice[k], part)
        parts.append(part)
    entries = jnp.concatenate(parts, axis=0)
    stats = entries[:, width:].astype(BF16)
    columns = part_ref.shape[0] // EXPERTS
    to = iota((EXPERTS * lines, EXPERTS * ent), 0)
    fro = iota((EXPERTS * lines, EXPERTS * ent), 1)
    flat = (over(to, lines) == over(fro, ent)) & (rest(to, lines) == slots + 1)
    flat = jnp.where(flat, 1.0, 0.0).astype(BF16)
    square = iota((HD, HD), 0)
    item = iota((HD, HD), 1) % 6
    mine = iota((EXPERTS * ent, HD), 1) // 6 == rest(iota((EXPERTS * ent, HD), 0), ent)
    for h in range(heads):
        origin = jnp.where(item < 3, 3 * h + item, 3 * heads + item - 3)
        spread = dot(stats, jnp.where(square == origin, 1.0, 0.0).astype(BF16))
        line = dot(flat, jnp.where(mine, spread, 0.0).astype(BF16))
        sent = (entries[:, h * HD : (h + 1) * HD] + line).astype(BF16)
        for e in range(EXPERTS):
            for z in range(columns // heads):
                part_ref[e * columns + z * heads + h] = sent[e * lines : (e + 1) * lines, :]
    part_store = pltpu.make_async_copy(part_ref, out_hbm.at[:, 0:lines, :], sems.at[3])
    part_store.start()
    row_store.wait()
    part_store.wait()


def middle_kernel(head_ref, got_hbm, pick_hbm, *refs):
    w_refs, (out_hbm, scr, terms, stack, parts, got_ref, pick_ref, out_ref, sems, out_sems) = (
        refs[:-10],
        refs[-10:],
    )
    heads = len(w_refs)
    head = head_ref[0]
    reqs, lines, _ = scr.shape
    slots = lines // 2
    depth = stack.shape[1]
    loads = [pltpu.make_async_copy(got_hbm.at[:, 0:lines, :], parts, sems.at[0])]
    loads.append(
        pltpu.make_async_copy(w_refs[0].at[0, pl.ds(head * depth, depth), :], stack.at[0], sems.at[1])
    )
    for d in range(1, heads):
        loads.append(pltpu.make_async_copy(w_refs[d], stack.at[d], sems.at[1 + d]))
    loads.append(pltpu.make_async_copy(got_hbm.at[:, lines:, :], got_ref, sems.at[heads + 1]))
    loads.append(pltpu.make_async_copy(pick_hbm, pick_ref, sems.at[heads + 2]))
    for load in loads:
        load.start()
    loads[0].wait()
    scr[...] = parts[...].astype(F32)
    stats = scr[:, slots + 1, :]
    stats = jnp.concatenate([stats, stats], axis=0).T
    left = iota((1, 2 * reqs), 1) < reqs
    target = iota((reqs, 2 * reqs), 0).astype(F32)

    def item(g, i):
        first = stats[6 * g + i : 6 * g + i + 1, :]
        if g == slots:
            return jnp.where(left, first, 0.0)
        return jnp.where(left, first, stats[6 * g + 6 + i : 6 * g + 7 + i, :])

    groups = range(0, slots + 1, 2)
    picks = [(item(g, 5) == target) & (item(g, 1) > 0.0) for g in groups]
    gate = jnp.zeros(target.shape, F32)
    peak = jnp.full(target.shape, NEGATIVE, F32)
    for g, pick in zip(groups, picks):
        gate = gate + jnp.where(pick, item(g, 3) + item(g, 4), 0.0)
        peak = jnp.maximum(peak, jnp.where(pick, item(g, 0), NEGATIVE))
    gate = jnp.sum(gate, axis=1, keepdims=True)
    peak = jnp.max(peak, axis=1, keepdims=True)
    den = jnp.zeros(target.shape, F32)
    num = jnp.zeros((2 * reqs, HD), F32)
    for g, pick in zip(groups, picks):
        factor = jnp.where(pick, jnp.exp(item(g, 0) - peak), 0.0)
        den = den + factor * (item(g, 1) + item(g, 2))
        high = factor.astype(BF16)
        low = (factor - high.astype(F32)).astype(BF16)
        entries = jnp.concatenate([scr[:, g, :], scr[:, min(g + 1, slots), :]], axis=0).astype(BF16)
        num = num + dot(jnp.concatenate([high, low], axis=0), entries)
    den = jnp.sum(den, axis=1, keepdims=True)
    some = den > 0.0
    value = (num[:reqs] + num[reqs:]) / jnp.where(some, den, 1.0)
    weighted = jnp.where(some, gate * value, 0.0).astype(BF16)
    tiles = stack.shape[2] // HD
    for load in loads[1 : 1 + heads]:
        load.wait()
    for b in range(heads):
        part = dot(weighted, stack[b ^ head])
        for t in range(tiles):
            terms[:, b * tiles + t, :] = part[:, t * HD : (t + 1) * HD]
    terms_at = out_ref.shape[1] - heads * tiles
    out_ref[:, terms_at:, :] = terms[...].astype(BF16)
    held = reqs * slots
    local = pick_ref.shape[0] // reqs
    for load in loads[1 + heads :]:
        load.wait()
    table = jnp.concatenate(
        [
            got_ref[:, t * slots : (t + 1) * slots, :]
            .astype(F32)
            .reshape(held, HD)
            .astype(BF16)
            for t in range(terms_at // local)
        ],
        axis=1,
    )
    step = 16
    stores = []
    for c in range(0, reqs, step):
        rows = dot(pick_ref[c * local : (c + step) * local, :], table)
        for t in range(terms_at // local):
            out_ref[c : c + step, t * local : (t + 1) * local, :] = (
                rows[:, t * HD : (t + 1) * HD].reshape(step, local, HD).astype(BF16)
            )
        at = pl.ds(c, step)
        stores.append(pltpu.make_async_copy(out_ref.at[at], out_hbm.at[at], out_sems.at[c // step]))
        stores[-1].start()
    for store in stores:
        store.wait()


def route_kernel(new_ref, table_ref, count_ref, out_ref):
    max_new = new_ref.shape[0]
    per_new = table_ref.shape[0] // max_new
    shape = (out_ref.shape[0], new_ref.shape[1])
    slot = over(iota(shape, 0), per_new)
    quarter = rest(iota(shape, 0), per_new)
    found = jnp.zeros(shape, jnp.int32)
    for i in range(max_new):
        filled = jnp.where(i * per_new < count_ref[...], new_ref[i : i + 1, :], -1)
        page = jnp.zeros(shape, jnp.int32)
        for w in range(per_new):
            page = jnp.where(quarter == w, table_ref[i * per_new + w : i * per_new + w + 1, :] + 1, page)
        found = jnp.where(filled == slot, page, found)
    source = jnp.sum(found, axis=1, keepdims=True) - 1
    out_ref[...] = jnp.where(source == iota(out_ref.shape, 1), 1.0, 0.0).astype(BF16)


def sum_kernel(shard_ref, got_hbm, *refs):
    out_refs, (quarters, got_ref, sem) = refs[:-3], refs[-3:]
    terms = got_ref.shape[1]
    load = pltpu.make_async_copy(got_hbm.at[:, got_hbm.shape[1] - terms :, :], got_ref, sem)
    load.start()
    load.wait()
    s = shard_ref[0]
    count = len(out_refs)
    heads = count
    columns = got_ref.shape[0] // EXPERTS
    got = got_ref[...].astype(F32)
    per = got.shape[1] // 2
    for z in range(columns // heads):
        total = jnp.zeros(got.shape[1:], F32)
        for e in range(EXPERTS):
            at = e * columns + z * heads
            total = total + jnp.sum(got[at : at + heads], axis=0)
        for i in range(2):
            quarters[2 * z + i] = total[i * per : (i + 1) * per]
    for t, out_ref in enumerate(out_refs):
        quarter = quarters[lax.rem(s + t, count)]
        for i in range(per):
            out_ref[:, i * HD : (i + 1) * HD] = quarter[i : i + 1, :]


def land_kernel(got_hbm, page_hbm, got_ref, page_ref, sems, *, base):
    rows, width, _ = got_ref.shape
    tiles = page_ref.shape[2] // HD
    local = width // tiles
    n = rows * local
    load = pltpu.make_async_copy(
        got_hbm.at[base : base + rows, 0:width, :], got_ref, sems.at[0]
    )
    load.start()
    to = iota((n, n), 0)
    fro = iota((n, n), 1)
    perm = (over(to, rows) == rest(fro, local)) & (rest(to, rows) == over(fro, local))
    perm = jnp.where(perm, 1.0, 0.0).astype(BF16)
    load.wait()
    flat = jnp.concatenate(
        [got_ref[:, t * local : (t + 1) * local, :].reshape(n, HD) for t in range(tiles)], axis=1
    )
    page_ref[...] = dot(perm, flat).reshape(page_ref.shape).astype(BF16)
    store = pltpu.make_async_copy(page_ref, page_hbm, sems.at[1])
    store.start()
    store.wait()


def shards(
    old_keys,
    old_values,
    keep_lists,
    drop_weights,
    request_pages,
    page_table,
    new_table,
    queries,
    new_keys,
    new_values,
    expert_ids,
    router_logits,
    out_weight,
):
    devices = lax.axis_size("pages")
    shard_count = lax.axis_size("expert")
    my = lax.axis_index("pages").astype(jnp.int32)
    slots, page_len, width = old_keys.shape
    rows = keep_lists.shape[1] + 1
    per_new = page_len // rows
    requests, max_pages = page_table.shape
    new_cap = 2 * (slots // per_new)
    local = new_cap * per_new
    heads = width // HD
    topk = queries.shape[1]
    lines = 2 * slots
    columns = devices // EXPERTS
    head = lax.rem(my, heads)
    shard = lax.axis_index("expert").astype(jnp.int32).reshape(1)
    table = page_table.T
    counts = request_pages.reshape(1, -1)

    outbox = pl.pallas_call(
        source_kernel,
        out_shape=jax.ShapeDtypeStruct((devices, lines + heads * slots, HD), BF16),
        in_specs=[SMEM] + [VMEM] * 5 + [ANY] * 2 + [VMEM] * 4,
        out_specs=ANY,
        scratch_shapes=[
            pltpu.VMEM((slots * rows, width), BF16),
            pltpu.VMEM((slots * rows, width), BF16),
            pltpu.VMEM((slots, HD), F32),
            pltpu.VMEM((requests, topk, width), F32),
            pltpu.VMEM((slots, page_len, width), BF16),
            pltpu.VMEM((slots, page_len, width), BF16),
            pltpu.VMEM((devices, heads * slots, HD), BF16),
            pltpu.VMEM((devices, lines, HD), BF16),
            pltpu.VMEM((slots, rows, page_len), BF16),
            pltpu.SemaphoreType.DMA((4,)),
        ],
        name="source",
    )(
        my.reshape(1),
        table,
        counts,
        expert_ids.T,
        keep_lists,
        drop_weights,
        old_keys,
        old_values,
        queries,
        new_keys,
        new_values,
        router_logits,
    )
    inbox = lax.all_to_all(outbox, "pages", split_axis=0, concat_axis=0, tiled=True)

    weight, _ = lax.optimization_barrier((out_weight[0], outbox))
    pieces = [lax.dynamic_slice_in_dim(weight, (head ^ d) * HD, HD, 0) for d in range(1, heads)]
    weights = [
        lax.ppermute(piece, "pages", [(p, p ^ d) for p in range(devices)])
        for d, piece in enumerate(pieces, 1)
    ]
    pick = pl.pallas_call(
        route_kernel,
        out_shape=jax.ShapeDtypeStruct((devices * local, devices * slots), BF16),
        in_specs=[VMEM] * 3,
        out_specs=VMEM,
        compiler_params=PARAMS,
        name="route",
    )(new_table.T, table, counts)
    inbox, pick, weights = lax.optimization_barrier((inbox, pick, weights))

    block_cols = out_weight.shape[2]
    terms = heads * block_cols // HD
    routed = pl.pallas_call(
        middle_kernel,
        out_shape=jax.ShapeDtypeStruct((devices, heads * local + terms, HD), BF16),
        in_specs=[SMEM] + [ANY] * (2 + heads),
        out_specs=ANY,
        scratch_shapes=[
            pltpu.VMEM((requests, lines, HD), F32),
            pltpu.VMEM((requests, terms, HD), F32),
            pltpu.VMEM((heads, HD, block_cols), BF16),
            pltpu.VMEM((devices, lines, HD), BF16),
            pltpu.VMEM((devices, heads * slots, HD), BF16),
            pltpu.VMEM((devices * local, devices * slots), BF16),
            pltpu.VMEM((devices, heads * local + terms, HD), BF16),
            pltpu.SemaphoreType.DMA((heads + 3,)),
            pltpu.SemaphoreType.DMA((devices // 16,)),
        ],
        compiler_params=PARAMS,
        name="middle",
    )(head.reshape(1), inbox, pick, out_weight, *weights)
    landed = lax.all_to_all(routed, "pages", split_axis=0, concat_axis=0, tiled=True)

    quarters = pl.pallas_call(
        sum_kernel,
        out_shape=[jax.ShapeDtypeStruct((1, width), F32)] * shard_count,
        in_specs=[SMEM, ANY],
        out_specs=[VMEM] * shard_count,
        scratch_shapes=[
            pltpu.VMEM((shard_count, width // HD, HD), F32),
            pltpu.VMEM((devices, terms, HD), BF16),
            pltpu.SemaphoreType.DMA(()),
        ],
        compiler_params=PARAMS,
        name="sum",
    )(shard, landed)
    new_page = jax.ShapeDtypeStruct((new_cap, per_new * rows, width), BF16)

    def land(got, base, name):
        return pl.pallas_call(
            functools.partial(land_kernel, base=base),
            out_shape=new_page,
            in_specs=[ANY],
            out_specs=ANY,
            scratch_shapes=[
                pltpu.VMEM((rows, heads * local, HD), BF16),
                pltpu.VMEM(new_page.shape, BF16),
                pltpu.SemaphoreType.DMA((2,)),
            ],
            compiler_params=PARAMS,
            name=name,
        )(got)

    compact_keys = land(landed, 0, "land_keys")
    landed, quarters, _ = lax.optimization_barrier((landed, quarters, compact_keys))
    moved = [quarters[0]]
    for t in range(1, shard_count):
        moved.append(
            lax.ppermute(quarters[t], "expert", [(i, (i + t) % shard_count) for i in range(shard_count)])
        )
    compact_values = land(landed, rows, "land_values")
    mixed = sum(moved[1:], moved[0]).astype(BF16)
    return (compact_keys, compact_values, mixed)


def solution(mesh):
    in_specs = (
        P("pages", None, "expert"),
        P("pages", None, "expert"),
        P("pages", None),
        P("pages", None),
        P(),
        P(),
        P(),
        P(None, None, "expert"),
        P("pages", "expert"),
        P("pages", "expert"),
        P(),
        P("pages", None),
        P("pages", "expert", None),
    )
    out_specs = (P("pages", None, "expert"), P("pages", None, "expert"), P("pages", "expert"))
    return jax.shard_map(shards, mesh=mesh, in_specs=in_specs, out_specs=out_specs, check_vma=False)
```

```python
import functools
import math

import jax
import jax.numpy as jnp
from jax import lax
from jax.experimental import pallas as pl
from jax.experimental.pallas import tpu as pltpu
from jax.sharding import PartitionSpec as P

HD = 128
EXPERTS = 8
NEGATIVE = -1e30
F32 = jnp.float32
BF16 = jnp.bfloat16
VMEM = pl.BlockSpec(memory_space=pltpu.VMEM)
SMEM = pl.BlockSpec(memory_space=pltpu.SMEM)
ANY = pl.BlockSpec(memory_space=pl.ANY)
PARAMS = pltpu.CompilerParams(vmem_limit_bytes=28 << 20)
NT = (((1,), (1,)), ((), ()))


def iota(shape, dim):
    return lax.broadcasted_iota(jnp.int32, shape, dim)


def over(x, n):
    return lax.shift_right_logical(x, n.bit_length() - 1) if n & (n - 1) == 0 else x // n


def rest(x, n):
    return x & (n - 1) if n & (n - 1) == 0 else x % n


def dot(a, b):
    return jnp.dot(a, b, preferred_element_type=F32)


def source_kernel(
    my_ref,
    table_ref,
    count_ref,
    ids_ref,
    keep_ref,
    drop_ref,
    k_ref,
    v_ref,
    q_ref,
    nk_ref,
    nv_ref,
    logit_ref,
    out_ref,
    kb,
    vb,
    keep_rows,
    q_rows,
):
    my = my_ref[0]
    slots, page_len, width = k_ref.shape
    keep_count = keep_ref.shape[1]
    rows = keep_count + 1
    heads = width // HD
    reqs, topk, _ = q_ref.shape
    keep_rows[...] = jnp.full(keep_rows.shape, -1.0, F32)
    keep_rows[:, 0:keep_count] = keep_ref[...].astype(F32)
    keep_columns = keep_rows[...].T[0:rows, :].astype(jnp.int32)
    q_rows[...] = q_ref[...].astype(F32)
    lane = iota((rows, page_len), 1)
    last = iota((rows, page_len), 0) == rows - 1
    for g in range(slots):
        onehot = jnp.where(keep_columns[:, g : g + 1] == lane, 1.0, 0.0)
        kept = jnp.max(onehot, axis=0, keepdims=True)
        coef = jnp.where(kept > 0.0, 0.0, drop_ref[g : g + 1, :].astype(F32))
        total = jnp.sum(coef, axis=1, keepdims=True)
        mat = jnp.where(last, coef, onehot).astype(BF16)
        denom = jnp.where(last[rows - 8 :, 0:1], total, 1.0)
        for ref, blocks in ((k_ref, kb), (v_ref, vb)):
            block = dot(mat, ref[g])
            block = jnp.concatenate([block[: rows - 8], block[rows - 8 :] / denom], axis=0)
            blocks[g * rows : (g + 1) * rows, :] = block.astype(BF16)
    n = slots * rows
    ent = 2 * slots
    ent_row = iota((ent, reqs), 0)
    req_lane = iota((ent, reqs), 1)
    sel = jnp.where((ent_row == slots) & (req_lane == my), 1.0, 0.0)
    in_use = iota(table_ref.shape, 0) < count_ref[...]
    table = jnp.where(in_use, table_ref[...], -1)
    for g in range(slots):
        hit = jnp.where(table == my * slots + g, 1.0, 0.0)
        sel = jnp.where(ent_row == g, jnp.max(hit, axis=0, keepdims=True), sel)
    sel_b = sel.astype(BF16)
    same = lax.dot_general(sel_b, sel_b, NT, preferred_element_type=F32)
    q_lane = over(iota((ent, width), 1), HD)
    pieces = []
    for k in range(topk):
        group_query = dot(sel_b, q_rows[:, k, :].astype(BF16))
        for h in range(heads):
            pieces.append(jnp.where(q_lane == h, group_query, 0.0))
    queries = jnp.concatenate(pieces, axis=0)
    kh = topk * heads
    scale = 1.0 / math.sqrt(HD)
    scores = lax.dot_general(queries.astype(BF16), kb[...], NT, preferred_element_type=F32) * scale
    col = iota((kh * ent, n), 1)
    scores = scores + jnp.where(rest(col, rows) == rows - 1, math.log(page_len - rows + 1), 0.0)
    of_page = jnp.where(over(iota((ent, n), 1), rows) == iota((ent, n), 0), 1.0, 0.0).astype(BF16)
    shared = dot(same.astype(BF16), of_page)
    mask = jnp.concatenate([shared] * kh, axis=0) > 0.5
    scores = jnp.where(mask, scores, NEGATIVE)
    is_own = rest(iota((kh * ent, 1), 0), ent) == slots
    own = jnp.sum(queries * nk_ref[...].astype(F32), axis=1, keepdims=True) * scale
    own = jnp.where(is_own, own, NEGATIVE)
    peak = jnp.maximum(jnp.max(scores, axis=1, keepdims=True), own)
    shift = peak.astype(BF16).astype(F32)
    probs = jnp.where(mask, jnp.exp(scores - shift), 0.0)
    own_prob = jnp.where(is_own, jnp.exp(own - shift), 0.0)
    den = jnp.sum(probs, axis=1, keepdims=True) + own_prob
    num = dot(probs.astype(BF16), vb[...])
    num = num + own_prob.astype(BF16).astype(F32) * nv_ref[...].astype(F32)
    high = den.astype(BF16).astype(F32)
    low = den - high
    er = iota((ent, ent), 0)
    ec = iota((ent, ent), 1)
    before = jnp.sum(jnp.where((ec < er) | (ec == slots), same, 0.0), axis=1, keepdims=True)
    row = ent_row[:, 0:1]
    first = (row == slots) | ((row < slots) & (before < 0.5))
    request = jnp.sum(jnp.where(sel > 0.5, req_lane.astype(F32), 0.0), axis=1, keepdims=True)
    expert = [
        jnp.sum(jnp.where(sel > 0.5, ids_ref[k : k + 1, :].astype(F32), 0.0), axis=1, keepdims=True)
        for k in range(topk)
    ]
    expert_lane = iota((1, EXPERTS), 1).astype(F32)
    logit = [
        jnp.sum(
            jnp.where(expert_lane == expert[k][slots : slots + 1, :], logit_ref[...], 0.0),
            axis=1,
            keepdims=True,
        )
        for k in range(topk)
    ]
    top = logit[0]
    for k in range(1, topk):
        top = jnp.maximum(top, logit[k])
    terms = [jnp.exp(logit[k] - top) for k in range(topk)]
    term_sum = terms[0]
    for k in range(1, topk):
        term_sum = term_sum + terms[k]
    stat_lane = iota((ent, HD), 1)
    by_choice = []
    for k in range(topk):
        gate = jnp.where(row == slots, terms[k] / term_sum, 0.0)
        gate_high = gate.astype(BF16).astype(F32)
        stats = jnp.where(stat_lane == 3 * heads, gate_high, 0.0)
        stats = jnp.where(stat_lane == 3 * heads + 1, gate - gate_high, stats)
        stats = jnp.where(stat_lane == 3 * heads + 2, request, stats)
        lanes = []
        for h in range(heads):
            at = slice((k * heads + h) * ent, (k * heads + h + 1) * ent)
            lanes.append(num[at, h * HD : (h + 1) * HD])
            for i, stat in enumerate((shift, high, low)):
                stats = jnp.where(stat_lane == 3 * h + i, stat[at, :], stats)
        by_choice.append(jnp.concatenate(lanes + [stats], axis=1))
    parts = []
    for e in range(EXPERTS):
        part = jnp.zeros(by_choice[0].shape, F32)
        for k in range(topk):
            part = jnp.where(first & (expert[k] == e), by_choice[k], part)
        parts.append(part)
    entries = jnp.concatenate(parts, axis=0)
    stats = entries[:, width:].astype(BF16)
    devices = out_ref.shape[0]
    lines = out_ref.shape[1] - heads * slots
    columns = devices // EXPERTS
    to = iota((EXPERTS * lines, EXPERTS * ent), 0)
    fro = iota((EXPERTS * lines, EXPERTS * ent), 1)
    flat = (over(to, lines) == over(fro, ent)) & (rest(to, lines) == slots + 1)
    flat = jnp.where(flat, 1.0, 0.0).astype(BF16)
    square = iota((HD, HD), 0)
    item = iota((HD, HD), 1) % 6
    mine = iota((EXPERTS * ent, HD), 1) // 6 == rest(iota((EXPERTS * ent, HD), 0), ent)
    for h in range(heads):
        origin = jnp.where(item < 3, 3 * h + item, 3 * heads + item - 3)
        spread = dot(stats, jnp.where(square == origin, 1.0, 0.0).astype(BF16))
        line = dot(flat, jnp.where(mine, spread, 0.0).astype(BF16))
        sent = (entries[:, h * HD : (h + 1) * HD] + line).astype(BF16)
        for e in range(EXPERTS):
            for z in range(columns // heads):
                out_ref[e * columns + z * heads + h, 0:lines, :] = sent[e * lines : (e + 1) * lines, :]
    to = iota((n, n), 0)
    fro = iota((n, n), 1)
    perm = jnp.where((rest(to, slots) == over(fro, rows)) & (over(to, slots) == rest(fro, rows)), 1.0, 0.0).astype(BF16)
    for base, blocks in ((0, kb), (rows, vb)):
        spread = dot(perm, blocks[...])
        for t in range(heads):
            at = slice(lines + t * slots, lines + (t + 1) * slots)
            out_ref[base : base + rows, at, :] = (
                spread[:, t * HD : (t + 1) * HD].reshape(rows, slots, HD).astype(BF16)
            )


def middle_kernel(head_ref, got_ref, pick_ref, *refs):
    w_refs, (out_hbm, scr, terms, stack, out_ref, out_sems) = refs[:-6], refs[-6:]
    heads = len(w_refs)
    head = head_ref[0]
    reqs, lines, _ = scr.shape
    slots = lines // 2
    depth = stack.shape[1]
    stack[0] = w_refs[0][0, pl.ds(head * depth, depth), :]
    for d in range(1, heads):
        stack[d] = w_refs[d][...]
    scr[...] = got_ref[:, 0:lines, :].astype(F32)
    stats = scr[:, slots + 1, :]
    stats = jnp.concatenate([stats, stats], axis=0).T
    left = iota((1, 2 * reqs), 1) < reqs
    target = iota((reqs, 2 * reqs), 0).astype(F32)

    def item(g, i):
        first = stats[6 * g + i : 6 * g + i + 1, :]
        if g == slots:
            return jnp.where(left, first, 0.0)
        return jnp.where(left, first, stats[6 * g + 6 + i : 6 * g + 7 + i, :])

    groups = range(0, slots + 1, 2)
    picks = [(item(g, 5) == target) & (item(g, 1) > 0.0) for g in groups]
    gate = jnp.zeros(target.shape, F32)
    peak = jnp.full(target.shape, NEGATIVE, F32)
    for g, pick in zip(groups, picks):
        gate = gate + jnp.where(pick, item(g, 3) + item(g, 4), 0.0)
        peak = jnp.maximum(peak, jnp.where(pick, item(g, 0), NEGATIVE))
    gate = jnp.sum(gate, axis=1, keepdims=True)
    peak = jnp.max(peak, axis=1, keepdims=True)
    den = jnp.zeros(target.shape, F32)
    num = jnp.zeros((2 * reqs, HD), F32)
    for g, pick in zip(groups, picks):
        factor = jnp.where(pick, jnp.exp(item(g, 0) - peak), 0.0)
        den = den + factor * (item(g, 1) + item(g, 2))
        high = factor.astype(BF16)
        low = (factor - high.astype(F32)).astype(BF16)
        entries = jnp.concatenate([scr[:, g, :], scr[:, min(g + 1, slots), :]], axis=0).astype(BF16)
        num = num + dot(jnp.concatenate([high, low], axis=0), entries)
    den = jnp.sum(den, axis=1, keepdims=True)
    some = den > 0.0
    value = (num[:reqs] + num[reqs:]) / jnp.where(some, den, 1.0)
    weighted = jnp.where(some, gate * value, 0.0).astype(BF16)
    tiles = stack.shape[2] // HD
    for b in range(heads):
        part = dot(weighted, stack[b ^ head])
        for t in range(tiles):
            terms[:, b * tiles + t, :] = part[:, t * HD : (t + 1) * HD]
    terms_at = out_ref.shape[1] - heads * tiles
    out_ref[:, terms_at:, :] = terms[...].astype(BF16)
    held = reqs * slots
    local = pick_ref.shape[0] // reqs
    table = jnp.concatenate(
        [
            got_ref[:, lines + t * slots : lines + (t + 1) * slots, :]
            .astype(F32)
            .reshape(held, HD)
            .astype(BF16)
            for t in range(terms_at // local)
        ],
        axis=1,
    )
    step = 16
    stores = []
    for c in range(0, reqs, step):
        rows = dot(pick_ref[c * local : (c + step) * local, :], table)
        for t in range(terms_at // local):
            out_ref[c : c + step, t * local : (t + 1) * local, :] = (
                rows[:, t * HD : (t + 1) * HD].reshape(step, local, HD).astype(BF16)
            )
        at = pl.ds(c, step)
        stores.append(pltpu.make_async_copy(out_ref.at[at], out_hbm.at[at], out_sems.at[c // step]))
        stores[-1].start()
    for store in stores:
        store.wait()


def route_kernel(new_ref, table_ref, count_ref, out_ref):
    max_new = new_ref.shape[0]
    per_new = table_ref.shape[0] // max_new
    shape = (out_ref.shape[0], new_ref.shape[1])
    slot = over(iota(shape, 0), per_new)
    quarter = rest(iota(shape, 0), per_new)
    found = jnp.zeros(shape, jnp.int32)
    for i in range(max_new):
        filled = jnp.where(i * per_new < count_ref[...], new_ref[i : i + 1, :], -1)
        page = jnp.zeros(shape, jnp.int32)
        for w in range(per_new):
            page = jnp.where(quarter == w, table_ref[i * per_new + w : i * per_new + w + 1, :] + 1, page)
        found = jnp.where(filled == slot, page, found)
    source = jnp.sum(found, axis=1, keepdims=True) - 1
    out_ref[...] = jnp.where(source == iota(out_ref.shape, 1), 1.0, 0.0).astype(BF16)


def sum_kernel(shard_ref, got_ref, keep_ref, send_ref, quarters, *, lines):
    mine = lax.shift_right_logical(shard_ref[0], 1)
    columns = got_ref.shape[0] // EXPERTS
    got = got_ref[:, got_ref.shape[1] - lines :, :].astype(F32)
    heads = columns // 2
    per = lines // 2
    for z in range(2):
        total = jnp.zeros(got.shape[1:], F32)
        for e in range(EXPERTS):
            at = e * columns + z * heads
            total = total + jnp.sum(got[at : at + heads], axis=0)
        quarters[z] = total
    for ref, half in ((keep_ref, quarters[mine]), (send_ref, quarters[1 - mine])):
        for i in range(2):
            for t in range(per):
                ref[i : i + 1, t * HD : (t + 1) * HD] = half[i * per + t : i * per + t + 1, :]


def halve_kernel(shard_ref, here_ref, came_ref, keep_ref, send_ref, total):
    mine = shard_ref[0] & 1
    total[...] = here_ref[...] + came_ref[...]
    keep_ref[...] = total[pl.ds(mine, 1), :]
    send_ref[...] = total[pl.ds(1 - mine, 1), :]


def land_kernel(got_ref, page_ref, *, base):
    tiles = page_ref.shape[2] // HD
    rows = got_ref.shape[0] // 2
    n = page_ref.shape[0] * page_ref.shape[1]
    local = n // rows
    to = iota((n, n), 0)
    fro = iota((n, n), 1)
    perm = (over(to, rows) == rest(fro, local)) & (rest(to, rows) == over(fro, local))
    perm = jnp.where(perm, 1.0, 0.0).astype(BF16)
    flat = jnp.concatenate(
        [
            got_ref[base : base + rows, t * local : (t + 1) * local, :].reshape(n, HD)
            for t in range(tiles)
        ],
        axis=1,
    )
    page_ref[...] = dot(perm, flat).reshape(page_ref.shape).astype(BF16)


def shards(
    old_keys,
    old_values,
    keep_lists,
    drop_weights,
    request_pages,
    page_table,
    new_table,
    queries,
    new_keys,
    new_values,
    expert_ids,
    router_logits,
    out_weight,
):
    devices = lax.axis_size("pages")
    shard_count = lax.axis_size("expert")
    my = lax.axis_index("pages").astype(jnp.int32)
    slots, page_len, width = old_keys.shape
    rows = keep_lists.shape[1] + 1
    per_new = page_len // rows
    requests, max_pages = page_table.shape
    new_cap = 2 * (slots // per_new)
    local = new_cap * per_new
    heads = width // HD
    topk = queries.shape[1]
    lines = 2 * slots
    columns = devices // EXPERTS
    head = lax.rem(my, heads)
    shard = lax.axis_index("expert").astype(jnp.int32).reshape(1)
    table = page_table.T
    counts = request_pages.reshape(1, -1)

    outbox = pl.pallas_call(
        source_kernel,
        out_shape=jax.ShapeDtypeStruct((devices, lines + heads * slots, HD), BF16),
        in_specs=[SMEM] + [VMEM] * 11,
        out_specs=VMEM,
        scratch_shapes=[
            pltpu.VMEM((slots * rows, width), BF16),
            pltpu.VMEM((slots * rows, width), BF16),
            pltpu.VMEM((slots, HD), F32),
            pltpu.VMEM((requests, topk, width), F32),
        ],
        name="source",
    )(
        my.reshape(1),
        table,
        counts,
        expert_ids.T,
        keep_lists,
        drop_weights,
        old_keys,
        old_values,
        queries,
        new_keys,
        new_values,
        router_logits,
    )
    inbox = lax.all_to_all(outbox, "pages", split_axis=0, concat_axis=0, tiled=True)

    weight, _ = lax.optimization_barrier((out_weight[0], outbox))
    pieces = [lax.dynamic_slice_in_dim(weight, (head ^ d) * HD, HD, 0) for d in range(1, heads)]
    weights = [
        lax.ppermute(piece, "pages", [(p, p ^ d) for p in range(devices)])
        for d, piece in enumerate(pieces, 1)
    ]
    pick = pl.pallas_call(
        route_kernel,
        out_shape=jax.ShapeDtypeStruct((devices * local, devices * slots), BF16),
        in_specs=[VMEM] * 3,
        out_specs=VMEM,
        compiler_params=PARAMS,
        name="route",
    )(new_table.T, table, counts)
    inbox, pick, weights = lax.optimization_barrier((inbox, pick, weights))

    block_cols = out_weight.shape[2]
    terms = heads * block_cols // HD
    routed = pl.pallas_call(
        middle_kernel,
        out_shape=jax.ShapeDtypeStruct((devices, heads * local + terms, HD), BF16),
        in_specs=[SMEM] + [VMEM] * (2 + heads),
        out_specs=ANY,
        scratch_shapes=[
            pltpu.VMEM((requests, lines, HD), F32),
            pltpu.VMEM((requests, terms, HD), F32),
            pltpu.VMEM((heads, HD, block_cols), BF16),
            pltpu.VMEM((devices, heads * local + terms, HD), BF16),
            pltpu.SemaphoreType.DMA((devices // 16,)),
        ],
        compiler_params=PARAMS,
        name="middle",
    )(head.reshape(1), inbox, pick, out_weight, *weights)
    landed = lax.all_to_all(routed, "pages", split_axis=0, concat_axis=0, tiled=True)

    def swap(array, bit):
        return lax.ppermute(array, "expert", [(i, i ^ bit) for i in range(shard_count)])

    def land(got, base, name):
        return pl.pallas_call(
            functools.partial(land_kernel, base=base),
            out_shape=jax.ShapeDtypeStruct((new_cap, per_new * rows, width), BF16),
            in_specs=[VMEM],
            out_specs=VMEM,
            compiler_params=PARAMS,
            name=name,
        )(got)

    here, there = pl.pallas_call(
        functools.partial(sum_kernel, lines=terms),
        out_shape=[jax.ShapeDtypeStruct((2, width), F32)] * 2,
        in_specs=[SMEM, VMEM],
        out_specs=[VMEM] * 2,
        scratch_shapes=[pltpu.VMEM((2, terms, HD), F32)],
        compiler_params=PARAMS,
        name="sum",
    )(shard, landed)
    came = swap(there, 2)
    landed, _ = lax.optimization_barrier((landed, there))
    compact_keys = land(landed, 0, "land_keys")
    came, _ = lax.optimization_barrier((came, compact_keys))
    here, there = pl.pallas_call(
        halve_kernel,
        out_shape=[jax.ShapeDtypeStruct((1, width), F32)] * 2,
        in_specs=[SMEM, VMEM, VMEM],
        out_specs=[VMEM] * 2,
        scratch_shapes=[pltpu.VMEM((2, width), F32)],
        compiler_params=PARAMS,
        name="halve",
    )(shard, here, came)
    came = swap(there, 1)
    landed, _ = lax.optimization_barrier((landed, there))
    compact_values = land(landed, rows, "land_values")
    mixed = (here + came).astype(BF16)
    return (compact_keys, compact_values, mixed)


def solution(mesh):
    in_specs = (
        P("pages", None, "expert"),
        P("pages", None, "expert"),
        P("pages", None),
        P("pages", None),
        P(),
        P(),
        P(),
        P(None, None, "expert"),
        P("pages", "expert"),
        P("pages", "expert"),
        P(),
        P("pages", None),
        P("pages", "expert", None),
    )
    out_specs = (P("pages", None, "expert"), P("pages", None, "expert"), P("pages", "expert"))
    return jax.shard_map(shards, mesh=mesh, in_specs=in_specs, out_specs=out_specs, check_vma=False)
```

```python
import functools
import math

import jax
import jax.numpy as jnp
from jax import lax
from jax.experimental import pallas as pl
from jax.experimental.pallas import tpu as pltpu
from jax.sharding import PartitionSpec as P

HD = 128
EXPERTS = 8
NEGATIVE = -1e30
F32 = jnp.float32
BF16 = jnp.bfloat16
VMEM = pl.BlockSpec(memory_space=pltpu.VMEM)
SMEM = pl.BlockSpec(memory_space=pltpu.SMEM)
ANY = pl.BlockSpec(memory_space=pl.ANY)
PARAMS = pltpu.CompilerParams(vmem_limit_bytes=28 << 20)
NT = (((1,), (1,)), ((), ()))


def iota(shape, dim):
    return lax.broadcasted_iota(jnp.int32, shape, dim)


def over(x, n):
    return lax.shift_right_logical(x, n.bit_length() - 1) if n & (n - 1) == 0 else x // n


def rest(x, n):
    return x & (n - 1) if n & (n - 1) == 0 else x % n


def dot(a, b):
    return jnp.dot(a, b, preferred_element_type=F32)


def source_kernel(
    my_ref,
    table_ref,
    count_ref,
    ids_ref,
    keep_ref,
    drop_ref,
    k_ref,
    v_ref,
    q_ref,
    nk_ref,
    nv_ref,
    logit_ref,
    out_ref,
    kb,
    vb,
    keep_rows,
    q_rows,
):
    my = my_ref[0]
    slots, page_len, width = k_ref.shape
    keep_count = keep_ref.shape[1]
    rows = keep_count + 1
    heads = width // HD
    reqs, topk, _ = q_ref.shape
    keep_rows[...] = jnp.full(keep_rows.shape, -1.0, F32)
    keep_rows[:, 0:keep_count] = keep_ref[...].astype(F32)
    keep_columns = keep_rows[...].T[0:rows, :].astype(jnp.int32)
    q_rows[...] = q_ref[...].astype(F32)
    lane = iota((rows, page_len), 1)
    last = iota((rows, page_len), 0) == rows - 1
    for g in range(slots):
        onehot = jnp.where(keep_columns[:, g : g + 1] == lane, 1.0, 0.0)
        kept = jnp.max(onehot, axis=0, keepdims=True)
        coef = jnp.where(kept > 0.0, 0.0, drop_ref[g : g + 1, :].astype(F32))
        total = jnp.sum(coef, axis=1, keepdims=True)
        mat = jnp.where(last, coef, onehot).astype(BF16)
        denom = jnp.where(last[rows - 8 :, 0:1], total, 1.0)
        for ref, blocks in ((k_ref, kb), (v_ref, vb)):
            block = dot(mat, ref[g])
            block = jnp.concatenate([block[: rows - 8], block[rows - 8 :] / denom], axis=0)
            blocks[g * rows : (g + 1) * rows, :] = block.astype(BF16)
    n = slots * rows
    ent = 2 * slots
    ent_row = iota((ent, reqs), 0)
    req_lane = iota((ent, reqs), 1)
    sel = jnp.where((ent_row == slots) & (req_lane == my), 1.0, 0.0)
    in_use = iota(table_ref.shape, 0) < count_ref[...]
    table = jnp.where(in_use, table_ref[...], -1)
    for g in range(slots):
        hit = jnp.where(table == my * slots + g, 1.0, 0.0)
        sel = jnp.where(ent_row == g, jnp.max(hit, axis=0, keepdims=True), sel)
    sel_b = sel.astype(BF16)
    same = lax.dot_general(sel_b, sel_b, NT, preferred_element_type=F32)
    q_lane = over(iota((ent, width), 1), HD)
    pieces = []
    for k in range(topk):
        group_query = dot(sel_b, q_rows[:, k, :].astype(BF16))
        for h in range(heads):
            pieces.append(jnp.where(q_lane == h, group_query, 0.0))
    queries = jnp.concatenate(pieces, axis=0)
    kh = topk * heads
    scale = 1.0 / math.sqrt(HD)
    scores = lax.dot_general(queries.astype(BF16), kb[...], NT, preferred_element_type=F32) * scale
    col = iota((kh * ent, n), 1)
    scores = scores + jnp.where(rest(col, rows) == rows - 1, math.log(page_len - rows + 1), 0.0)
    of_page = jnp.where(over(iota((ent, n), 1), rows) == iota((ent, n), 0), 1.0, 0.0).astype(BF16)
    shared = dot(same.astype(BF16), of_page)
    mask = jnp.concatenate([shared] * kh, axis=0) > 0.5
    scores = jnp.where(mask, scores, NEGATIVE)
    is_own = rest(iota((kh * ent, 1), 0), ent) == slots
    own = jnp.sum(queries * nk_ref[...].astype(F32), axis=1, keepdims=True) * scale
    own = jnp.where(is_own, own, NEGATIVE)
    peak = jnp.maximum(jnp.max(scores, axis=1, keepdims=True), own)
    shift = peak.astype(BF16).astype(F32)
    probs = jnp.where(mask, jnp.exp(scores - shift), 0.0)
    own_prob = jnp.where(is_own, jnp.exp(own - shift), 0.0)
    den = jnp.sum(probs, axis=1, keepdims=True) + own_prob
    num = dot(probs.astype(BF16), vb[...])
    num = num + own_prob.astype(BF16).astype(F32) * nv_ref[...].astype(F32)
    high = den.astype(BF16).astype(F32)
    low = den - high
    er = iota((ent, ent), 0)
    ec = iota((ent, ent), 1)
    before = jnp.sum(jnp.where((ec < er) | (ec == slots), same, 0.0), axis=1, keepdims=True)
    row = ent_row[:, 0:1]
    first = (row == slots) | ((row < slots) & (before < 0.5))
    request = jnp.sum(jnp.where(sel > 0.5, req_lane.astype(F32), 0.0), axis=1, keepdims=True)
    expert = [
        jnp.sum(jnp.where(sel > 0.5, ids_ref[k : k + 1, :].astype(F32), 0.0), axis=1, keepdims=True)
        for k in range(topk)
    ]
    expert_lane = iota((1, EXPERTS), 1).astype(F32)
    logit = [
        jnp.sum(
            jnp.where(expert_lane == expert[k][slots : slots + 1, :], logit_ref[...], 0.0),
            axis=1,
            keepdims=True,
        )
        for k in range(topk)
    ]
    top = logit[0]
    for k in range(1, topk):
        top = jnp.maximum(top, logit[k])
    terms = [jnp.exp(logit[k] - top) for k in range(topk)]
    term_sum = terms[0]
    for k in range(1, topk):
        term_sum = term_sum + terms[k]
    stat_lane = iota((ent, HD), 1)
    by_choice = []
    for k in range(topk):
        gate = jnp.where(row == slots, terms[k] / term_sum, 0.0)
        gate_high = gate.astype(BF16).astype(F32)
        stats = jnp.where(stat_lane == 3 * heads, gate_high, 0.0)
        stats = jnp.where(stat_lane == 3 * heads + 1, gate - gate_high, stats)
        stats = jnp.where(stat_lane == 3 * heads + 2, request, stats)
        lanes = []
        for h in range(heads):
            at = slice((k * heads + h) * ent, (k * heads + h + 1) * ent)
            lanes.append(num[at, h * HD : (h + 1) * HD])
            for i, stat in enumerate((shift, high, low)):
                stats = jnp.where(stat_lane == 3 * h + i, stat[at, :], stats)
        by_choice.append(jnp.concatenate(lanes + [stats], axis=1))
    parts = []
    for e in range(EXPERTS):
        part = jnp.zeros(by_choice[0].shape, F32)
        for k in range(topk):
            part = jnp.where(first & (expert[k] == e), by_choice[k], part)
        parts.append(part)
    entries = jnp.concatenate(parts, axis=0)
    stats = entries[:, width:].astype(BF16)
    devices = out_ref.shape[0]
    lines = out_ref.shape[1] - heads * slots
    columns = devices // EXPERTS
    to = iota((EXPERTS * lines, EXPERTS * ent), 0)
    fro = iota((EXPERTS * lines, EXPERTS * ent), 1)
    flat = (over(to, lines) == over(fro, ent)) & (rest(to, lines) == slots + 1)
    flat = jnp.where(flat, 1.0, 0.0).astype(BF16)
    square = iota((HD, HD), 0)
    item = iota((HD, HD), 1) % 6
    mine = iota((EXPERTS * ent, HD), 1) // 6 == rest(iota((EXPERTS * ent, HD), 0), ent)
    for h in range(heads):
        origin = jnp.where(item < 3, 3 * h + item, 3 * heads + item - 3)
        spread = dot(stats, jnp.where(square == origin, 1.0, 0.0).astype(BF16))
        line = dot(flat, jnp.where(mine, spread, 0.0).astype(BF16))
        sent = (entries[:, h * HD : (h + 1) * HD] + line).astype(BF16)
        for e in range(EXPERTS):
            for z in range(columns // heads):
                out_ref[e * columns + z * heads + h, 0:lines, :] = sent[e * lines : (e + 1) * lines, :]
    to = iota((n, n), 0)
    fro = iota((n, n), 1)
    perm = jnp.where((rest(to, slots) == over(fro, rows)) & (over(to, slots) == rest(fro, rows)), 1.0, 0.0).astype(BF16)
    for base, blocks in ((0, kb), (rows, vb)):
        spread = dot(perm, blocks[...])
        for t in range(heads):
            at = slice(lines + t * slots, lines + (t + 1) * slots)
            out_ref[base : base + rows, at, :] = (
                spread[:, t * HD : (t + 1) * HD].reshape(rows, slots, HD).astype(BF16)
            )


def middle_kernel(head_ref, got_ref, pick_ref, *refs):
    w_refs, (out_hbm, scr, terms, stack, out_ref, out_sems) = refs[:-6], refs[-6:]
    heads = len(w_refs)
    head = head_ref[0]
    reqs, lines, _ = scr.shape
    slots = lines // 2
    depth = stack.shape[1]
    stack[0] = w_refs[0][0, pl.ds(head * depth, depth), :]
    for d in range(1, heads):
        stack[d] = w_refs[d][...]
    scr[...] = got_ref[:, 0:lines, :].astype(F32)
    stats = scr[:, slots + 1, :]
    stats = jnp.concatenate([stats, stats], axis=0).T
    left = iota((1, 2 * reqs), 1) < reqs
    target = iota((reqs, 2 * reqs), 0).astype(F32)

    def item(g, i):
        first = stats[6 * g + i : 6 * g + i + 1, :]
        if g == slots:
            return jnp.where(left, first, 0.0)
        return jnp.where(left, first, stats[6 * g + 6 + i : 6 * g + 7 + i, :])

    groups = range(0, slots + 1, 2)
    picks = [(item(g, 5) == target) & (item(g, 1) > 0.0) for g in groups]
    gate = jnp.zeros(target.shape, F32)
    peak = jnp.full(target.shape, NEGATIVE, F32)
    for g, pick in zip(groups, picks):
        gate = gate + jnp.where(pick, item(g, 3) + item(g, 4), 0.0)
        peak = jnp.maximum(peak, jnp.where(pick, item(g, 0), NEGATIVE))
    gate = jnp.sum(gate, axis=1, keepdims=True)
    peak = jnp.max(peak, axis=1, keepdims=True)
    den = jnp.zeros(target.shape, F32)
    num = jnp.zeros((2 * reqs, HD), F32)
    for g, pick in zip(groups, picks):
        factor = jnp.where(pick, jnp.exp(item(g, 0) - peak), 0.0)
        den = den + factor * (item(g, 1) + item(g, 2))
        high = factor.astype(BF16)
        low = (factor - high.astype(F32)).astype(BF16)
        entries = jnp.concatenate([scr[:, g, :], scr[:, min(g + 1, slots), :]], axis=0).astype(BF16)
        num = num + dot(jnp.concatenate([high, low], axis=0), entries)
    den = jnp.sum(den, axis=1, keepdims=True)
    some = den > 0.0
    value = (num[:reqs] + num[reqs:]) / jnp.where(some, den, 1.0)
    weighted = jnp.where(some, gate * value, 0.0).astype(BF16)
    tiles = stack.shape[2] // HD
    for b in range(heads):
        part = dot(weighted, stack[b ^ head])
        for t in range(tiles):
            terms[:, b * tiles + t, :] = part[:, t * HD : (t + 1) * HD]
    terms_at = out_ref.shape[1] - heads * tiles
    out_ref[:, terms_at:, :] = terms[...].astype(BF16)
    held = reqs * slots
    local = pick_ref.shape[0] // reqs
    table = jnp.concatenate(
        [
            got_ref[:, lines + t * slots : lines + (t + 1) * slots, :]
            .astype(F32)
            .reshape(held, HD)
            .astype(BF16)
            for t in range(terms_at // local)
        ],
        axis=1,
    )
    step = 16
    stores = []
    for c in range(0, reqs, step):
        rows = dot(pick_ref[c * local : (c + step) * local, :], table)
        for t in range(terms_at // local):
            out_ref[c : c + step, t * local : (t + 1) * local, :] = (
                rows[:, t * HD : (t + 1) * HD].reshape(step, local, HD).astype(BF16)
            )
        at = pl.ds(c, step)
        stores.append(pltpu.make_async_copy(out_ref.at[at], out_hbm.at[at], out_sems.at[c // step]))
        stores[-1].start()
    for store in stores:
        store.wait()


def route_kernel(new_ref, table_ref, count_ref, out_ref):
    max_new = new_ref.shape[0]
    per_new = table_ref.shape[0] // max_new
    shape = (out_ref.shape[0], new_ref.shape[1])
    slot = over(iota(shape, 0), per_new)
    quarter = rest(iota(shape, 0), per_new)
    found = jnp.zeros(shape, jnp.int32)
    for i in range(max_new):
        filled = jnp.where(i * per_new < count_ref[...], new_ref[i : i + 1, :], -1)
        page = jnp.zeros(shape, jnp.int32)
        for w in range(per_new):
            page = jnp.where(quarter == w, table_ref[i * per_new + w : i * per_new + w + 1, :] + 1, page)
        found = jnp.where(filled == slot, page, found)
    source = jnp.sum(found, axis=1, keepdims=True) - 1
    out_ref[...] = jnp.where(source == iota(out_ref.shape, 1), 1.0, 0.0).astype(BF16)


def sum_kernel(shard_ref, got_ref, *refs, lines):
    out_refs, (quarters,) = refs[:-1], refs[-1:]
    s = shard_ref[0]
    columns = got_ref.shape[0] // EXPERTS
    got = got_ref[:, got_ref.shape[1] - lines :, :].astype(F32)
    heads = columns // 2
    per = lines // 2
    for z in range(2):
        total = jnp.zeros(got.shape[1:], F32)
        for e in range(EXPERTS):
            at = e * columns + z * heads
            total = total + jnp.sum(got[at : at + heads], axis=0)
        for i in range(2):
            quarters[2 * z + i] = total[i * per : (i + 1) * per]
    for t, out_ref in enumerate(out_refs):
        quarter = quarters[s ^ t]
        for i in range(per):
            out_ref[:, i * HD : (i + 1) * HD] = quarter[i : i + 1, :]


def land_kernel(got_ref, k_hbm, v_hbm, k_ref, v_ref, sems):
    tiles = k_ref.shape[2] // HD
    rows = got_ref.shape[0] // 2
    n = k_ref.shape[0] * k_ref.shape[1]
    local = n // rows
    to = iota((n, n), 0)
    fro = iota((n, n), 1)
    perm = (over(to, rows) == rest(fro, local)) & (rest(to, rows) == over(fro, local))
    perm = jnp.where(perm, 1.0, 0.0).astype(BF16)
    stores = []
    for i, (ref, hbm) in enumerate(((k_ref, k_hbm), (v_ref, v_hbm))):
        flat = jnp.concatenate(
            [
                got_ref[i * rows : (i + 1) * rows, t * local : (t + 1) * local, :].reshape(n, HD)
                for t in range(tiles)
            ],
            axis=1,
        )
        ref[...] = dot(perm, flat).reshape(ref.shape).astype(BF16)
        stores.append(pltpu.make_async_copy(ref, hbm, sems.at[i]))
        stores[i].start()
    for store in stores:
        store.wait()


def shards(
    old_keys,
    old_values,
    keep_lists,
    drop_weights,
    request_pages,
    page_table,
    new_table,
    queries,
    new_keys,
    new_values,
    expert_ids,
    router_logits,
    out_weight,
):
    devices = lax.axis_size("pages")
    shard_count = lax.axis_size("expert")
    my = lax.axis_index("pages").astype(jnp.int32)
    slots, page_len, width = old_keys.shape
    rows = keep_lists.shape[1] + 1
    per_new = page_len // rows
    requests, max_pages = page_table.shape
    new_cap = 2 * (slots // per_new)
    local = new_cap * per_new
    heads = width // HD
    topk = queries.shape[1]
    lines = 2 * slots
    columns = devices // EXPERTS
    head = lax.rem(my, heads)
    shard = lax.axis_index("expert").astype(jnp.int32).reshape(1)
    table = page_table.T
    counts = request_pages.reshape(1, -1)

    outbox = pl.pallas_call(
        source_kernel,
        out_shape=jax.ShapeDtypeStruct((devices, lines + heads * slots, HD), BF16),
        in_specs=[SMEM] + [VMEM] * 11,
        out_specs=VMEM,
        scratch_shapes=[
            pltpu.VMEM((slots * rows, width), BF16),
            pltpu.VMEM((slots * rows, width), BF16),
            pltpu.VMEM((slots, HD), F32),
            pltpu.VMEM((requests, topk, width), F32),
        ],
        name="source",
    )(
        my.reshape(1),
        table,
        counts,
        expert_ids.T,
        keep_lists,
        drop_weights,
        old_keys,
        old_values,
        queries,
        new_keys,
        new_values,
        router_logits,
    )
    inbox = lax.all_to_all(outbox, "pages", split_axis=0, concat_axis=0, tiled=True)

    weight, _ = lax.optimization_barrier((out_weight[0], outbox))
    pieces = [lax.dynamic_slice_in_dim(weight, (head ^ d) * HD, HD, 0) for d in range(1, heads)]
    weights = [
        lax.ppermute(piece, "pages", [(p, p ^ d) for p in range(devices)])
        for d, piece in enumerate(pieces, 1)
    ]
    pick = pl.pallas_call(
        route_kernel,
        out_shape=jax.ShapeDtypeStruct((devices * local, devices * slots), BF16),
        in_specs=[VMEM] * 3,
        out_specs=VMEM,
        compiler_params=PARAMS,
        name="route",
    )(new_table.T, table, counts)
    inbox, pick, weights = lax.optimization_barrier((inbox, pick, weights))

    block_cols = out_weight.shape[2]
    terms = heads * block_cols // HD
    routed = pl.pallas_call(
        middle_kernel,
        out_shape=jax.ShapeDtypeStruct((devices, heads * local + terms, HD), BF16),
        in_specs=[SMEM] + [VMEM] * (2 + heads),
        out_specs=ANY,
        scratch_shapes=[
            pltpu.VMEM((requests, lines, HD), F32),
            pltpu.VMEM((requests, terms, HD), F32),
            pltpu.VMEM((heads, HD, block_cols), BF16),
            pltpu.VMEM((devices, heads * local + terms, HD), BF16),
            pltpu.SemaphoreType.DMA((devices // 16,)),
        ],
        compiler_params=PARAMS,
        name="middle",
    )(head.reshape(1), inbox, pick, out_weight, *weights)
    landed = lax.all_to_all(routed, "pages", split_axis=0, concat_axis=0, tiled=True)

    quarters = pl.pallas_call(
        functools.partial(sum_kernel, lines=terms),
        out_shape=[jax.ShapeDtypeStruct((1, width), F32)] * shard_count,
        in_specs=[SMEM, VMEM],
        out_specs=[VMEM] * shard_count,
        scratch_shapes=[pltpu.VMEM((shard_count, width // HD, HD), F32)],
        compiler_params=PARAMS,
        name="sum",
    )(shard, landed)
    landed, quarters = lax.optimization_barrier((landed, quarters))
    moved = [quarters[0]]
    for t in range(1, shard_count):
        moved.append(lax.ppermute(quarters[t], "expert", [(i, i ^ t) for i in range(shard_count)]))
    new_page = jax.ShapeDtypeStruct((new_cap, per_new * rows, width), BF16)
    compact_keys, compact_values = pl.pallas_call(
        land_kernel,
        out_shape=(new_page, new_page),
        in_specs=[VMEM],
        out_specs=(ANY, ANY),
        scratch_shapes=[
            pltpu.VMEM(new_page.shape, BF16),
            pltpu.VMEM(new_page.shape, BF16),
            pltpu.SemaphoreType.DMA((2,)),
        ],
        compiler_params=PARAMS,
        name="land",
    )(landed)
    mixed = sum(moved[1:], moved[0]).astype(BF16)
    return (compact_keys, compact_values, mixed)


def solution(mesh):
    in_specs = (
        P("pages", None, "expert"),
        P("pages", None, "expert"),
        P("pages", None),
        P("pages", None),
        P(),
        P(),
        P(),
        P(None, None, "expert"),
        P("pages", "expert"),
        P("pages", "expert"),
        P(),
        P("pages", None),
        P("pages", "expert", None),
    )
    out_specs = (P("pages", None, "expert"), P("pages", None, "expert"), P("pages", "expert"))
    return jax.shard_map(shards, mesh=mesh, in_specs=in_specs, out_specs=out_specs, check_vma=False)
```

```python
import functools
import math

import jax
import jax.numpy as jnp
from jax import lax
from jax.experimental import pallas as pl
from jax.experimental.pallas import tpu as pltpu
from jax.sharding import PartitionSpec as P

HD = 128
EXPERTS = 8
NEGATIVE = -1e30
F32 = jnp.float32
BF16 = jnp.bfloat16
VMEM = pl.BlockSpec(memory_space=pltpu.VMEM)
SMEM = pl.BlockSpec(memory_space=pltpu.SMEM)
ANY = pl.BlockSpec(memory_space=pl.ANY)
PARAMS = pltpu.CompilerParams(vmem_limit_bytes=28 << 20)
NT = (((1,), (1,)), ((), ()))


def iota(shape, dim):
    return lax.broadcasted_iota(jnp.int32, shape, dim)


def over(x, n):
    return lax.shift_right_logical(x, n.bit_length() - 1) if n & (n - 1) == 0 else x // n


def rest(x, n):
    return x & (n - 1) if n & (n - 1) == 0 else x % n


def dot(a, b):
    return jnp.dot(a, b, preferred_element_type=F32)


def source_kernel(
    my_ref,
    table_ref,
    count_ref,
    ids_ref,
    keep_ref,
    drop_ref,
    k_ref,
    v_ref,
    q_ref,
    nk_ref,
    nv_ref,
    logit_ref,
    out_ref,
    kb,
    vb,
    keep_rows,
    q_rows,
):
    my = my_ref[0]
    slots, page_len, width = k_ref.shape
    keep_count = keep_ref.shape[1]
    rows = keep_count + 1
    heads = width // HD
    reqs, topk, _ = q_ref.shape
    keep_rows[...] = jnp.full(keep_rows.shape, -1.0, F32)
    keep_rows[:, 0:keep_count] = keep_ref[...].astype(F32)
    keep_columns = keep_rows[...].T[0:rows, :].astype(jnp.int32)
    q_rows[...] = q_ref[...].astype(F32)
    lane = iota((rows, page_len), 1)
    last = iota((rows, page_len), 0) == rows - 1
    for g in range(slots):
        onehot = jnp.where(keep_columns[:, g : g + 1] == lane, 1.0, 0.0)
        kept = jnp.max(onehot, axis=0, keepdims=True)
        coef = jnp.where(kept > 0.0, 0.0, drop_ref[g : g + 1, :].astype(F32))
        total = jnp.sum(coef, axis=1, keepdims=True)
        mat = jnp.where(last, coef, onehot).astype(BF16)
        denom = jnp.where(last[rows - 8 :, 0:1], total, 1.0)
        for ref, blocks in ((k_ref, kb), (v_ref, vb)):
            block = dot(mat, ref[g])
            block = jnp.concatenate([block[: rows - 8], block[rows - 8 :] / denom], axis=0)
            blocks[g * rows : (g + 1) * rows, :] = block.astype(BF16)
    n = slots * rows
    ent = 2 * slots
    ent_row = iota((ent, reqs), 0)
    req_lane = iota((ent, reqs), 1)
    sel = jnp.where((ent_row == slots) & (req_lane == my), 1.0, 0.0)
    in_use = iota(table_ref.shape, 0) < count_ref[...]
    table = jnp.where(in_use, table_ref[...], -1)
    for g in range(slots):
        hit = jnp.where(table == my * slots + g, 1.0, 0.0)
        sel = jnp.where(ent_row == g, jnp.max(hit, axis=0, keepdims=True), sel)
    sel_b = sel.astype(BF16)
    same = lax.dot_general(sel_b, sel_b, NT, preferred_element_type=F32)
    q_lane = over(iota((ent, width), 1), HD)
    pieces = []
    for k in range(topk):
        group_query = dot(sel_b, q_rows[:, k, :].astype(BF16))
        for h in range(heads):
            pieces.append(jnp.where(q_lane == h, group_query, 0.0))
    queries = jnp.concatenate(pieces, axis=0)
    kh = topk * heads
    scale = 1.0 / math.sqrt(HD)
    scores = lax.dot_general(queries.astype(BF16), kb[...], NT, preferred_element_type=F32) * scale
    col = iota((kh * ent, n), 1)
    scores = scores + jnp.where(rest(col, rows) == rows - 1, math.log(page_len - rows + 1), 0.0)
    of_page = jnp.where(over(iota((ent, n), 1), rows) == iota((ent, n), 0), 1.0, 0.0).astype(BF16)
    shared = dot(same.astype(BF16), of_page)
    mask = jnp.concatenate([shared] * kh, axis=0) > 0.5
    scores = jnp.where(mask, scores, NEGATIVE)
    is_own = rest(iota((kh * ent, 1), 0), ent) == slots
    own = jnp.sum(queries * nk_ref[...].astype(F32), axis=1, keepdims=True) * scale
    own = jnp.where(is_own, own, NEGATIVE)
    peak = jnp.maximum(jnp.max(scores, axis=1, keepdims=True), own)
    shift = peak.astype(BF16).astype(F32)
    probs = jnp.where(mask, jnp.exp(scores - shift), 0.0)
    own_prob = jnp.where(is_own, jnp.exp(own - shift), 0.0)
    den = jnp.sum(probs, axis=1, keepdims=True) + own_prob
    num = dot(probs.astype(BF16), vb[...])
    num = num + own_prob.astype(BF16).astype(F32) * nv_ref[...].astype(F32)
    high = den.astype(BF16).astype(F32)
    low = den - high
    er = iota((ent, ent), 0)
    ec = iota((ent, ent), 1)
    before = jnp.sum(jnp.where((ec < er) | (ec == slots), same, 0.0), axis=1, keepdims=True)
    row = ent_row[:, 0:1]
    first = (row == slots) | ((row < slots) & (before < 0.5))
    request = jnp.sum(jnp.where(sel > 0.5, req_lane.astype(F32), 0.0), axis=1, keepdims=True)
    expert = [
        jnp.sum(jnp.where(sel > 0.5, ids_ref[k : k + 1, :].astype(F32), 0.0), axis=1, keepdims=True)
        for k in range(topk)
    ]
    expert_lane = iota((1, EXPERTS), 1).astype(F32)
    logit = [
        jnp.sum(
            jnp.where(expert_lane == expert[k][slots : slots + 1, :], logit_ref[...], 0.0),
            axis=1,
            keepdims=True,
        )
        for k in range(topk)
    ]
    top = logit[0]
    for k in range(1, topk):
        top = jnp.maximum(top, logit[k])
    terms = [jnp.exp(logit[k] - top) for k in range(topk)]
    term_sum = terms[0]
    for k in range(1, topk):
        term_sum = term_sum + terms[k]
    stat_lane = iota((ent, HD), 1)
    by_choice = []
    for k in range(topk):
        gate = jnp.where(row == slots, terms[k] / term_sum, 0.0)
        gate_high = gate.astype(BF16).astype(F32)
        stats = jnp.where(stat_lane == 3 * heads, gate_high, 0.0)
        stats = jnp.where(stat_lane == 3 * heads + 1, gate - gate_high, stats)
        stats = jnp.where(stat_lane == 3 * heads + 2, request, stats)
        lanes = []
        for h in range(heads):
            at = slice((k * heads + h) * ent, (k * heads + h + 1) * ent)
            lanes.append(num[at, h * HD : (h + 1) * HD])
            for i, stat in enumerate((shift, high, low)):
                stats = jnp.where(stat_lane == 3 * h + i, stat[at, :], stats)
        by_choice.append(jnp.concatenate(lanes + [stats], axis=1))
    parts = []
    for e in range(EXPERTS):
        part = jnp.zeros(by_choice[0].shape, F32)
        for k in range(topk):
            part = jnp.where(first & (expert[k] == e), by_choice[k], part)
        parts.append(part)
    entries = jnp.concatenate(parts, axis=0)
    stats = entries[:, width:].astype(BF16)
    devices = out_ref.shape[0]
    lines = out_ref.shape[1] - heads * slots
    columns = devices // EXPERTS
    to = iota((EXPERTS * lines, EXPERTS * ent), 0)
    fro = iota((EXPERTS * lines, EXPERTS * ent), 1)
    flat = (over(to, lines) == over(fro, ent)) & (rest(to, lines) == slots + 1)
    flat = jnp.where(flat, 1.0, 0.0).astype(BF16)
    square = iota((HD, HD), 0)
    item = iota((HD, HD), 1) % 6
    mine = iota((EXPERTS * ent, HD), 1) // 6 == rest(iota((EXPERTS * ent, HD), 0), ent)
    for h in range(heads):
        origin = jnp.where(item < 3, 3 * h + item, 3 * heads + item - 3)
        spread = dot(stats, jnp.where(square == origin, 1.0, 0.0).astype(BF16))
        line = dot(flat, jnp.where(mine, spread, 0.0).astype(BF16))
        sent = (entries[:, h * HD : (h + 1) * HD] + line).astype(BF16)
        for e in range(EXPERTS):
            for z in range(columns // heads):
                out_ref[e * columns + z * heads + h, 0:lines, :] = sent[e * lines : (e + 1) * lines, :]
    to = iota((n, n), 0)
    fro = iota((n, n), 1)
    perm = jnp.where((rest(to, slots) == over(fro, rows)) & (over(to, slots) == rest(fro, rows)), 1.0, 0.0).astype(BF16)
    for base, blocks in ((0, kb), (rows, vb)):
        spread = dot(perm, blocks[...])
        for t in range(heads):
            at = slice(lines + t * slots, lines + (t + 1) * slots)
            out_ref[base : base + rows, at, :] = (
                spread[:, t * HD : (t + 1) * HD].reshape(rows, slots, HD).astype(BF16)
            )


def expert_kernel(head_ref, routed_hbm, got_ref, *refs):
    del routed_hbm
    w_refs, (out_hbm, scr, terms, stack, out_ref, sem) = refs[:-6], refs[-6:]
    heads = len(w_refs)
    head = head_ref[0]
    reqs, lines, _ = scr.shape
    slots = lines // 2
    depth = stack.shape[1]
    stack[0] = w_refs[0][0, pl.ds(head * depth, depth), :]
    for d in range(1, heads):
        stack[d] = w_refs[d][...]
    scr[...] = got_ref[:, 0:lines, :].astype(F32)
    stats = scr[:, slots + 1, :]
    stats = jnp.concatenate([stats, stats], axis=0).T
    left = iota((1, 2 * reqs), 1) < reqs
    target = iota((reqs, 2 * reqs), 0).astype(F32)

    def item(g, i):
        first = stats[6 * g + i : 6 * g + i + 1, :]
        if g == slots:
            return jnp.where(left, first, 0.0)
        return jnp.where(left, first, stats[6 * g + 6 + i : 6 * g + 7 + i, :])

    groups = range(0, slots + 1, 2)
    picks = [(item(g, 5) == target) & (item(g, 1) > 0.0) for g in groups]
    gate = jnp.zeros(target.shape, F32)
    peak = jnp.full(target.shape, NEGATIVE, F32)
    for g, pick in zip(groups, picks):
        gate = gate + jnp.where(pick, item(g, 3) + item(g, 4), 0.0)
        peak = jnp.maximum(peak, jnp.where(pick, item(g, 0), NEGATIVE))
    gate = jnp.sum(gate, axis=1, keepdims=True)
    peak = jnp.max(peak, axis=1, keepdims=True)
    den = jnp.zeros(target.shape, F32)
    num = jnp.zeros((2 * reqs, HD), F32)
    for g, pick in zip(groups, picks):
        factor = jnp.where(pick, jnp.exp(item(g, 0) - peak), 0.0)
        den = den + factor * (item(g, 1) + item(g, 2))
        high = factor.astype(BF16)
        low = (factor - high.astype(F32)).astype(BF16)
        entries = jnp.concatenate([scr[:, g, :], scr[:, min(g + 1, slots), :]], axis=0).astype(BF16)
        num = num + dot(jnp.concatenate([high, low], axis=0), entries)
    den = jnp.sum(den, axis=1, keepdims=True)
    some = den > 0.0
    value = (num[:reqs] + num[reqs:]) / jnp.where(some, den, 1.0)
    weighted = jnp.where(some, gate * value, 0.0).astype(BF16)
    tiles = stack.shape[2] // HD
    for b in range(heads):
        part = dot(weighted, stack[b ^ head])
        for t in range(tiles):
            terms[:, b * tiles + t, :] = part[:, t * HD : (t + 1) * HD]
    out_ref[...] = terms[...].astype(BF16)
    terms_at = out_hbm.shape[1] - out_ref.shape[1]
    store = pltpu.make_async_copy(out_ref, out_hbm.at[:, terms_at:, :], sem)
    store.start()
    store.wait()


def relay_kernel(got_ref, pick_ref, out_hbm, out_ref, out_sems):
    reqs = got_ref.shape[0]
    held = pick_ref.shape[1]
    slots = held // reqs
    lines = 2 * slots
    local = pick_ref.shape[0] // reqs
    terms_at = out_ref.shape[1]
    table = jnp.concatenate(
        [
            got_ref[:, lines + t * slots : lines + (t + 1) * slots, :]
            .astype(F32)
            .reshape(held, HD)
            .astype(BF16)
            for t in range(terms_at // local)
        ],
        axis=1,
    )
    step = 16
    stores = []
    for c in range(0, reqs, step):
        rows = dot(pick_ref[c * local : (c + step) * local, :], table)
        for t in range(terms_at // local):
            out_ref[c : c + step, t * local : (t + 1) * local, :] = (
                rows[:, t * HD : (t + 1) * HD].reshape(step, local, HD).astype(BF16)
            )
        at = pl.ds(c, step)
        stores.append(
            pltpu.make_async_copy(
                out_ref.at[at], out_hbm.at[at, 0:terms_at, :], out_sems.at[c // step]
            )
        )
        stores[-1].start()
    for store in stores:
        store.wait()


def route_kernel(new_ref, table_ref, count_ref, out_ref):
    max_new = new_ref.shape[0]
    per_new = table_ref.shape[0] // max_new
    shape = (out_ref.shape[0], new_ref.shape[1])
    slot = over(iota(shape, 0), per_new)
    quarter = rest(iota(shape, 0), per_new)
    found = jnp.zeros(shape, jnp.int32)
    for i in range(max_new):
        filled = jnp.where(i * per_new < count_ref[...], new_ref[i : i + 1, :], -1)
        page = jnp.zeros(shape, jnp.int32)
        for w in range(per_new):
            page = jnp.where(quarter == w, table_ref[i * per_new + w : i * per_new + w + 1, :] + 1, page)
        found = jnp.where(filled == slot, page, found)
    source = jnp.sum(found, axis=1, keepdims=True) - 1
    out_ref[...] = jnp.where(source == iota(out_ref.shape, 1), 1.0, 0.0).astype(BF16)


def sum_kernel(shard_ref, got_ref, *refs, lines):
    out_refs, (quarters,) = refs[:-1], refs[-1:]
    s = shard_ref[0]
    columns = got_ref.shape[0] // EXPERTS
    got = got_ref[:, got_ref.shape[1] - lines :, :].astype(F32)
    heads = columns // 2
    per = lines // 2
    for z in range(2):
        total = jnp.zeros(got.shape[1:], F32)
        for e in range(EXPERTS):
            at = e * columns + z * heads
            total = total + jnp.sum(got[at : at + heads], axis=0)
        for i in range(2):
            quarters[2 * z + i] = total[i * per : (i + 1) * per]
    for t, out_ref in enumerate(out_refs):
        quarter = quarters[s ^ t]
        for i in range(per):
            out_ref[:, i * HD : (i + 1) * HD] = quarter[i : i + 1, :]


def land_kernel(got_ref, k_hbm, v_hbm, k_ref, v_ref, sems):
    tiles = k_ref.shape[2] // HD
    rows = got_ref.shape[0] // 2
    n = k_ref.shape[0] * k_ref.shape[1]
    local = n // rows
    to = iota((n, n), 0)
    fro = iota((n, n), 1)
    perm = (over(to, rows) == rest(fro, local)) & (rest(to, rows) == over(fro, local))
    perm = jnp.where(perm, 1.0, 0.0).astype(BF16)
    stores = []
    for i, (ref, hbm) in enumerate(((k_ref, k_hbm), (v_ref, v_hbm))):
        flat = jnp.concatenate(
            [
                got_ref[i * rows : (i + 1) * rows, t * local : (t + 1) * local, :].reshape(n, HD)
                for t in range(tiles)
            ],
            axis=1,
        )
        ref[...] = dot(perm, flat).reshape(ref.shape).astype(BF16)
        stores.append(pltpu.make_async_copy(ref, hbm, sems.at[i]))
        stores[i].start()
    for store in stores:
        store.wait()


def shards(
    old_keys,
    old_values,
    keep_lists,
    drop_weights,
    request_pages,
    page_table,
    new_table,
    queries,
    new_keys,
    new_values,
    expert_ids,
    router_logits,
    out_weight,
):
    devices = lax.axis_size("pages")
    shard_count = lax.axis_size("expert")
    my = lax.axis_index("pages").astype(jnp.int32)
    slots, page_len, width = old_keys.shape
    rows = keep_lists.shape[1] + 1
    per_new = page_len // rows
    requests, max_pages = page_table.shape
    new_cap = 2 * (slots // per_new)
    local = new_cap * per_new
    heads = width // HD
    topk = queries.shape[1]
    lines = 2 * slots
    columns = devices // EXPERTS
    head = lax.rem(my, heads)
    shard = lax.axis_index("expert").astype(jnp.int32).reshape(1)
    table = page_table.T
    counts = request_pages.reshape(1, -1)

    outbox = pl.pallas_call(
        source_kernel,
        out_shape=jax.ShapeDtypeStruct((devices, lines + heads * slots, HD), BF16),
        in_specs=[SMEM] + [VMEM] * 11,
        out_specs=VMEM,
        scratch_shapes=[
            pltpu.VMEM((slots * rows, width), BF16),
            pltpu.VMEM((slots * rows, width), BF16),
            pltpu.VMEM((slots, HD), F32),
            pltpu.VMEM((requests, topk, width), F32),
        ],
        name="source",
    )(
        my.reshape(1),
        table,
        counts,
        expert_ids.T,
        keep_lists,
        drop_weights,
        old_keys,
        old_values,
        queries,
        new_keys,
        new_values,
        router_logits,
    )
    inbox = lax.all_to_all(outbox, "pages", split_axis=0, concat_axis=0, tiled=True)

    weight, _ = lax.optimization_barrier((out_weight[0], outbox))
    pieces = [lax.dynamic_slice_in_dim(weight, (head ^ d) * HD, HD, 0) for d in range(1, heads)]
    weights = [
        lax.ppermute(piece, "pages", [(p, p ^ d) for p in range(devices)])
        for d, piece in enumerate(pieces, 1)
    ]
    pick = pl.pallas_call(
        route_kernel,
        out_shape=jax.ShapeDtypeStruct((devices * local, devices * slots), BF16),
        in_specs=[VMEM] * 3,
        out_specs=VMEM,
        compiler_params=PARAMS,
        name="route",
    )(new_table.T, table, counts)
    inbox, pick = lax.optimization_barrier((inbox, pick))

    block_cols = out_weight.shape[2]
    terms = heads * block_cols // HD
    outgoing = jax.ShapeDtypeStruct((devices, heads * local + terms, HD), BF16)
    routed = pl.pallas_call(
        relay_kernel,
        out_shape=outgoing,
        in_specs=[VMEM, VMEM],
        out_specs=ANY,
        scratch_shapes=[
            pltpu.VMEM((devices, heads * local, HD), BF16),
            pltpu.SemaphoreType.DMA((devices // 16,)),
        ],
        compiler_params=PARAMS,
        name="relay",
    )(inbox, pick)
    routed = pl.pallas_call(
        expert_kernel,
        out_shape=outgoing,
        in_specs=[SMEM, ANY] + [VMEM] * (1 + heads),
        out_specs=ANY,
        scratch_shapes=[
            pltpu.VMEM((requests, lines, HD), F32),
            pltpu.VMEM((requests, terms, HD), F32),
            pltpu.VMEM((heads, HD, block_cols), BF16),
            pltpu.VMEM((requests, terms, HD), BF16),
            pltpu.SemaphoreType.DMA(()),
        ],
        input_output_aliases={1: 0},
        compiler_params=PARAMS,
        name="expert",
    )(head.reshape(1), routed, inbox, out_weight, *weights)
    landed = lax.all_to_all(routed, "pages", split_axis=0, concat_axis=0, tiled=True)

    quarters = pl.pallas_call(
        functools.partial(sum_kernel, lines=terms),
        out_shape=[jax.ShapeDtypeStruct((1, width), F32)] * shard_count,
        in_specs=[SMEM, VMEM],
        out_specs=[VMEM] * shard_count,
        scratch_shapes=[pltpu.VMEM((shard_count, width // HD, HD), F32)],
        compiler_params=PARAMS,
        name="sum",
    )(shard, landed)
    landed, quarters = lax.optimization_barrier((landed, quarters))
    moved = [quarters[0]]
    for t in range(1, shard_count):
        moved.append(lax.ppermute(quarters[t], "expert", [(i, i ^ t) for i in range(shard_count)]))
    new_page = jax.ShapeDtypeStruct((new_cap, per_new * rows, width), BF16)
    compact_keys, compact_values = pl.pallas_call(
        land_kernel,
        out_shape=(new_page, new_page),
        in_specs=[VMEM],
        out_specs=(ANY, ANY),
        scratch_shapes=[
            pltpu.VMEM(new_page.shape, BF16),
            pltpu.VMEM(new_page.shape, BF16),
            pltpu.SemaphoreType.DMA((2,)),
        ],
        compiler_params=PARAMS,
        name="land",
    )(landed)
    mixed = sum(moved[1:], moved[0]).astype(BF16)
    return (compact_keys, compact_values, mixed)


def solution(mesh):
    in_specs = (
        P("pages", None, "expert"),
        P("pages", None, "expert"),
        P("pages", None),
        P("pages", None),
        P(),
        P(),
        P(),
        P(None, None, "expert"),
        P("pages", "expert"),
        P("pages", "expert"),
        P(),
        P("pages", None),
        P("pages", "expert", None),
    )
    out_specs = (P("pages", None, "expert"), P("pages", None, "expert"), P("pages", "expert"))
    return jax.shard_map(shards, mesh=mesh, in_specs=in_specs, out_specs=out_specs, check_vma=False)
```
